32 devices in a mesh: dp: 4 (over y, core), expert: 8 (over z, x).
Axes of the slice: x: 2, y: 2, z: 4, core: 2. Of those that a mesh axis runs over, the one named last changes fastest.
Arguments:
- tokens: bfloat16 [4096, 2048], P(('dp', 'expert')), may hold values from -6 to 6
- seq_lengths: int32 [4], replicated, may hold values from 256 to 1024, as said below
- routes: int32 [4096, 8], P(('dp', 'expert')), may hold values from 0 to 15, all different within a row; in each aligned block of 128 rows (0 to 127, 128 to 255, ...) at most 72 rows name the same one
- w_query: bfloat16 [2048, 2048], P(('dp', 'expert')), may hold values from -0.125 to 0.125
- w_key: bfloat16 [2048, 2048], P(('dp', 'expert')), may hold values from -0.125 to 0.125
- w_value: bfloat16 [2048, 2048], P(('dp', 'expert')), may hold values from -0.125 to 0.125
- w_out: bfloat16 [2048, 2048], P(('dp', 'expert')), may hold values from -2 to 2
- gain_attn: bfloat16 [2048], P(('dp', 'expert')), may hold values from 0.5 to 1.5
- gain_query: bfloat16 [2048], P(('dp', 'expert')), may hold values from 0.5 to 1.5
- gain_key: bfloat16 [2048], P(('dp', 'expert')), may hold values from 0.5 to 1.5
- gain_ffn: bfloat16 [2048], P(('dp', 'expert')), may hold values from 0.5 to 1.5
- w_router: bfloat16 [2048, 16], P(('dp', 'expert')), may hold values from -0.0625 to 0.0625
- w_gate: bfloat16 [16, 2048, 1024], P('expert'), may hold values from -0.125 to 0.125
- w_up: bfloat16 [16, 2048, 1024], P('expert'), may hold values from -0.125 to 0.125
- w_down_t: bfloat16 [16, 2048, 1024], P('expert'), may hold values from -3 to 3
- cotangent: bfloat16 [4096, 2048], P(('dp', 'expert')), may hold values from -6 to 6
Outputs:
- output: bfloat16 [4096, 2048], P(('dp', 'expert'))
- input_grad: bfloat16 [4096, 2048], P(('dp', 'expert'))
- grad_query: float32 [2048, 2048], P(('dp', 'expert'))
- grad_key: float32 [2048, 2048], P(('dp', 'expert'))
- grad_value: float32 [2048, 2048], P(('dp', 'expert'))
- grad_out: float32 [2048, 2048], P(('dp', 'expert'))
- grad_gain_attn: float32 [2048], P(('dp', 'expert'))
- grad_gain_query: float32 [2048], P(('dp', 'expert'))
- grad_gain_key: float32 [2048], P(('dp', 'expert'))
- grad_gain_ffn: float32 [2048], P(('dp', 'expert'))
- grad_router: float32 [2048, 16], P(('dp', 'expert'))
- grad_gate: float32 [16, 2048, 1024], P('expert', None, 'dp')
- grad_up: float32 [16, 2048, 1024], P('expert', None, 'dp')
- grad_down_t: float32 [16, 2048, 1024], P('expert', None, 'dp')
- rms_resid: float32 [], replicated
- rms_moe: float32 [], replicated
The draws below stay inside these ranges and needn't reach their ends.
Inputs may be any that keep to these rules, and one draw needn't show every extreme that they name: `routes`: in the rows of one device no expert is named by more than 72 rows, a bound that some block reaches. `seq_lengths`: some sequence is full in every draw.
All inputs are finite; a program needn't handle non-finite values.
Results may differ from the reference program's by a relative error of at most 0.02.
Values may be sent and summed in bfloat16 or wider, within the bound.
No kernel may reach another device: no remote copies, remote signals or barrier semaphores. Data moves between devices by JAX's collectives and lax.ppermute only.
A program may use at most 320 MiB of HBM per device.

```python
import math
import jax
import jax.numpy as jnp
import numpy as np
from jax import lax

D = 2048
HEADS = 16
HEAD_DIM = 128
FF = 1024
TOP = 8
TOK_DEV = 128
SEQ_LEN = 1024
EXPERTS = 16
TOKENS = 4096
SEQS = 4
CAP = 72
N_DP = 4
N_EXPERT = 8


def draw_seq_lengths(key, part):
    first_key, second_key = jax.random.split(jax.random.fold_in(key, 17))
    values = jax.random.randint(first_key, (SEQS,), SEQ_LEN // 4, SEQ_LEN + 1, dtype=jnp.int32)
    chosen = jax.random.randint(second_key, (), 0, SEQS, dtype=jnp.int32)
    return values.at[chosen].set(SEQ_LEN)


def block_scale(key, dims, cuts, low, high):
    factor_of = 1.0
    for axis_at, shards_of in cuts:
        steps = jax.random.uniform(jax.random.fold_in(jax.random.fold_in(key, 6), axis_at), (shards_of,), jnp.float32, low / len(cuts), high / len(cuts))
        factor_of = factor_of * jnp.repeat(jnp.exp(steps), dims[axis_at] // shards_of).reshape((-1,) + (1,) * (len(dims) - 1 - axis_at))
    return factor_of


def shared_out(rng, own, number, rows, count, top, most, lean):
    order = jax.random.permutation(rng, count)
    crowded, usual = load_shares(count, rows * top, most, lean, True), load_shares(count, rows * top, most, lean, False)
    places = jnp.arange(count)

    def named(tallies, offset_by):
        used = int((tallies > 0).sum())
        fixed = max(1, used // 4)
        moved = fixed + (places - fixed + offset_by * (used - fixed)) % max(1, count - fixed)
        return jnp.zeros((count,), jnp.int32).at[order[jnp.where(places < fixed, places, moved)]].set(jnp.asarray(tallies, jnp.int32))

    tallies = jnp.where(number % 4 == 0, named(crowded, number // 4), named(usual, number - number // 4 - 1))
    mixed = jax.random.permutation(jax.random.fold_in(own, 3), count)
    donor, sink = mixed[0:count // 2 * 2:2], mixed[1:count // 2 * 2:2]
    room = jnp.minimum(tallies[donor] - 1, most - tallies[sink]) // 2
    room = jnp.where((donor == order[0]) | (sink == order[0]) | (tallies[sink] == 0), 0, jnp.maximum(room, 0))
    moved = jax.random.randint(jax.random.fold_in(own, 4), (count // 2,), 0, 1 << 20) % (room + 1)
    tallies = tallies.at[donor].add(-moved).at[sink].add(moved)
    items = jnp.searchsorted(jnp.cumsum(tallies), jnp.arange(rows * top), side="right").astype(jnp.int32)
    table = items.reshape(top, rows).T
    table = table[jax.random.permutation(jax.random.fold_in(own, 1), rows)]
    offset_by = jax.random.randint(jax.random.fold_in(own, 2), (rows, 1), 0, top)
    return jnp.take_along_axis(table, (jnp.arange(top)[None, :] + offset_by) % top, axis=1)


def load_shares(amount, total, reach, lean, full):
    portions = [(1 << 20) // math.isqrt(rank ** lean) + 1 for rank in range(1, amount + 1)]
    largest = reach if full else min(reach, max(-(-total // amount), total * portions[0] // sum(portions)))
    least = 1 if total - largest >= amount - 1 else 0
    counts, spare = [largest] + [least] * (amount - 1), total - largest - least * (amount - 1)
    while spare > 0:
        candidates = [i for i in range(1, amount) if counts[i] < largest] or [i for i in range(1, amount) if counts[i] < reach]
        mass, left = sum([portions[i] for i in candidates]), spare
        for i in candidates:
            more = min(reach - counts[i], max(1, left * portions[i] // mass), spare)
            counts[i] = counts[i] + more
            spare = spare - more
    return np.array(counts)


def centred(key, extent, width, limit, cuts=(), kind=jnp.bfloat16):
    drawn = width * jax.random.normal(key, extent, jnp.float32)
    if cuts:
        drawn = drawn * block_scale(key, extent, cuts, -0.22, 0.18)
    return jnp.clip(drawn, -limit, limit).astype(kind)


def setup_inputs(seed: int = 0) -> dict:
    seeds = jax.random.split(jax.random.key(seed), 17)
    tokens = centred(seeds[0], (TOKENS, D), 1.0, 6.0, ((0, 32),))
    seq_lengths = draw_seq_lengths(jax.random.fold_in(seeds[16], 71), 0)
    routes_keys = jax.random.split(jax.random.fold_in(seeds[2], 1), TOKENS // TOK_DEV)
    routes_turns = jax.random.permutation(jax.random.fold_in(seeds[2], 3), TOKENS // TOK_DEV)
    routes = jax.vmap(lambda own, number: shared_out(jax.random.fold_in(seeds[2], 2), own, number, TOK_DEV, EXPERTS, TOP, CAP, 1))(routes_keys, routes_turns).reshape((TOKENS, TOP))
    w_query = centred(seeds[3], (D, D), D ** -0.5, 0.125, ((0, 32),))
    w_key = centred(seeds[4], (D, D), D ** -0.5, 0.125, ((0, 32),))
    w_value = centred(seeds[5], (D, D), D ** -0.5, 0.125, ((0, 32),))
    w_out = centred(seeds[6], (D, D), (max(D // 256, 1)) ** -0.5, 2.0, ((0, 32),))
    gain_attn = jnp.clip(1.0 + 0.1 * jax.random.normal(seeds[7], (D,), jnp.float32), 0.5, 1.5).astype(jnp.bfloat16)
    gain_query = jnp.clip(1.0 + 0.1 * jax.random.normal(seeds[8], (D,), jnp.float32), 0.5, 1.5).astype(jnp.bfloat16)
    gain_key = jnp.clip(1.0 + 0.1 * jax.random.normal(seeds[9], (D,), jnp.float32), 0.5, 1.5).astype(jnp.bfloat16)
    gain_ffn = jnp.clip(1.0 + 0.1 * jax.random.normal(seeds[10], (D,), jnp.float32), 0.5, 1.5).astype(jnp.bfloat16)
    w_router = centred(seeds[11], (D, EXPERTS), (4 * D) ** -0.5, 0.0625, ((0, 32),))
    w_gate = centred(seeds[12], (EXPERTS, D, FF), D ** -0.5, 0.125, ((0, 8),))
    w_up = centred(seeds[13], (EXPERTS, D, FF), D ** -0.5, 0.125, ((0, 8),))
    w_down_t = centred(seeds[14], (EXPERTS, D, FF), (max(FF // 256, 1)) ** -0.5, 3.0, ((0, 8),))
    cotangent = centred(seeds[15], (TOKENS, D), 1.0, 6.0, ((0, 32),))
    return {"tokens": tokens, "seq_lengths": seq_lengths, "routes": routes, "w_query": w_query, "w_key": w_key, "w_value": w_value, "w_out": w_out, "gain_attn": gain_attn, "gain_query": gain_query, "gain_key": gain_key, "gain_ffn": gain_ffn, "w_router": w_router, "w_gate": w_gate, "w_up": w_up, "w_down_t": w_down_t, "cotangent": cotangent}


EPSILON = 1e-05
ROPE_BASE = 10000.0
PRECISE = lax.Precision.HIGHEST

@jax.custom_vjp
def low(v):
    return lax.optimization_barrier(v.astype(jnp.bfloat16)).astype(jnp.float32)

@jax.custom_vjp
def low_back(v):
    return v

def low_keep(v):
    return (low(v), None)

def low_pass(kept, grad):
    return (grad,)

def back_keep(v):
    return (v, None)

def back_low(kept, grad):
    return (low(grad),)
low.defvjp(low_keep, low_pass)
low_back.defvjp(back_keep, back_low)

def norm_rows(values, gain):
    mean_square = lax.optimization_barrier(jnp.mean(values * values, axis=-1, keepdims=True))
    return values * lax.rsqrt(mean_square + EPSILON) * gain

def rotary(values, positions):
    row_count = values.shape[0]
    half_dim = HEAD_DIM // 2
    frequency = ROPE_BASE ** (-(jnp.arange(half_dim, dtype=jnp.float32) * 2.0) / HEAD_DIM)
    angles = positions.astype(jnp.float32)[:, None] * frequency[None, :]
    cosine = jnp.cos(angles)[:, None, :]
    sine_part = jnp.sin(angles)[:, None, :]
    shaped = values.reshape(row_count, HEADS, HEAD_DIM)
    first_half = shaped[:, :, :half_dim]
    second_half = shaped[:, :, half_dim:]
    turned = jnp.concatenate([first_half * cosine - second_half * sine_part, second_half * cosine + first_half * sine_part], axis=-1)
    return turned.reshape(row_count, HEADS * HEAD_DIM)

def softmax_rows(scores):
    highest = lax.optimization_barrier(jnp.max(scores, axis=-1, keepdims=True))
    expos = jnp.exp(scores - highest)
    return expos / lax.optimization_barrier(jnp.sum(expos, axis=-1, keepdims=True))

def swiglu(gate_vals, up_vals):
    return jax.nn.silu(gate_vals) * up_vals

def matmul(left, right):
    return jnp.dot(left, right, preferred_element_type=jnp.float32, precision=PRECISE)

def sequence_attention(pieces):
    query, keys, values, seq_length = pieces
    places = jnp.arange(SEQ_LEN, dtype=jnp.int32)
    query_heads = query.reshape(SEQ_LEN, HEADS, HEAD_DIM)
    key_heads = keys.reshape(SEQ_LEN, HEADS, HEAD_DIM)
    value_heads = values.reshape(SEQ_LEN, HEADS, HEAD_DIM)
    raw = jnp.einsum('qhd,khd->hqk', query_heads, key_heads, precision=PRECISE) * HEAD_DIM ** (-0.5)
    allowed = (places[None, :] <= places[:, None]) & (places[None, :] < seq_length)
    scores = low_back(jnp.where(allowed[None], raw, -1e+30))
    weights = low(softmax_rows(scores))
    result = jnp.einsum('hqk,khd->qhd', weights, value_heads, precision=PRECISE)
    return result.reshape(SEQ_LEN, HEADS * HEAD_DIM)

def reference(tokens, seq_lengths, routes, w_query, w_key, w_value, w_out, gain_attn, gain_query, gain_key, gain_ffn, w_router, w_gate, w_up, w_down_t, cotangent):
    devices = N_DP * N_EXPERT
    per_expert = devices * CAP
    row_ids = jnp.arange(TOKENS, dtype=jnp.int32)
    positions = row_ids % SEQ_LEN
    seq_of = row_ids // SEQ_LEN
    used = (positions < seq_lengths[seq_of]).astype(jnp.float32)[:, None]
    flat = routes.reshape(devices, TOK_DEV * TOP)
    expert_ids = jnp.arange(EXPERTS, dtype=jnp.int32)
    hits = (flat[:, :, None] == expert_ids[None, None, :]).astype(jnp.int32)
    earlier = jnp.cumsum(hits, axis=1) - hits
    slot_of = lax.optimization_barrier(jnp.sum(earlier * hits, axis=2))
    source = jnp.arange(devices, dtype=jnp.int32)[:, None]
    place = (flat * per_expert + source * CAP + slot_of).reshape(TOKENS, TOP)
    owners = jnp.repeat(row_ids, TOP)
    buffer_tok = jnp.full((EXPERTS * per_expert,), TOKENS, jnp.int32).at[place.reshape(-1)].set(owners).reshape(EXPERTS, per_expert)

    def forward(resid_in, wq, wk, wv, wo, gain_a, gain_q, gain_k, gain_f, wr, wg, wu, wd):
        attn_in = low(norm_rows(resid_in, gain_a))
        query_raw = low_back(matmul(attn_in, wq))
        key_raw = low_back(matmul(attn_in, wk))
        value_raw = low_back(matmul(attn_in, wv))
        query_rows = low(rotary(norm_rows(query_raw, gain_q), positions))
        key_rows = low(rotary(norm_rows(key_raw, gain_k), positions))
        value_rows = low(value_raw)
        attended = lax.map(jax.checkpoint(sequence_attention), (query_rows.reshape(SEQS, SEQ_LEN, D), key_rows.reshape(SEQS, SEQ_LEN, D), value_rows.reshape(SEQS, SEQ_LEN, D), seq_lengths))
        attn_rows = low(low_back(attended.reshape(TOKENS, D)))
        resid_mid = resid_in + low_back(matmul(attn_rows, wo))
        ffn_in = low(norm_rows(resid_mid, gain_f))
        router_probs = softmax_rows(low_back(matmul(ffn_in, wr)))
        route_weights = jnp.take_along_axis(router_probs, routes, axis=1)
        padded_in = jnp.concatenate([ffn_in, jnp.zeros((1, D), jnp.float32)], axis=0)

        def expert_block(pieces):
            index, gate_w, up_w, down_w = pieces
            rows_in = low_back(padded_in[index])
            gate_vals = low_back(matmul(rows_in, gate_w))
            up_vals = low_back(matmul(rows_in, up_w))
            hidden = low(swiglu(gate_vals, up_vals))
            return low(low_back(jnp.dot(hidden, down_w.T, preferred_element_type=jnp.float32, precision=PRECISE)))
        expert_out = lax.map(jax.checkpoint(expert_block), (buffer_tok, wg, wu, wd))
        picked = expert_out.reshape(EXPERTS * per_expert, D)[place]
        moe_rows = lax.optimization_barrier(jnp.sum(route_weights[:, :, None] * picked, axis=1))
        return (resid_mid + moe_rows, (resid_mid, moe_rows))
    result, pullback, extra = jax.vjp(forward, tokens.astype(jnp.float32), w_query.astype(jnp.float32), w_key.astype(jnp.float32), w_value.astype(jnp.float32), w_out.astype(jnp.float32), gain_attn.astype(jnp.float32), gain_query.astype(jnp.float32), gain_key.astype(jnp.float32), gain_ffn.astype(jnp.float32), w_router.astype(jnp.float32), w_gate.astype(jnp.float32), w_up.astype(jnp.float32), w_down_t.astype(jnp.float32), has_aux=True)
    grads = pullback(cotangent.astype(jnp.float32))
    resid_mid, moe_rows = extra
    counted = jnp.sum(seq_lengths).astype(jnp.float32) * D
    rms_resid = jnp.sqrt(jnp.sum(used * resid_mid * resid_mid) / counted)
    rms_moe = jnp.sqrt(jnp.sum(used * moe_rows * moe_rows) / counted)
    return (result.astype(jnp.bfloat16), grads[0].astype(jnp.bfloat16), grads[1], grads[2], grads[3], grads[4], grads[5], grads[6], grads[7], grads[8], grads[9], grads[10], grads[11], grads[12], rms_resid, rms_moe)
```

```python
import jax
import jax.numpy as jnp
import numpy as np
from jax import lax
from jax.experimental import pallas as pl
from jax.experimental.pallas import tpu as pltpu
from jax.sharding import PartitionSpec as P

HEADS = 16
HEAD_DIM = 128
TOP = 8
EPSILON = 1e-05
ROPE_BASE = 10000.0
SCALE = HEAD_DIM ** (-0.5)
NEG = -1e30
Z_CHIPS = 4
CORES = 2
F32 = jnp.float32
BF16 = jnp.bfloat16


def ring_tables(groups):
    x_chips = groups // Z_CHIPS
    walk = []
    for x in range(x_chips):
        column = range(1, Z_CHIPS) if x % 2 == 0 else range(Z_CHIPS - 1, 0, -1)
        walk += [z * x_chips + x for z in column]
    walk += [x for x in range(x_chips - 1, -1, -1)]
    place = np.zeros((groups,), np.int32)
    for at, owner in enumerate(walk):
        place[owner] = at
    return np.array(walk, np.int32), place


class Ring:
    def __init__(self, groups):
        self.size = groups
        self.walk, self.place = ring_tables(groups)
        size = groups
        self.ahead = [(int(self.walk[i]), int(self.walk[(i + 1) % size])) for i in range(size)]
        self.back = [(b, a) for a, b in self.ahead]
        mine = jnp.asarray(self.place)[lax.axis_index("expert")]
        self.natural = jnp.asarray(self.walk)[(mine + jnp.arange(size, dtype=jnp.int32)) % size]

    def up(self, value):
        return lax.ppermute(value, "expert", self.ahead)

    def down(self, value):
        return lax.ppermute(value, "expert", self.back)

    def gather(self, block):
        half = self.size // 2
        rows = block.shape[0]
        pieces = [(0, 0, block)]
        up, down = block, block
        for step in range(1, half):
            up = self.up(up)
            down = self.down(down)
            pieces += [(self.size - step, 0, up), (step, 0, down)]
        pieces.append((half, 0, self.up(up[: rows // 2])))
        pieces.append((half, rows // 2, self.down(down[rows // 2 :])))
        return pieces

    def scatter(self, term):
        half = self.size // 2
        far = term(half)
        rows = far.shape[0]
        up = self.up(far[: rows // 2])
        down = self.down(far[rows // 2 :])

        def add(left, right):
            return (left.astype(F32) + right.astype(F32)).astype(BF16)

        for step in range(half - 1, 0, -1):
            ahead, behind = term(step), term(self.size - step)
            if step == half - 1:
                ahead = jnp.concatenate([add(up, ahead[: rows // 2]), ahead[rows // 2 :]], axis=0)
                behind = jnp.concatenate(
                    [behind[: rows // 2], add(down, behind[rows // 2 :])], axis=0
                )
            else:
                ahead, behind = add(up, ahead), add(down, behind)
            up, down = self.up(ahead), self.down(behind)
        return up.astype(F32) + down.astype(F32) + term(0).astype(F32)


def place_blocks(ring, pieces, rows, width, dtype=BF16):
    buffer = jnp.zeros((ring.size * rows, width), dtype)
    for o, start, piece in pieces:
        buffer = lax.dynamic_update_slice(
            buffer, piece.astype(dtype), (ring.natural[o] * rows + start, 0)
        )
    return buffer


def expert_sum(value, groups):
    step = 1
    while step < groups:
        value = value + lax.ppermute(value, "expert", [(i, i ^ step) for i in range(groups)])
        step *= 2
    return value


def dp_sum(value, n_dp):
    step = 1
    while step < n_dp:
        value = value + lax.ppermute(value, "dp", [(i, i ^ step) for i in range(n_dp)])
        step *= 2
    return value


def dp_gather(chunk, n_dp):
    rows, width = chunk.shape
    me = lax.axis_index("dp")
    held = [(0, chunk)]
    for y in range(1, n_dp // CORES):
        held.append((2 * y, lax.ppermute(chunk, "dp", [(i, i ^ (2 * y)) for i in range(n_dp)])))
    swap = [(i, i ^ 1) for i in range(n_dp)]
    held += [(rel ^ 1, lax.ppermute(part, "dp", swap)) for rel, part in held]
    buffer = jnp.zeros((n_dp * rows, width), chunk.dtype)
    for rel, part in held:
        buffer = lax.dynamic_update_slice(buffer, part, ((me ^ rel) * rows, 0))
    return buffer


def dp_reduce(term, n_dp):
    swap = [(i, i ^ 1) for i in range(n_dp)]
    chips = n_dp // CORES
    other = [lax.ppermute(term(2 * y + 1).astype(BF16), "dp", swap) for y in range(chips)]
    total = None
    for y in range(1, chips):
        part = (term(2 * y) + other[y].astype(F32)).astype(BF16)
        part = lax.ppermute(part, "dp", [(i, i ^ (2 * y)) for i in range(n_dp)]).astype(F32)
        total = part if total is None else total + part
    own = term(0) + other[0].astype(F32)
    return own if total is None else own + total


def norm_scale(values):
    return lax.rsqrt(jnp.mean(values * values, axis=-1, keepdims=True) + EPSILON)


def matmul(left, right):
    return jnp.dot(left, right, preferred_element_type=F32)


def matmul_nt(left, right):
    return lax.dot_general(left, right, (((1,), (1,)), ((), ())), preferred_element_type=F32)


def matmul_tn(left, right):
    return lax.dot_general(left, right, (((0,), (0,)), ((), ())), preferred_element_type=F32)


def masked(scores, first_row, length):
    rows, columns = scores.shape
    row = first_row + lax.broadcasted_iota(jnp.int32, (rows, columns), 0)
    column = lax.broadcasted_iota(jnp.int32, (rows, columns), 1)
    return jnp.where((column <= row) & (column < length), scores * SCALE, NEG)


def turn(values, cosine, sine):
    return values * cosine + pltpu.roll(values, HEAD_DIM // 2, 1) * sine


def turn_back(values, cosine, sine):
    return values * cosine - pltpu.roll(values, HEAD_DIM // 2, 1) * sine


def attend_kernel(
    length_ref, qkv_ref, squares_ref, gain_ref, cos_ref, sin_ref, q_ref, k_ref, v_ref, o_ref
):
    seq, own = q_ref.shape
    tile = min(256, seq)
    width = HEADS * HEAD_DIM
    length = length_ref[0]
    for start in range(0, seq, tile):
        rows = slice(start, start + tile)
        squares = squares_ref[rows, :]
        cosine, sine = cos_ref[rows, :], sin_ref[rows, :]
        for part, out_ref in ((0, q_ref), (1, k_ref)):
            scale = lax.rsqrt(squares[:, part : part + 1] / width + EPSILON)
            for first in range(0, own, HEAD_DIM):
                columns = slice(first, first + HEAD_DIM)
                raw = qkv_ref[rows, part * own + first : part * own + first + HEAD_DIM]
                normed = raw * scale * gain_ref[part : part + 1, columns]
                out_ref[rows, columns] = turn(normed, cosine, sine).astype(BF16)
        v_ref[rows, :] = qkv_ref[rows, 2 * own : 3 * own].astype(BF16)
    for first in range(0, own, HEAD_DIM):
        columns = slice(first, first + HEAD_DIM)
        for start in range(0, seq, tile):
            rows, keys = slice(start, start + tile), slice(0, start + tile)
            scores = masked(matmul_nt(q_ref[rows, columns], k_ref[keys, columns]), start, length)
            expo = jnp.exp(scores - jnp.max(scores, axis=-1, keepdims=True))
            total = jnp.sum(expo, axis=-1, keepdims=True)
            probs = (expo / total).astype(BF16)
            o_ref[rows, columns] = matmul(probs, v_ref[keys, columns]).astype(BF16)


def attend_back_kernel(
    length_ref,
    qkv_ref,
    squares_ref,
    gain_ref,
    cos_ref,
    sin_ref,
    q_ref,
    k_ref,
    v_ref,
    do_ref,
    dq_ref,
    dk_ref,
    dv_ref,
    dots_ref,
    dgain_ref,
    k_total,
    v_total,
):
    seq, own = q_ref.shape
    tile = min(256, seq)
    width = HEADS * HEAD_DIM
    length = length_ref[0]
    for first in range(0, own, HEAD_DIM):
        columns = slice(first, first + HEAD_DIM)
        k_total[...] = jnp.zeros_like(k_total)
        v_total[...] = jnp.zeros_like(v_total)
        for start in range(0, seq, tile):
            rows, keys = slice(start, start + tile), slice(0, start + tile)
            q, k, v = q_ref[rows, columns], k_ref[keys, columns], v_ref[keys, columns]
            do = do_ref[rows, columns]
            scores = masked(matmul_nt(q, k), start, length)
            expo = jnp.exp(scores - jnp.max(scores, axis=-1, keepdims=True))
            probs = expo / jnp.sum(expo, axis=-1, keepdims=True)
            dprobs = matmul_nt(do, v)
            mean = jnp.sum(probs * dprobs, axis=-1, keepdims=True)
            dscores = (probs * (dprobs - mean)).astype(BF16)
            dq_ref[rows, columns] = matmul(dscores, k) * SCALE
            k_total[keys, :] += matmul_tn(dscores, q)
            v_total[keys, :] += matmul_tn(probs.astype(BF16), do)
        dk_ref[:, columns] = k_total[...] * SCALE
        dv_ref[:, columns] = v_total[...].astype(BF16)
    dgain_ref[...] = jnp.zeros_like(dgain_ref)
    for start in range(0, seq, tile):
        rows = slice(start, start + tile)
        squares = squares_ref[rows, :]
        cosine, sine = cos_ref[rows, :], sin_ref[rows, :]
        for part, out_ref in ((0, dq_ref), (1, dk_ref)):
            scale = lax.rsqrt(squares[:, part : part + 1] / width + EPSILON)
            dot = jnp.zeros((tile, 1), F32)
            for first in range(0, own, HEAD_DIM):
                columns = slice(first, first + HEAD_DIM)
                raw = qkv_ref[rows, part * own + first : part * own + first + HEAD_DIM]
                grad = turn_back(out_ref[rows, columns], cosine, sine)
                dgain_ref[part : part + 1, columns] += jnp.sum(
                    grad * raw * scale, axis=0, keepdims=True
                )
                grad = grad * gain_ref[part : part + 1, columns]
                dot += jnp.sum(grad * raw, axis=-1, keepdims=True)
                out_ref[rows, columns] = grad * scale
            dots_ref[rows, part : part + 1] = dot


def attend(length, qkv, squares, gains, cosine, sine):
    seq, own = qkv.shape[0], qkv.shape[1] // 3
    shape = jax.ShapeDtypeStruct((seq, own), BF16)
    return pl.pallas_call(
        attend_kernel,
        out_shape=[shape] * 4,
        in_specs=[pl.BlockSpec(memory_space=pltpu.SMEM)]
        + [pl.BlockSpec(memory_space=pltpu.VMEM)] * 5,
        out_specs=[pl.BlockSpec(memory_space=pltpu.VMEM)] * 4,
        compiler_params=pltpu.CompilerParams(vmem_limit_bytes=56 << 20),
        cost_estimate=pl.CostEstimate(
            flops=4 * seq * seq * own, bytes_accessed=20 * seq * own, transcendentals=seq * seq
        ),
    )(length, qkv, squares, gains, cosine, sine)


def attend_back(length, qkv, squares, gains, cosine, sine, q, k, v, do):
    seq, own = q.shape
    wide = jax.ShapeDtypeStruct((seq, own), F32)
    return pl.pallas_call(
        attend_back_kernel,
        out_shape=[
            wide,
            wide,
            jax.ShapeDtypeStruct((seq, own), BF16),
            jax.ShapeDtypeStruct((seq, 2), F32),
            jax.ShapeDtypeStruct((2, own), F32),
        ],
        in_specs=[pl.BlockSpec(memory_space=pltpu.SMEM)]
        + [pl.BlockSpec(memory_space=pltpu.VMEM)] * 9,
        out_specs=[pl.BlockSpec(memory_space=pltpu.VMEM)] * 5,
        scratch_shapes=[pltpu.VMEM((seq, HEAD_DIM), F32)] * 2,
        compiler_params=pltpu.CompilerParams(vmem_limit_bytes=56 << 20),
        cost_estimate=pl.CostEstimate(
            flops=10 * seq * seq * own, bytes_accessed=40 * seq * own, transcendentals=seq * seq
        ),
    )(length, qkv, squares, gains, cosine, sine, q, k, v, do)


def body(
    tokens,
    seq_lengths,
    routes,
    w_query,
    w_key,
    w_value,
    w_out,
    gain_attn,
    gain_query,
    gain_key,
    gain_ffn,
    w_router,
    w_gate,
    w_up,
    w_down_t,
    cotangent,
):
    rows, width = tokens.shape
    local_experts, _, hidden_units = w_gate.shape
    groups, n_dp = lax.axis_size("expert"), lax.axis_size("dp")
    experts_all = local_experts * groups
    seq = groups * rows
    own = width // groups
    weight_rows = w_query.shape[0]
    me, dp = lax.axis_index("expert"), lax.axis_index("dp")
    ring = Ring(groups)
    positions = jnp.arange(seq, dtype=jnp.int32)
    my_rows = me * rows + jnp.arange(rows, dtype=jnp.int32)
    seq_length = lax.dynamic_index_in_dim(seq_lengths, dp, 0, keepdims=True)
    used = (my_rows < seq_length[0]).astype(F32)[:, None]

    expert_ids = jnp.arange(experts_all, dtype=jnp.int32)
    chosen = jnp.any(routes[:, :, None] == expert_ids[None, None, :], axis=1)
    chosen_low = chosen.astype(BF16)

    hit_columns = rows * local_experts // weight_rows
    hits_out = chosen_low.reshape(rows, groups, local_experts).transpose(1, 0, 2)
    extra = jnp.concatenate(
        [
            jnp.stack([gain_attn, gain_query, gain_key, gain_ffn], axis=1),
            w_router,
        ],
        axis=1,
    )
    extra_columns = extra.shape[1]
    pad = -(extra_columns + hit_columns) % 128
    send = jnp.concatenate(
        [w.reshape(weight_rows, groups, own).transpose(1, 0, 2) for w in (w_query, w_key, w_value)]
        + [
            jnp.broadcast_to(extra[None], (groups, weight_rows, extra_columns)),
            hits_out.reshape(groups, weight_rows, hit_columns),
            jnp.zeros((groups, weight_rows, pad), BF16),
        ],
        axis=2,
    )
    got = lax.all_to_all(send, "expert", split_axis=0, concat_axis=0, tiled=True)
    hits = got[:, :, 3 * own + extra_columns : 3 * own + extra_columns + hit_columns]
    hits = hits.reshape(seq, local_experts).astype(F32)
    projections = dp_gather(got.reshape(groups * weight_rows, -1), n_dp)
    w_qkv = projections[:, : 3 * own]
    small = projections[:, 3 * own : 3 * own + extra_columns]
    gains_full = small[:, :4].T.astype(F32)
    full_router = small[:, 4:]
    full_out = lax.all_gather(w_out, ("dp", "expert"), axis=0, tiled=True)
    cot_all = lax.all_gather(cotangent, "expert", axis=0, tiled=True)

    resid_in = tokens.astype(F32)
    attn_gain, ffn_gain = gains_full[0:1], gains_full[3:4]
    tokens_all = place_blocks(ring, ring.gather(tokens), rows, width)
    wide = tokens_all.astype(F32)
    attn_in = (wide * norm_scale(wide) * attn_gain).astype(BF16)
    qkv = matmul(attn_in, w_qkv)
    squares = jnp.stack(
        [
            jnp.sum(qkv[:, :own] ** 2, axis=1),
            jnp.sum(qkv[:, own : 2 * own] ** 2, axis=1),
        ]
    )
    squares = expert_sum(squares, groups).T
    gains_own = lax.dynamic_slice(gains_full, (1, me * own), (2, own))
    half = HEAD_DIM // 2
    frequency = ROPE_BASE ** (-(jnp.arange(half, dtype=F32) * 2.0) / HEAD_DIM)
    angles = positions.astype(F32)[:, None] * frequency[None, :]
    cosine, sine = jnp.cos(angles), jnp.sin(angles)
    cosine = jnp.concatenate([cosine, cosine], axis=1)
    sine = jnp.concatenate([-sine, sine], axis=1)
    q, k, v, attended = attend(seq_length, qkv, squares, gains_own, cosine, sine)
    attn_rows = lax.all_to_all(
        attended.reshape(groups, rows, own), "expert", split_axis=0, concat_axis=0, tiled=True
    )
    attn_rows = attn_rows.transpose(1, 0, 2).reshape(rows, width)
    attn_rows_all = lax.all_gather(attn_rows, "expert", axis=0, tiled=True)
    resid_mid = resid_in + matmul(attn_rows, full_out)
    mid_scale = norm_scale(resid_mid)
    ffn_in = (resid_mid * mid_scale * ffn_gain).astype(BF16)
    logits = matmul(ffn_in, full_router)
    probs = jax.nn.softmax(logits, axis=-1)

    ffn_all = place_blocks(ring, ring.gather(ffn_in), rows, width)
    logits_all = matmul(ffn_all, full_router)
    probs_all = jax.nn.softmax(logits_all, axis=-1)
    weights = lax.dynamic_slice(probs_all, (0, me * local_experts), (seq, local_experts)) * hits
    moe_part = 0.0
    pair_dots, scaled_hidden, dgates, dups = [], [], [], []
    for expert in range(local_experts):
        gate = matmul(ffn_all, w_gate[expert])
        up = matmul(ffn_all, w_up[expert])
        back = matmul(cot_all, w_down_t[expert])
        weight = weights[:, expert : expert + 1]
        sig = 1.0 / (1.0 + jnp.exp(-gate))
        silu = gate * sig
        hidden = silu * up
        pair_dots.append(jnp.sum(hidden * back, axis=1) * hits[:, expert])
        back = back * weight
        scaled_hidden.append((hidden * weight).astype(BF16))
        dgates.append((back * up * sig * (1.0 + gate * (1.0 - sig))).astype(BF16))
        dups.append((back * silu).astype(BF16))
        moe_part += matmul_nt(scaled_hidden[-1], w_down_t[expert])
    moe_rows = lax.psum_scatter(
        moe_part.astype(BF16), "expert", scatter_dimension=0, tiled=True
    ).astype(F32)
    output = (resid_mid + moe_rows).astype(BF16)
    drow_part = sum(
        matmul_nt(dgates[i], w_gate[i]) + matmul_nt(dups[i], w_up[i]) for i in range(local_experts)
    ).astype(BF16)
    pairs = jnp.stack(pair_dots, axis=1)
    spread = (
        (expert_ids[None, :] // local_experts == me) * jnp.tile(pairs, (1, groups))
    )
    high = spread.astype(BF16)
    low = (spread - high.astype(F32)).astype(BF16)
    drow_part = jnp.concatenate(
        [drow_part, high, low, jnp.zeros((seq, -2 * experts_all % 128), BF16)], axis=1
    )

    def drow_term(o):
        return lax.dynamic_slice(
            drow_part, (ring.natural[o] * rows, 0), (rows, drow_part.shape[1])
        )

    drow = ring.scatter(drow_term)

    slice_width = hidden_units // n_dp

    def expert_term(left, rights):
        def term(rel):
            first = (dp ^ rel) * slice_width
            return jnp.stack(
                [
                    matmul_tn(left, lax.dynamic_slice(right, (0, first), (seq, slice_width)))
                    for right in rights
                ]
            )

        return term

    expert_grads = [
        dp_reduce(expert_term(left, rights), n_dp)
        for left, rights in ((cot_all, scaled_hidden), (ffn_all, dgates), (ffn_all, dups))
    ]
    grad_down, grad_gate_w, grad_up_w = expert_grads

    grad_rows = cotangent.astype(F32)
    dprobs = drow[:, width : width + experts_all]
    dprobs = dprobs + drow[:, width + experts_all : width + 2 * experts_all]
    dlogits = probs * (dprobs - jnp.sum(probs * dprobs, axis=1, keepdims=True))
    dlogits = dlogits.astype(BF16)
    grad_router = matmul_tn(ffn_in, dlogits)
    dffn = drow[:, :width] + matmul_nt(dlogits, full_router)
    grad_gain_ffn = jnp.sum(dffn * resid_mid * mid_scale, axis=0, keepdims=True)
    scaled = dffn * ffn_gain
    mid_grads = (
        grad_rows
        + mid_scale * scaled
        - resid_mid * mid_scale**3 * jnp.mean(scaled * resid_mid, axis=1, keepdims=True)
    )
    mid_low = mid_grads.astype(BF16)
    attn_grads = matmul_nt(mid_low, full_out).astype(BF16)
    both = jnp.stack([attn_grads.reshape(rows, groups, own), mid_low.reshape(rows, groups, own)], 2)
    both = both.reshape(rows, groups, 2 * own).transpose(1, 0, 2)
    both = lax.all_to_all(both, "expert", split_axis=0, concat_axis=0, tiled=True)
    both = both.reshape(seq, 2 * own)
    grad_heads, mid_columns = both[:, :own], both[:, own:]

    dq, dk, dv, dots, dgains = attend_back(
        seq_length, qkv, squares, gains_own, cosine, sine, q, k, v, grad_heads
    )
    dots = expert_sum(dots.T, groups).T / width
    scales = lax.rsqrt(squares / width + EPSILON)
    factor = scales**3 * dots
    dq = (dq - qkv[:, :own] * factor[:, 0:1]).astype(BF16)
    dk = (dk - qkv[:, own : 2 * own] * factor[:, 1:2]).astype(BF16)
    dqkv = jnp.concatenate([dq, dk, dv], axis=1)
    dattn_part = matmul_nt(dqkv, w_qkv).astype(BF16)

    def dattn_term(o):
        return lax.dynamic_slice(dattn_part, (ring.natural[o] * rows, 0), (rows, width))

    dattn = ring.scatter(dattn_term)
    in_scale = norm_scale(resid_in)
    scaled = dattn * attn_gain
    input_grad = (
        mid_grads
        + in_scale * scaled
        - resid_in * in_scale**3 * jnp.mean(scaled * resid_in, axis=1, keepdims=True)
    ).astype(BF16)

    block = width // n_dp

    def projection_term(rel):
        first = (dp ^ rel) * block
        left = lax.dynamic_slice(attn_in, (0, first), (seq, block))
        left_out = lax.dynamic_slice(attn_rows_all, (0, first), (seq, block))
        return jnp.concatenate([matmul_tn(left, dqkv), matmul_tn(left_out, mid_columns)], axis=1)

    reduced = dp_reduce(projection_term, n_dp).astype(BF16)
    reduced = lax.all_to_all(
        reduced.reshape(groups, weight_rows, 4 * own),
        "expert",
        split_axis=0,
        concat_axis=0,
        tiled=True,
    ).astype(F32)
    grads = [
        reduced[:, :, i * own : (i + 1) * own].transpose(1, 0, 2).reshape(weight_rows, width)
        for i in range(4)
    ]
    grad_gain_attn = (
        sum(jnp.sum(g * w.astype(F32), axis=1) for g, w in zip(grads, (w_query, w_key, w_value)))
        / gain_attn.astype(F32)
    )

    spread_gains = lax.dynamic_update_slice(jnp.zeros((2, width), F32), dgains, (0, me * own))
    sums = jnp.zeros((1, width), F32)
    sums = sums.at[0, 0].set(jnp.sum(used * resid_mid * resid_mid))
    sums = sums.at[0, 1].set(jnp.sum(used * moe_rows * moe_rows))
    rest = jnp.concatenate([spread_gains, grad_gain_ffn, sums, grad_router.T], axis=0)
    rest = dp_sum(expert_sum(rest, groups), n_dp)
    mine = lax.dynamic_slice(
        rest, (0, (dp * groups + me) * weight_rows), (rest.shape[0], weight_rows)
    )
    counted = jnp.sum(seq_lengths).astype(F32) * width
    rms_resid = jnp.sqrt(rest[3, 0] / counted)
    rms_moe = jnp.sqrt(rest[3, 1] / counted)
    return (
        output,
        input_grad,
        grads[0],
        grads[1],
        grads[2],
        grads[3],
        grad_gain_attn,
        mine[0],
        mine[1],
        mine[2],
        mine[4:].T,
        grad_gate_w,
        grad_up_w,
        grad_down,
        rms_resid,
        rms_moe,
    )


def solution(mesh):
    both = ("dp", "expert")
    row, vector, expert = P(both, None), P(both), P("expert", None, None)
    placed = (
        row,
        P(),
        row,
        row,
        row,
        row,
        row,
        vector,
        vector,
        vector,
        vector,
        row,
        expert,
        expert,
        expert,
        row,
    )
    grads = P("expert", None, "dp")
    return jax.shard_map(
        body,
        mesh=mesh,
        in_specs=placed,
        out_specs=(row,) * 6 + (vector,) * 4 + (row, grads, grads, grads, P(), P()),
        check_vma=False,
    )
```

```python
import jax
import jax.numpy as jnp
import numpy as np
from jax import lax
from jax.experimental import pallas as pl
from jax.experimental.pallas import tpu as pltpu
from jax.sharding import PartitionSpec as P

HEADS = 16
HEAD_DIM = 128
TOP = 8
EPSILON = 1e-05
ROPE_BASE = 10000.0
SCALE = HEAD_DIM ** (-0.5)
NEG = -1e30
Z_CHIPS = 4
CORES = 2
F32 = jnp.float32
BF16 = jnp.bfloat16


def ring_tables(groups):
    x_chips = groups // Z_CHIPS
    walk = []
    for x in range(x_chips):
        column = range(1, Z_CHIPS) if x % 2 == 0 else range(Z_CHIPS - 1, 0, -1)
        walk += [z * x_chips + x for z in column]
    walk += [x for x in range(x_chips - 1, -1, -1)]
    place = np.zeros((groups,), np.int32)
    for at, owner in enumerate(walk):
        place[owner] = at
    return np.array(walk, np.int32), place


class Ring:
    def __init__(self, groups):
        self.size = groups
        self.walk, self.place = ring_tables(groups)
        size = groups
        self.ahead = [(int(self.walk[i]), int(self.walk[(i + 1) % size])) for i in range(size)]
        self.back = [(b, a) for a, b in self.ahead]
        mine = jnp.asarray(self.place)[lax.axis_index("expert")]
        self.natural = jnp.asarray(self.walk)[(mine + jnp.arange(size, dtype=jnp.int32)) % size]

    def up(self, value):
        return lax.ppermute(value, "expert", self.ahead)

    def down(self, value):
        return lax.ppermute(value, "expert", self.back)

    def gather(self, block, hooks=None):
        hooks = hooks or {}
        half = self.size // 2
        rows = block.shape[0]
        pieces = [(0, 0, block)]
        up, down = block, block
        for step in range(1, half):
            made = hooks[step](pieces) if step in hooks else ()
            up, down = together((self.up(up), self.down(down)), made)
            pieces += [(self.size - step, 0, up), (step, 0, down)]
        if half in hooks:
            hooks[half](pieces)
        pieces.append((half, 0, self.up(up[: rows // 2])))
        pieces.append((half, rows // 2, self.down(down[rows // 2 :])))
        return pieces

    def scatter(self, term, hooks=None):
        hooks = hooks or {}
        half = self.size // 2
        far = term(half)
        rows = far.shape[0]
        up = self.up(far[: rows // 2])
        down = self.down(far[rows // 2 :])

        def add(left, right):
            return (left.astype(F32) + right.astype(F32)).astype(BF16)

        for step in range(half - 1, 0, -1):
            made = hooks[half - step]() if half - step in hooks else ()
            up, down = together((up, down), made)
            ahead, behind = term(step), term(self.size - step)
            if step == half - 1:
                ahead = jnp.concatenate([add(up, ahead[: rows // 2]), ahead[rows // 2 :]], axis=0)
                behind = jnp.concatenate(
                    [behind[: rows // 2], add(down, behind[rows // 2 :])], axis=0
                )
            else:
                ahead, behind = add(up, ahead), add(down, behind)
            up, down = self.up(ahead), self.down(behind)
        made = hooks[half]() if half in hooks else ()
        up, down = together((up, down), made)
        return up.astype(F32) + down.astype(F32) + term(0).astype(F32)


def together(values, made):
    if not made:
        return values
    return lax.optimization_barrier((*values, *made))[: len(values)]


def place_blocks(ring, pieces, rows, width, dtype=BF16):
    buffer = jnp.zeros((ring.size * rows, width), dtype)
    for o, start, piece in pieces:
        buffer = lax.dynamic_update_slice(
            buffer, piece.astype(dtype), (ring.natural[o] * rows + start, 0)
        )
    return buffer


def expert_sum(value, groups):
    step = 1
    while step < groups:
        value = value + lax.ppermute(value, "expert", [(i, i ^ step) for i in range(groups)])
        step *= 2
    return value


def dp_sum(value, n_dp):
    step = 1
    while step < n_dp:
        value = value + lax.ppermute(value, "dp", [(i, i ^ step) for i in range(n_dp)])
        step *= 2
    return value


def dp_gather(chunk, n_dp):
    rows, width = chunk.shape
    me = lax.axis_index("dp")
    held = [(0, chunk)]
    for y in range(1, n_dp // CORES):
        held.append((2 * y, lax.ppermute(chunk, "dp", [(i, i ^ (2 * y)) for i in range(n_dp)])))
    swap = [(i, i ^ 1) for i in range(n_dp)]
    held += [(rel ^ 1, lax.ppermute(part, "dp", swap)) for rel, part in held]
    buffer = jnp.zeros((n_dp * rows, width), chunk.dtype)
    for rel, part in held:
        buffer = lax.dynamic_update_slice(buffer, part, ((me ^ rel) * rows, 0))
    return buffer


def dp_reduce(term, n_dp):
    swap = [(i, i ^ 1) for i in range(n_dp)]
    chips = n_dp // CORES
    other = [lax.ppermute(term(2 * y + 1).astype(BF16), "dp", swap) for y in range(chips)]
    total = None
    for y in range(1, chips):
        part = (term(2 * y) + other[y].astype(F32)).astype(BF16)
        part = lax.ppermute(part, "dp", [(i, i ^ (2 * y)) for i in range(n_dp)]).astype(F32)
        total = part if total is None else total + part
    own = term(0) + other[0].astype(F32)
    return own if total is None else own + total


def norm_scale(values):
    return lax.rsqrt(jnp.mean(values * values, axis=-1, keepdims=True) + EPSILON)


def matmul(left, right):
    return jnp.dot(left, right, preferred_element_type=F32)


def matmul_nt(left, right):
    return lax.dot_general(left, right, (((1,), (1,)), ((), ())), preferred_element_type=F32)


def matmul_tn(left, right):
    return lax.dot_general(left, right, (((0,), (0,)), ((), ())), preferred_element_type=F32)


def masked(scores, first_row, length):
    rows, columns = scores.shape
    row = first_row + lax.broadcasted_iota(jnp.int32, (rows, columns), 0)
    column = lax.broadcasted_iota(jnp.int32, (rows, columns), 1)
    return jnp.where((column <= row) & (column < length), scores * SCALE, NEG)


def turn(values, cosine, sine):
    return values * cosine + pltpu.roll(values, HEAD_DIM // 2, 1) * sine


def turn_back(values, cosine, sine):
    return values * cosine - pltpu.roll(values, HEAD_DIM // 2, 1) * sine


VMEM_LIMIT = 56 << 20
SMEM_SPEC = pl.BlockSpec(memory_space=pltpu.SMEM)
VMEM_SPEC = pl.BlockSpec(memory_space=pltpu.VMEM)
ANY_SPEC = pl.BlockSpec(memory_space=pl.ANY)


def params():
    return pltpu.CompilerParams(vmem_limit_bytes=VMEM_LIMIT)


def cost(flops, bytes_accessed, transcendentals=0):
    return pl.CostEstimate(
        flops=flops, bytes_accessed=bytes_accessed, transcendentals=transcendentals
    )


def as_rows(first, second):
    lane = lax.broadcasted_iota(jnp.int32, (first.shape[0], 128), 1)
    both = jnp.where(lane == 0, first, jnp.where(lane == 1, second, 0.0))
    return both.T[:8]


def as_columns(rows):
    return rows.T


def project_kernel(tokens_ref, gain_ref, w_ref, in_ref, qkv_ref, squares_ref):
    own = w_ref.shape[1] // 3
    values = tokens_ref[...].astype(F32)
    normed = (values * norm_scale(values) * gain_ref[...]).astype(BF16)
    in_ref[...] = normed
    qkv = matmul(normed, w_ref[...])
    qkv_ref[...] = qkv
    query, key = qkv[:, :own], qkv[:, own : 2 * own]
    squares_ref[...] = as_rows(
        jnp.sum(query * query, axis=1, keepdims=True), jnp.sum(key * key, axis=1, keepdims=True)
    )


def project(tokens, gain, w_qkv):
    seq, width = tokens.shape
    columns = w_qkv.shape[1]
    tile = min(256, seq)
    return pl.pallas_call(
        project_kernel,
        grid=(seq // tile,),
        out_shape=[
            jax.ShapeDtypeStruct((seq, width), BF16),
            jax.ShapeDtypeStruct((seq, columns), F32),
            jax.ShapeDtypeStruct((8, seq), F32),
        ],
        in_specs=[
            pl.BlockSpec((tile, width), lambda i: (i, 0)),
            pl.BlockSpec((1, width), lambda i: (0, 0)),
            pl.BlockSpec((width, columns), lambda i: (0, 0)),
        ],
        out_specs=[
            pl.BlockSpec((tile, width), lambda i: (i, 0)),
            pl.BlockSpec((tile, columns), lambda i: (i, 0)),
            pl.BlockSpec((8, tile), lambda i: (0, i)),
        ],
        compiler_params=params(),
        cost_estimate=cost(2 * seq * width * columns, 8 * seq * width),
    )(tokens, gain, w_qkv)


def attend_kernel(
    length_ref, qkv_ref, squares_ref, gain_ref, cos_ref, sin_ref, q_ref, k_ref, v_ref, o_ref
):
    seq, own = q_ref.shape
    tile = min(256, seq)
    width = HEADS * HEAD_DIM
    length = length_ref[0]
    for start in range(0, seq, tile):
        rows = slice(start, start + tile)
        squares = as_columns(squares_ref[:, rows])
        cosine, sine = cos_ref[rows, :], sin_ref[rows, :]
        for part, out_ref in ((0, q_ref), (1, k_ref)):
            scale = lax.rsqrt(squares[:, part : part + 1] / width + EPSILON)
            for first in range(0, own, HEAD_DIM):
                columns = slice(first, first + HEAD_DIM)
                raw = qkv_ref[rows, part * own + first : part * own + first + HEAD_DIM]
                normed = raw * scale * gain_ref[part : part + 1, columns]
                out_ref[rows, columns] = turn(normed, cosine, sine).astype(BF16)
        v_ref[rows, :] = qkv_ref[rows, 2 * own : 3 * own].astype(BF16)
    for first in range(0, own, HEAD_DIM):
        columns = slice(first, first + HEAD_DIM)
        for start in range(0, seq, tile):
            rows, keys = slice(start, start + tile), slice(0, start + tile)
            scores = masked(matmul_nt(q_ref[rows, columns], k_ref[keys, columns]), start, length)
            expo = jnp.exp(scores - jnp.max(scores, axis=-1, keepdims=True))
            total = jnp.sum(expo, axis=-1, keepdims=True)
            probs = (expo / total).astype(BF16)
            o_ref[rows, columns] = matmul(probs, v_ref[keys, columns]).astype(BF16)


def attend_back_kernel(
    length_ref,
    qkv_ref,
    squares_ref,
    gain_ref,
    cos_ref,
    sin_ref,
    q_ref,
    k_ref,
    v_ref,
    do_ref,
    dq_ref,
    dk_ref,
    dv_ref,
    dots_ref,
    dgain_ref,
    k_total,
    v_total,
):
    seq, own = q_ref.shape
    tile = min(256, seq)
    width = HEADS * HEAD_DIM
    length = length_ref[0]
    for first in range(0, own, HEAD_DIM):
        columns = slice(first, first + HEAD_DIM)
        k_total[...] = jnp.zeros_like(k_total)
        v_total[...] = jnp.zeros_like(v_total)
        for start in range(0, seq, tile):
            rows, keys = slice(start, start + tile), slice(0, start + tile)
            q, k, v = q_ref[rows, columns], k_ref[keys, columns], v_ref[keys, columns]
            do = do_ref[rows, columns]
            scores = masked(matmul_nt(q, k), start, length)
            expo = jnp.exp(scores - jnp.max(scores, axis=-1, keepdims=True))
            probs = expo / jnp.sum(expo, axis=-1, keepdims=True)
            dprobs = matmul_nt(do, v)
            mean = jnp.sum(probs * dprobs, axis=-1, keepdims=True)
            dscores = (probs * (dprobs - mean)).astype(BF16)
            dq_ref[rows, columns] = matmul(dscores, k) * SCALE
            k_total[keys, :] += matmul_tn(dscores, q)
            v_total[keys, :] += matmul_tn(probs.astype(BF16), do)
        dk_ref[:, columns] = k_total[...] * SCALE
        dv_ref[:, columns] = v_total[...].astype(BF16)
    dgain_ref[...] = jnp.zeros_like(dgain_ref)
    for start in range(0, seq, tile):
        rows = slice(start, start + tile)
        squares = as_columns(squares_ref[:, rows])
        cosine, sine = cos_ref[rows, :], sin_ref[rows, :]
        both = []
        for part, out_ref in ((0, dq_ref), (1, dk_ref)):
            scale = lax.rsqrt(squares[:, part : part + 1] / width + EPSILON)
            dot = jnp.zeros((tile, 1), F32)
            for first in range(0, own, HEAD_DIM):
                columns = slice(first, first + HEAD_DIM)
                raw = qkv_ref[rows, part * own + first : part * own + first + HEAD_DIM]
                grad = turn_back(out_ref[rows, columns], cosine, sine)
                dgain_ref[part : part + 1, columns] += jnp.sum(
                    grad * raw * scale, axis=0, keepdims=True
                )
                grad = grad * gain_ref[part : part + 1, columns]
                dot += jnp.sum(grad * raw, axis=-1, keepdims=True)
                out_ref[rows, columns] = grad * scale
            both.append(dot)
        dots_ref[:, rows] = as_rows(*both)


def attend(length, qkv, squares, gains, cosine, sine):
    seq, own = qkv.shape[0], qkv.shape[1] // 3
    shape = jax.ShapeDtypeStruct((seq, own), BF16)
    return pl.pallas_call(
        attend_kernel,
        out_shape=[shape] * 4,
        in_specs=[SMEM_SPEC] + [VMEM_SPEC] * 5,
        out_specs=[VMEM_SPEC] * 4,
        compiler_params=params(),
        cost_estimate=cost(4 * seq * seq * own, 20 * seq * own, seq * seq),
    )(length, qkv, squares, gains, cosine, sine)


def attend_back(length, qkv, squares, gains, cosine, sine, q, k, v, do):
    seq, own = q.shape
    wide = jax.ShapeDtypeStruct((seq, own), F32)
    return pl.pallas_call(
        attend_back_kernel,
        out_shape=[
            wide,
            wide,
            jax.ShapeDtypeStruct((seq, own), BF16),
            jax.ShapeDtypeStruct((8, seq), F32),
            jax.ShapeDtypeStruct((2, own), F32),
        ],
        in_specs=[SMEM_SPEC] + [VMEM_SPEC] * 9,
        out_specs=[VMEM_SPEC] * 5,
        scratch_shapes=[pltpu.VMEM((seq, HEAD_DIM), F32)] * 2,
        compiler_params=params(),
        cost_estimate=cost(10 * seq * seq * own, 40 * seq * own, seq * seq),
    )(length, qkv, squares, gains, cosine, sine, q, k, v, do)


def finish_kernel(
    dq_ref, dk_ref, dv_ref, qkv_ref, squares_ref, dots_ref, w_ref, dqkv_ref, din_ref
):
    own = dq_ref.shape[1]
    width = HEADS * HEAD_DIM
    scale = lax.rsqrt(as_columns(squares_ref[...]) / width + EPSILON)
    factor = scale * scale * scale * as_columns(dots_ref[...]) / width
    for part, grad_ref in ((0, dq_ref), (1, dk_ref)):
        columns = slice(part * own, (part + 1) * own)
        grad = grad_ref[...] - qkv_ref[:, columns] * factor[:, part : part + 1]
        dqkv_ref[:, columns] = grad.astype(BF16)
    dqkv_ref[:, 2 * own :] = dv_ref[...]
    din_ref[...] = matmul_nt(dqkv_ref[...], w_ref[...]).astype(BF16)


def finish(dq, dk, dv, qkv, squares, dots, w_qkv):
    seq, own = dq.shape
    width = w_qkv.shape[0]
    tile = min(256, seq)
    narrow = pl.BlockSpec((tile, own), lambda i: (i, 0))
    wide = pl.BlockSpec((tile, 3 * own), lambda i: (i, 0))
    flat = pl.BlockSpec((8, tile), lambda i: (0, i))
    return pl.pallas_call(
        finish_kernel,
        grid=(seq // tile,),
        out_shape=[
            jax.ShapeDtypeStruct((seq, 3 * own), BF16),
            jax.ShapeDtypeStruct((seq, width), BF16),
        ],
        in_specs=[narrow, narrow, narrow, wide, flat, flat]
        + [pl.BlockSpec((width, 3 * own), lambda i: (0, 0))],
        out_specs=[wide, pl.BlockSpec((tile, width), lambda i: (i, 0))],
        compiler_params=params(),
        cost_estimate=cost(6 * seq * width * own, 4 * seq * width),
    )(dq, dk, dv, qkv, squares, dots, w_qkv)


def expert_kernel(n_pieces, piece_rows, n_blocks, n_slices, index_ref, column_ref, *refs):
    pieces, refs = refs[:n_pieces], refs[n_pieces:]
    hits_refs, router_ref, refs = refs[:n_blocks], refs[n_blocks], refs[n_blocks + 1 :]
    local_experts, _, wide = refs[0].shape
    gate_ref, up_ref, gate_rows_ref, up_rows_ref, refs = *refs[:4], refs[4:]
    back_refs = refs[: n_blocks * local_experts]
    x_ref, weight_ref, dots_ref, made_ref, grads_ref, sems, row_sems = refs[-7:]
    rows_out, dots_out, *outs = refs[-7 - n_blocks - 5 : -7 - n_blocks]
    grad_outs = refs[-7 - n_blocks : -7]
    step = pl.program_id(0)
    total, block = x_ref.shape[0], x_ref.shape[0] // n_blocks
    hidden_units = wide * n_slices
    slot = lax.rem(step, 2)
    lane = lax.broadcasted_iota(jnp.int32, (total, 128), 1)

    def row_copy(source, target, at, which):
        return pltpu.make_async_copy(
            source.at[pl.ds(at * block, block)],
            target.at[pl.ds(index_ref[at] * block, block)],
            row_sems.at[which, at],
        )

    def made_copy(which, at, of_step, from_slot):
        span = local_experts * wide
        return pltpu.make_async_copy(
            made_ref.at[from_slot, which, pl.ds(at * block, block)],
            outs[which].at[
                pl.ds(index_ref[at] * block, block),
                pl.ds(pl.multiple_of(column_ref[of_step] * span, span), span),
            ],
            sems.at[from_slot, which, at],
        )

    def all_made(of_step, from_slot):
        return [made_copy(w, at, of_step, from_slot) for w in range(3) for at in range(n_blocks)]

    def hit_of(expert):
        return jnp.concatenate([ref[:, expert : expert + 1] for ref in hits_refs], axis=0)

    @pl.when(step == 0)
    def _():
        start = 0
        for piece, rows in zip(pieces, piece_rows):
            x_ref[start : start + rows, :] = piece[...]
            start += rows
        for at in range(n_blocks):
            row_copy(x_ref, rows_out, at, 0).start()
        logits = matmul(x_ref[...], router_ref[...])
        expo = jnp.exp(logits - jnp.max(logits, axis=-1, keepdims=True))
        probs = expo / jnp.sum(expo, axis=-1, keepdims=True)
        which = lax.broadcasted_iota(jnp.int32, probs.shape, 1)
        weights = jnp.zeros((total, 128), F32)
        for expert in range(local_experts):
            mine = which == index_ref[n_blocks] * local_experts + expert
            weight = jnp.sum(jnp.where(mine, probs, 0.0), axis=-1, keepdims=True)
            weights = jnp.where(lane == expert, weight * hit_of(expert), weights)
        weight_ref[...] = weights
        dots_ref[...] = jnp.zeros_like(dots_ref)

    @pl.when((step >= 2) & (step < n_slices))
    def _():
        for copy in all_made(step - 2, slot):
            copy.wait()

    @pl.when(step < n_slices)
    def _():
        for expert in range(local_experts):
            gate = matmul(x_ref[...], gate_ref[expert])
            up = matmul(x_ref[...], up_ref[expert])
            back = jnp.concatenate(
                [ref[...] for ref in back_refs[n_blocks * expert : n_blocks * (expert + 1)]], axis=0
            ).astype(F32)
            weight = weight_ref[:, expert : expert + 1]
            sig = 0.5 + 0.5 * jnp.tanh(0.5 * gate)
            silu = gate * sig
            hidden = silu * up
            dot = jnp.sum(hidden * back, axis=-1, keepdims=True)
            dots_ref[...] += jnp.where(lane == expert, dot, 0.0)
            back = back * weight
            dgate = (back * up * (sig + silu * (1.0 - sig))).astype(BF16)
            dup = (back * silu).astype(BF16)
            columns = slice(expert * wide, (expert + 1) * wide)
            made_ref[slot, 0, :, columns] = (hidden * weight).astype(BF16)
            for which, value in ((0, dgate), (1, dup)):
                made_ref[slot, 1 + which, :, columns] = value
                first = (which * local_experts + expert) * hidden_units
                grads_ref[:, pl.ds(pl.multiple_of(first + step * wide, wide), wide)] = value
        for copy in all_made(step, slot):
            copy.start()

    @pl.when(step == n_slices - 1)
    def _():
        for expert in range(local_experts):
            dots_ref[...] = jnp.where(lane == expert, dots_ref[...] * hit_of(expert), dots_ref[...])
        for at in range(n_blocks):
            row_copy(dots_ref, dots_out, at, 1).start()

    @pl.when(step >= n_slices)
    def _():
        result = None
        for which, weights in enumerate((gate_rows_ref, up_rows_ref)):
            for expert in range(local_experts):
                first = (which * local_experts + expert) * hidden_units
                part = matmul_nt(grads_ref[:, first : first + hidden_units], weights[expert])
                result = part if result is None else result + part
        for at in range(n_blocks):
            grad_outs[at][...] = result[at * block : (at + 1) * block].astype(BF16)

    @pl.when(step == pl.num_programs(0) - 1)
    def _():
        for at in range(n_blocks):
            row_copy(x_ref, rows_out, at, 0).wait()
            row_copy(dots_ref, dots_out, at, 1).wait()
        for copy in all_made(n_slices - 1, (n_slices - 1) % 2) + all_made(
            n_slices - 2, n_slices % 2
        ):
            copy.wait()


def expert_call(index, column_place, pieces, hits, router, w_gate, w_up, backs, held, seq):
    local_experts, width, hidden_units = w_gate.shape
    n_slices, n_blocks = column_place.shape[0], index.shape[0] - 1
    wide = hidden_units // n_slices
    total = sum(piece.shape[0] for piece in pieces)
    block = total // n_blocks
    span = local_experts * hidden_units
    tile = 512
    assert n_slices >= 2

    def at_slice(step):
        return jnp.minimum(step, n_slices - 1)

    def at_tile(step):
        return jnp.maximum(step - n_slices, 0)

    weight_spec = pl.BlockSpec(
        (local_experts, width, wide), lambda i, index, column: (0, 0, at_slice(i))
    )
    rows_spec = pl.BlockSpec(
        (local_experts, tile, hidden_units), lambda i, index, column: (0, at_tile(i), 0)
    )

    def block_spec(at, columns, tiled):
        if tiled:
            return pl.BlockSpec(
                (block, columns), lambda i, index, column: (index[at], at_slice(i))
            )
        return pl.BlockSpec((block, columns), lambda i, index, column: (index[at], 0))

    in_specs = [pl.BlockSpec(piece.shape, lambda i, index, column: (0, 0)) for piece in pieces]
    in_specs += [block_spec(at, local_experts, False) for at in range(n_blocks)]
    in_specs += [pl.BlockSpec(router.shape, lambda i, index, column: (0, 0))]
    in_specs += [weight_spec, weight_spec, rows_spec, rows_spec]
    in_specs += [block_spec(at, wide, True) for _ in range(local_experts) for at in range(n_blocks)]
    operands = [*pieces, *[hits] * n_blocks, router, w_gate, w_up, w_gate, w_up]
    operands += [back for back in backs for _ in range(n_blocks)]
    aliases = {}
    if held is not None:
        aliases = {2 + len(operands) + i: i for i in range(5)}
        in_specs += [ANY_SPEC] * 5
        operands += held
    made = jax.ShapeDtypeStruct((seq, span), BF16)
    rows = [piece.shape[0] for piece in pieces]
    results = pl.pallas_call(
        lambda *refs: expert_kernel(len(pieces), rows, n_blocks, n_slices, *refs),
        out_shape=[
            jax.ShapeDtypeStruct((seq, width), BF16),
            jax.ShapeDtypeStruct((seq, 128), F32),
            made,
            made,
            made,
        ]
        + [jax.ShapeDtypeStruct((block, width), BF16)] * n_blocks,
        grid_spec=pltpu.PrefetchScalarGridSpec(
            num_scalar_prefetch=2,
            grid=(n_slices + width // tile,),
            in_specs=in_specs,
            out_specs=[ANY_SPEC] * 5
            + [pl.BlockSpec((block, tile), lambda i, index, column: (0, at_tile(i)))] * n_blocks,
            scratch_shapes=[
                pltpu.VMEM((total, width), BF16),
                pltpu.VMEM((total, 128), F32),
                pltpu.VMEM((total, 128), F32),
                pltpu.VMEM((2, 3, total, local_experts * wide), BF16),
                pltpu.VMEM((total, 2 * span), BF16),
                pltpu.SemaphoreType.DMA((2, 3, n_blocks)),
                pltpu.SemaphoreType.DMA((2, n_blocks)),
            ],
        ),
        input_output_aliases=aliases,
        compiler_params=params(),
        cost_estimate=cost(
            8 * total * width * span, 8 * width * span + 10 * total * span, total * span
        ),
    )(index, column_place, *operands)
    return results[:5], results[5:]


def back_rows_kernel(n_blocks, n_arrays, index_ref, column_ref, *refs):
    rows_refs, refs = refs[: n_blocks * n_arrays], refs[n_blocks * n_arrays :]
    weight_refs, outs, held = refs[:n_arrays], refs[n_arrays:-1], refs[-1]
    local_experts, _, hidden_units = weight_refs[0].shape
    n_slices = column_ref.shape[0]
    wide = hidden_units // n_slices
    block = rows_refs[0].shape[0]

    @pl.when(pl.program_id(0) == 0)
    def _():
        for at in range(n_blocks):
            for array in range(n_arrays):
                for expert in range(local_experts):
                    for part in range(n_slices):
                        first = (array * local_experts + expert) * hidden_units + part * wide
                        source = pl.multiple_of(
                            (column_ref[part] * local_experts + expert) * wide, 128
                        )
                        held[at * block : (at + 1) * block, first : first + wide] = rows_refs[
                            at * n_arrays + array
                        ][:, pl.ds(source, wide)]

    total = None
    for array in range(n_arrays):
        for expert in range(local_experts):
            first = (array * local_experts + expert) * hidden_units
            part = matmul_nt(held[:, first : first + hidden_units], weight_refs[array][expert])
            total = part if total is None else total + part
    for at in range(n_blocks):
        outs[at][...] = total[at * block : (at + 1) * block].astype(BF16)


def back_rows(index, column_place, arrays, weights, block, tile=256):
    n_blocks, n_arrays = index.shape[0], len(arrays)
    local_experts, width, hidden_units = weights[0].shape
    span = local_experts * hidden_units

    def row_spec(at):
        return pl.BlockSpec((block, span), lambda i, index, column: (index[at], 0))

    return pl.pallas_call(
        lambda *refs: back_rows_kernel(n_blocks, n_arrays, *refs),
        out_shape=[jax.ShapeDtypeStruct((block, width), BF16)] * n_blocks,
        grid_spec=pltpu.PrefetchScalarGridSpec(
            num_scalar_prefetch=2,
            grid=(width // tile,),
            in_specs=[row_spec(at) for at in range(n_blocks) for _ in range(n_arrays)]
            + [
                pl.BlockSpec(
                    (local_experts, tile, hidden_units), lambda i, index, column: (0, i, 0)
                )
            ]
            * n_arrays,
            out_specs=[pl.BlockSpec((block, tile), lambda i, index, column: (0, i))] * n_blocks,
            scratch_shapes=[pltpu.VMEM((n_blocks * block, n_arrays * span), BF16)],
        ),
        compiler_params=params(),
        cost_estimate=cost(
            2 * n_blocks * block * width * span * n_arrays, 2 * width * span * n_arrays
        ),
    )(index, column_place, *(list(arrays) * n_blocks), *weights)


def weight_grad_kernel(n_adds, left_ref, right_ref, *refs):
    total = matmul_tn(left_ref[...], right_ref[...])
    for ref in refs[:n_adds]:
        total += ref[...].astype(F32)
    out_ref = refs[-1]
    if len(out_ref.shape) == 2:
        out_ref[...] = total.astype(out_ref.dtype)
    else:
        wide = out_ref.shape[2]
        for expert in range(out_ref.shape[0]):
            out_ref[expert] = total[:, expert * wide : (expert + 1) * wide]


def weight_grad(left, right, first, columns, adds=(), experts=None, tile=512):
    seq, width = left.shape
    assert first % columns == 0
    if experts is None:
        out_shape = jax.ShapeDtypeStruct((width, columns), BF16)
        out_spec = pl.BlockSpec((tile, columns), lambda i: (i, 0))
    else:
        out_shape = jax.ShapeDtypeStruct((experts, width, columns // experts), F32)
        out_spec = pl.BlockSpec((experts, tile, columns // experts), lambda i: (0, i, 0))

    def add_spec(at):
        return pl.BlockSpec((tile, columns), lambda i: (i, at))

    return pl.pallas_call(
        lambda *refs: weight_grad_kernel(len(adds), *refs),
        out_shape=out_shape,
        grid=(width // tile,),
        in_specs=[
            pl.BlockSpec((seq, tile), lambda i: (0, i)),
            pl.BlockSpec((seq, columns), lambda i: (0, first // columns)),
        ]
        + [add_spec(at) for _, at in adds],
        out_specs=out_spec,
        compiler_params=params(),
        cost_estimate=cost(2 * seq * width * columns, 2 * width * (seq + columns)),
    )(left, right, *(value for value, _ in adds))


def body(
    tokens,
    seq_lengths,
    routes,
    w_query,
    w_key,
    w_value,
    w_out,
    gain_attn,
    gain_query,
    gain_key,
    gain_ffn,
    w_router,
    w_gate,
    w_up,
    w_down_t,
    cotangent,
):
    rows, width = tokens.shape
    local_experts, _, hidden_units = w_gate.shape
    groups, n_dp = lax.axis_size("expert"), lax.axis_size("dp")
    experts_all = local_experts * groups
    seq = groups * rows
    own = width // groups
    weight_rows = w_query.shape[0]
    chips = n_dp // CORES
    me, dp = lax.axis_index("expert"), lax.axis_index("dp")
    both_axes = ("dp", "expert")
    ring = Ring(groups)
    positions = jnp.arange(seq, dtype=jnp.int32)
    my_rows = me * rows + jnp.arange(rows, dtype=jnp.int32)
    seq_length = lax.dynamic_index_in_dim(seq_lengths, dp, 0, keepdims=True)
    used = (my_rows < seq_length[0]).astype(F32)[:, None]

    expert_ids = jnp.arange(experts_all, dtype=jnp.int32)
    chosen = jnp.any(routes[:, :, None] == expert_ids[None, None, :], axis=1)
    chosen_low = chosen.astype(BF16)

    hit_columns = rows * local_experts // weight_rows
    hits_out = chosen_low.reshape(rows, groups, local_experts).transpose(1, 0, 2)
    extra = jnp.concatenate(
        [jnp.stack([gain_attn, gain_query, gain_key, gain_ffn], axis=1), w_router], axis=1
    )
    extra_columns = extra.shape[1]
    pad = -(extra_columns + hit_columns) % 128
    send = jnp.concatenate(
        [w.reshape(weight_rows, groups, own).transpose(1, 0, 2) for w in (w_query, w_key, w_value)]
        + [
            jnp.broadcast_to(extra[None], (groups, weight_rows, extra_columns)),
            hits_out.reshape(groups, weight_rows, hit_columns),
            jnp.zeros((groups, weight_rows, pad), BF16),
        ],
        axis=2,
    )
    got = lax.all_to_all(send, "expert", split_axis=0, concat_axis=0, tiled=True)
    hits = got[:, :, 3 * own + extra_columns : 3 * own + extra_columns + hit_columns]
    hits = hits.reshape(seq, local_experts).astype(F32)
    projections = dp_gather(got.reshape(groups * weight_rows, -1), n_dp)
    w_qkv = projections[:, : 3 * own]
    small = projections[:, 3 * own : 3 * own + extra_columns]
    gains_full = small[:, :4].T.astype(F32)
    full_router = small[:, 4:]
    moves = [(e * n_dp + i, i * groups + e) for e in range(groups) for i in range(n_dp)]
    own_out = dp_gather(lax.ppermute(w_out, both_axes, moves), n_dp)

    resid_in = tokens.astype(F32)
    attn_gain, ffn_gain = gains_full[0:1], gains_full[3:4]
    tokens_all = place_blocks(ring, ring.gather(tokens), rows, width)
    [cot_own] = together((cotangent,), (tokens_all,))
    cot_all = lax.all_gather(cot_own, "expert", axis=0, tiled=True)
    attn_in, qkv, squares = project(tokens_all, attn_gain, w_qkv)
    own_out, squares = lax.optimization_barrier((own_out, squares))
    squares = expert_sum(squares, groups)
    gains_own = lax.dynamic_slice(gains_full, (1, me * own), (2, own))
    half = HEAD_DIM // 2
    frequency = ROPE_BASE ** (-(jnp.arange(half, dtype=F32) * 2.0) / HEAD_DIM)
    angles = positions.astype(F32)[:, None] * frequency[None, :]
    cosine, sine = jnp.cos(angles), jnp.sin(angles)
    cosine = jnp.concatenate([cosine, cosine], axis=1)
    sine = jnp.concatenate([-sine, sine], axis=1)
    q, k, v, attended = attend(seq_length, qkv, squares, gains_own, cosine, sine)

    def block_of(value, o):
        return lax.dynamic_slice(value, (ring.natural[o] * rows, 0), (rows, value.shape[1]))

    far = groups // 2
    out_far = matmul(block_of(attended, far), own_out).astype(BF16)
    out_part = matmul(attended, own_out).astype(BF16)
    backs = []

    def make_back(expert):
        backs.append(matmul(cot_all, w_down_t[expert]).astype(BF16))
        return (backs[-1],)

    hooks = {
        2: lambda: make_back(0),
        3: lambda: [make_back(expert)[0] for expert in range(1, local_experts)],
    }
    resid_mid = resid_in + ring.scatter(
        lambda o: out_far if o == far else block_of(out_part, o), hooks
    )
    mid_scale = norm_scale(resid_mid)
    ffn_in = (resid_mid * mid_scale * ffn_gain).astype(BF16)

    distances = (
        [2 * y + 1 for y in range(chips)] + [2 * y for y in range(1, chips)] + [0]
    )
    place_of = np.zeros((n_dp,), np.int32)
    place_of[np.array(distances)] = np.arange(n_dp)
    column_place = jnp.asarray(place_of)[jnp.arange(n_dp, dtype=jnp.int32) ^ dp]
    per_call = 4
    calls = groups // per_call
    held, drow_terms = [], {}

    def expert_pieces(pieces, at):
        given = pieces[at:] if at + per_call == groups else pieces[at : at + per_call]
        order = [o for o, _, _ in given[:per_call]]
        result, blocks = expert_call(
            jnp.stack([ring.natural[o] for o in order] + [me]),
            column_place,
            [piece for _, _, piece in given],
            hits,
            full_router,
            w_gate,
            w_up,
            backs,
            held[-1] if held else None,
            seq,
        )
        held.append(result)
        drow_terms.update(zip(order, blocks))
        return result

    hooks = {}
    for call in range(calls - 1):
        step = (call + 1) * per_call // 2 + 1
        hooks[step] = lambda pieces, at=call * per_call: expert_pieces(pieces, at)
    pieces = ring.gather(ffn_in, hooks)
    expert_pieces(pieces, groups - per_call)
    ffn_all, pair_dots, scaled_hidden, dgates, dups = held[-1]
    pairs = []

    def make_pairs():
        out = pair_dots[:, :local_experts].reshape(groups, rows, local_experts).transpose(0, 2, 1)
        pairs.append(lax.all_to_all(out, "expert", split_axis=0, concat_axis=0, tiled=True))
        return tuple(pairs)

    slice_columns = local_experts * hidden_units // n_dp
    swap = [(i, i ^ 1) for i in range(n_dp)]
    sides = [(cot_all, scaled_hidden), (ffn_all, dgates), (ffn_all, dups)]
    other, adds = {}, {}

    def make_sent(which):
        sent = weight_grad(*sides[which], 0, chips * slice_columns)
        other[which] = lax.ppermute(sent, "dp", swap)
        adds[which] = [(other[which], 0)]
        return (sent,)

    parts = {}

    def make_part(which):
        parts[which] = [
            weight_grad(
                *sides[which],
                (chips + y - 1) * slice_columns,
                slice_columns,
                [(other[which], y)],
            )
            for y in range(1, chips)
        ]
        return tuple(parts[which])

    def send_part(which, after):
        sent = together(tuple(parts[which]), (after,))
        got = [
            lax.ppermute(part, "dp", [(i, i ^ (2 * y)) for i in range(n_dp)])
            for y, part in zip(range(1, chips), sent)
        ]
        adds[which] += [(part, 0) for part in got]
        return tuple(got)

    hooks = {
        far - 2: lambda: make_sent(0),
        far - 1: lambda: (*make_sent(1), *make_part(0)),
        far: lambda: (*make_pairs(), *make_sent(2), *make_part(1)),
    }
    drow = ring.scatter(lambda o: drow_terms[o], hooks)

    grad_rows = cotangent.astype(F32)
    dprobs = pairs[0].reshape(experts_all, rows).T
    probs = jax.nn.softmax(matmul(ffn_in, full_router), axis=-1)
    dlogits = probs * (dprobs - jnp.sum(probs * dprobs, axis=1, keepdims=True))
    dlogits = dlogits.astype(BF16)
    grad_router = matmul_tn(ffn_in, dlogits)
    dffn = drow + matmul_nt(dlogits, full_router)
    grad_gain_ffn = jnp.sum(dffn * resid_mid * mid_scale, axis=0, keepdims=True)
    scaled = dffn * ffn_gain
    mid_grads = (
        grad_rows
        + mid_scale * scaled
        - resid_mid * mid_scale**3 * jnp.mean(scaled * resid_mid, axis=1, keepdims=True)
    )
    mid_low = mid_grads.astype(BF16)

    def make_moe(pieces):
        return back_rows(
            jnp.zeros((1,), jnp.int32), column_place, (scaled_hidden,), (w_down_t,), seq
        )

    moe_made = []
    first = send_part(0, mid_low)
    mid_pieces = ring.gather(
        mid_low,
        {
            1: lambda pieces: make_part(2),
            2: lambda pieces: moe_made.extend(make_moe(pieces)) or moe_made,
        },
    )
    mid_all = place_blocks(ring, mid_pieces, rows, width)
    [mid_all] = together((mid_all,), first)
    second = send_part(1, mid_all)
    grad_heads = matmul_nt(mid_all, own_out).astype(BF16)

    moe_part, grad_heads = lax.optimization_barrier((moe_made[0], grad_heads))
    moe_rows = lax.psum_scatter(moe_part, "expert", scatter_dimension=0, tiled=True).astype(F32)
    output = (resid_mid + moe_rows).astype(BF16)

    dq, dk, dv, dots, dgains = attend_back(
        seq_length, qkv, squares, gains_own, cosine, sine, q, k, v, grad_heads
    )
    dots = expert_sum(dots, groups)
    dqkv, din_part = finish(dq, dk, dv, qkv, squares, dots, w_qkv)
    third = []

    def make_own(which, after):
        left, right = sides[which]
        [left] = together((left,), after)
        return weight_grad(
            left,
            right,
            (n_dp - 1) * slice_columns,
            slice_columns,
            adds[which],
            local_experts,
        )

    def middle():
        third.extend(send_part(2, second[0]))
        return second

    hooks = {far - 2: middle}
    dattn = ring.scatter(lambda o: block_of(din_part, o), hooks)
    grad_down, grad_gate_w = make_own(0, (dattn,)), make_own(1, (dattn,))
    grad_up_w = make_own(2, (dattn,))
    in_scale = norm_scale(resid_in)
    scaled = dattn * attn_gain
    input_grad = (
        mid_grads
        + in_scale * scaled
        - resid_in * in_scale**3 * jnp.mean(scaled * resid_in, axis=1, keepdims=True)
    ).astype(BF16)

    block = width // n_dp

    def projection_term(rel):
        left = lax.dynamic_slice(attn_in, (0, (dp ^ rel) * block), (seq, block))
        return matmul_tn(left, dqkv)

    reduced = dp_reduce(projection_term, n_dp).astype(BF16)
    reduced = lax.all_to_all(
        reduced.reshape(groups, weight_rows, 3 * own),
        "expert",
        split_axis=0,
        concat_axis=0,
        tiled=True,
    ).astype(F32)
    grads = [
        reduced[:, :, i * own : (i + 1) * own].transpose(1, 0, 2).reshape(weight_rows, width)
        for i in range(3)
    ]
    grad_gain_attn = (
        sum(jnp.sum(g * w.astype(F32), axis=1) for g, w in zip(grads, (w_query, w_key, w_value)))
        / gain_attn.astype(F32)
    )
    out_grads = matmul_tn(attended, mid_all)

    def out_term(rel):
        return lax.dynamic_slice(out_grads, ((dp ^ rel) * weight_rows, 0), (weight_rows, width))

    grad_out = dp_reduce(out_term, n_dp).astype(BF16)
    grad_out = lax.ppermute(grad_out, both_axes, [(b, a) for a, b in moves]).astype(F32)

    spread_gains = lax.dynamic_update_slice(jnp.zeros((2, width), F32), dgains, (0, me * own))
    lane = lax.broadcasted_iota(jnp.int32, (1, width), 1)
    sums = jnp.where(
        lane == 0,
        jnp.sum(used * resid_mid * resid_mid),
        jnp.where(lane == 1, jnp.sum(used * moe_rows * moe_rows), 0.0),
    )
    rest = jnp.concatenate([spread_gains, grad_gain_ffn, sums, grad_router.T], axis=0)
    [rest] = together((rest,), (dattn,))
    rest = dp_sum(expert_sum(rest, groups), n_dp)
    mine = lax.dynamic_slice(
        rest, (0, (dp * groups + me) * weight_rows), (rest.shape[0], weight_rows)
    )
    counted = jnp.sum(seq_lengths).astype(F32) * width
    rms_resid = jnp.sqrt(rest[3, 0] / counted)
    rms_moe = jnp.sqrt(rest[3, 1] / counted)
    return (
        output,
        input_grad,
        grads[0],
        grads[1],
        grads[2],
        grad_out,
        grad_gain_attn,
        mine[0],
        mine[1],
        mine[2],
        mine[4:].T,
        grad_gate_w,
        grad_up_w,
        grad_down,
        rms_resid,
        rms_moe,
    )


def solution(mesh):
    both = ("dp", "expert")
    row, vector, expert = P(both, None), P(both), P("expert", None, None)
    placed = (
        row,
        P(),
        row,
        row,
        row,
        row,
        row,
        vector,
        vector,
        vector,
        vector,
        row,
        expert,
        expert,
        expert,
        row,
    )
    grads = P("expert", None, "dp")
    return jax.shard_map(
        body,
        mesh=mesh,
        in_specs=placed,
        out_specs=(row,) * 6 + (vector,) * 4 + (row, grads, grads, grads, P(), P()),
        check_vma=False,
    )
```

```python
import jax
import jax.numpy as jnp
import numpy as np
from jax import lax
from jax.experimental import pallas as pl
from jax.experimental.pallas import tpu as pltpu
from jax.sharding import PartitionSpec as P

HEADS = 16
HEAD_DIM = 128
TOP = 8
EPSILON = 1e-05
ROPE_BASE = 10000.0
SCALE = HEAD_DIM ** (-0.5)
NEG = -1e30
Z_CHIPS = 4
CORES = 2
F32 = jnp.float32
BF16 = jnp.bfloat16


def ring_tables(groups):
    x_chips = groups // Z_CHIPS
    walk = []
    for x in range(x_chips):
        column = range(1, Z_CHIPS) if x % 2 == 0 else range(Z_CHIPS - 1, 0, -1)
        walk += [z * x_chips + x for z in column]
    walk += [x for x in range(x_chips - 1, -1, -1)]
    place = np.zeros((groups,), np.int32)
    for at, owner in enumerate(walk):
        place[owner] = at
    return np.array(walk, np.int32), place


class Ring:
    def __init__(self, groups):
        self.size = groups
        self.walk, self.place = ring_tables(groups)
        size = groups
        self.ahead = [(int(self.walk[i]), int(self.walk[(i + 1) % size])) for i in range(size)]
        self.back = [(b, a) for a, b in self.ahead]
        mine = jnp.asarray(self.place)[lax.axis_index("expert")]
        self.natural = jnp.asarray(self.walk)[(mine + jnp.arange(size, dtype=jnp.int32)) % size]

    def up(self, value):
        return lax.ppermute(value, "expert", self.ahead)

    def down(self, value):
        return lax.ppermute(value, "expert", self.back)

    def gather(self, block, hooks=None):
        hooks = hooks or {}
        half = self.size // 2
        rows = block.shape[0]
        pieces = [(0, 0, block)]
        up, down = block, block
        for step in range(1, half):
            made = hooks[step](pieces) if step in hooks else ()
            up, down = together((self.up(up), self.down(down)), made)
            pieces += [(self.size - step, 0, up), (step, 0, down)]
        if half in hooks:
            hooks[half](pieces)
        pieces.append((half, 0, self.up(up[: rows // 2])))
        pieces.append((half, rows // 2, self.down(down[rows // 2 :])))
        return pieces

    def scatter(self, term, hooks=None):
        hooks = hooks or {}
        half = self.size // 2
        far = term(half)
        rows = far.shape[0]
        up = self.up(far[: rows // 2])
        down = self.down(far[rows // 2 :])

        def add(left, right):
            return (left.astype(F32) + right.astype(F32)).astype(BF16)

        for step in range(half - 1, 0, -1):
            made = hooks[half - step]() if half - step in hooks else ()
            up, down = together((up, down), made)
            ahead, behind = term(step), term(self.size - step)
            if step == half - 1:
                ahead = jnp.concatenate([add(up, ahead[: rows // 2]), ahead[rows // 2 :]], axis=0)
                behind = jnp.concatenate(
                    [behind[: rows // 2], add(down, behind[rows // 2 :])], axis=0
                )
            else:
                ahead, behind = add(up, ahead), add(down, behind)
            up, down = self.up(ahead), self.down(behind)
        made = hooks[half]() if half in hooks else ()
        up, down = together((up, down), made)
        return up.astype(F32) + down.astype(F32) + term(0).astype(F32)


def together(values, made):
    if not made:
        return values
    return lax.optimization_barrier((*values, *made))[: len(values)]


def place_blocks(ring, pieces, rows, width, dtype=BF16):
    buffer = jnp.zeros((ring.size * rows, width), dtype)
    for o, start, piece in pieces:
        buffer = lax.dynamic_update_slice(
            buffer, piece.astype(dtype), (ring.natural[o] * rows + start, 0)
        )
    return buffer


def expert_sum(value, groups):
    step = 1
    while step < groups:
        value = value + lax.ppermute(value, "expert", [(i, i ^ step) for i in range(groups)])
        step *= 2
    return value


def dp_sum(value, n_dp):
    step = 1
    while step < n_dp:
        value = value + lax.ppermute(value, "dp", [(i, i ^ step) for i in range(n_dp)])
        step *= 2
    return value


def dp_gather(chunk, n_dp):
    rows, width = chunk.shape
    me = lax.axis_index("dp")
    held = [(0, chunk)]
    for y in range(1, n_dp // CORES):
        held.append((2 * y, lax.ppermute(chunk, "dp", [(i, i ^ (2 * y)) for i in range(n_dp)])))
    swap = [(i, i ^ 1) for i in range(n_dp)]
    held += [(rel ^ 1, lax.ppermute(part, "dp", swap)) for rel, part in held]
    buffer = jnp.zeros((n_dp * rows, width), chunk.dtype)
    for rel, part in held:
        buffer = lax.dynamic_update_slice(buffer, part, ((me ^ rel) * rows, 0))
    return buffer


def dp_reduce(term, n_dp):
    swap = [(i, i ^ 1) for i in range(n_dp)]
    chips = n_dp // CORES
    other = [lax.ppermute(term(2 * y + 1).astype(BF16), "dp", swap) for y in range(chips)]
    total = None
    for y in range(1, chips):
        part = (term(2 * y) + other[y].astype(F32)).astype(BF16)
        part = lax.ppermute(part, "dp", [(i, i ^ (2 * y)) for i in range(n_dp)]).astype(F32)
        total = part if total is None else total + part
    own = term(0) + other[0].astype(F32)
    return own if total is None else own + total


def norm_scale(values):
    return lax.rsqrt(jnp.mean(values * values, axis=-1, keepdims=True) + EPSILON)


def matmul(left, right):
    return jnp.dot(left, right, preferred_element_type=F32)


def matmul_nt(left, right):
    return lax.dot_general(left, right, (((1,), (1,)), ((), ())), preferred_element_type=F32)


def matmul_tn(left, right):
    return lax.dot_general(left, right, (((0,), (0,)), ((), ())), preferred_element_type=F32)


def masked(scores, first_row, length):
    rows, columns = scores.shape
    row = first_row + lax.broadcasted_iota(jnp.int32, (rows, columns), 0)
    column = lax.broadcasted_iota(jnp.int32, (rows, columns), 1)
    return jnp.where((column <= row) & (column < length), scores * SCALE, NEG)


def turn(values, cosine, sine):
    return values * cosine + pltpu.roll(values, HEAD_DIM // 2, 1) * sine


def turn_back(values, cosine, sine):
    return values * cosine - pltpu.roll(values, HEAD_DIM // 2, 1) * sine


VMEM_LIMIT = 56 << 20
SMEM_SPEC = pl.BlockSpec(memory_space=pltpu.SMEM)
VMEM_SPEC = pl.BlockSpec(memory_space=pltpu.VMEM)
ANY_SPEC = pl.BlockSpec(memory_space=pl.ANY)


def params():
    return pltpu.CompilerParams(vmem_limit_bytes=VMEM_LIMIT)


def cost(flops, bytes_accessed, transcendentals=0):
    return pl.CostEstimate(
        flops=flops, bytes_accessed=bytes_accessed, transcendentals=transcendentals
    )


def as_rows(first, second):
    lane = lax.broadcasted_iota(jnp.int32, (first.shape[0], 128), 1)
    both = jnp.where(lane == 0, first, jnp.where(lane == 1, second, 0.0))
    return both.T[:8]


def as_columns(rows):
    return rows.T


def project_kernel(tokens_ref, gain_ref, w_ref, in_ref, qkv_ref, squares_ref):
    own = w_ref.shape[1] // 3
    values = tokens_ref[...].astype(F32)
    normed = (values * norm_scale(values) * gain_ref[...]).astype(BF16)
    in_ref[...] = normed
    qkv = matmul(normed, w_ref[...])
    qkv_ref[...] = qkv
    query, key = qkv[:, :own], qkv[:, own : 2 * own]
    squares_ref[...] = as_rows(
        jnp.sum(query * query, axis=1, keepdims=True), jnp.sum(key * key, axis=1, keepdims=True)
    )


def project(tokens, gain, w_qkv):
    seq, width = tokens.shape
    columns = w_qkv.shape[1]
    tile = min(256, seq)
    return pl.pallas_call(
        project_kernel,
        grid=(seq // tile,),
        out_shape=[
            jax.ShapeDtypeStruct((seq, width), BF16),
            jax.ShapeDtypeStruct((seq, columns), F32),
            jax.ShapeDtypeStruct((8, seq), F32),
        ],
        in_specs=[
            pl.BlockSpec((tile, width), lambda i: (i, 0)),
            pl.BlockSpec((1, width), lambda i: (0, 0)),
            pl.BlockSpec((width, columns), lambda i: (0, 0)),
        ],
        out_specs=[
            pl.BlockSpec((tile, width), lambda i: (i, 0)),
            pl.BlockSpec((tile, columns), lambda i: (i, 0)),
            pl.BlockSpec((8, tile), lambda i: (0, i)),
        ],
        compiler_params=params(),
        cost_estimate=cost(2 * seq * width * columns, 8 * seq * width),
    )(tokens, gain, w_qkv)


def attend_kernel(
    length_ref, qkv_ref, squares_ref, gain_ref, cos_ref, sin_ref, q_ref, k_ref, v_ref, o_ref
):
    seq, own = q_ref.shape
    tile = min(256, seq)
    width = HEADS * HEAD_DIM
    length = length_ref[0]
    for start in range(0, seq, tile):
        rows = slice(start, start + tile)
        squares = as_columns(squares_ref[:, rows])
        cosine, sine = cos_ref[rows, :], sin_ref[rows, :]
        for part, out_ref in ((0, q_ref), (1, k_ref)):
            scale = lax.rsqrt(squares[:, part : part + 1] / width + EPSILON)
            for first in range(0, own, HEAD_DIM):
                columns = slice(first, first + HEAD_DIM)
                raw = qkv_ref[rows, part * own + first : part * own + first + HEAD_DIM]
                normed = raw * scale * gain_ref[part : part + 1, columns]
                out_ref[rows, columns] = turn(normed, cosine, sine).astype(BF16)
        v_ref[rows, :] = qkv_ref[rows, 2 * own : 3 * own].astype(BF16)
    for first in range(0, own, HEAD_DIM):
        columns = slice(first, first + HEAD_DIM)
        for start in range(0, seq, tile):
            rows, keys = slice(start, start + tile), slice(0, start + tile)
            scores = masked(matmul_nt(q_ref[rows, columns], k_ref[keys, columns]), start, length)
            expo = jnp.exp(scores - jnp.max(scores, axis=-1, keepdims=True))
            total = jnp.sum(expo, axis=-1, keepdims=True)
            probs = (expo / total).astype(BF16)
            o_ref[rows, columns] = matmul(probs, v_ref[keys, columns]).astype(BF16)


def attend_back_kernel(
    length_ref,
    qkv_ref,
    squares_ref,
    gain_ref,
    cos_ref,
    sin_ref,
    q_ref,
    k_ref,
    v_ref,
    do_ref,
    dq_ref,
    dk_ref,
    dv_ref,
    dots_ref,
    dgain_ref,
    k_total,
    v_total,
):
    seq, own = q_ref.shape
    tile = min(256, seq)
    width = HEADS * HEAD_DIM
    length = length_ref[0]
    for first in range(0, own, HEAD_DIM):
        columns = slice(first, first + HEAD_DIM)
        k_total[...] = jnp.zeros_like(k_total)
        v_total[...] = jnp.zeros_like(v_total)
        for start in range(0, seq, tile):
            rows, keys = slice(start, start + tile), slice(0, start + tile)
            q, k, v = q_ref[rows, columns], k_ref[keys, columns], v_ref[keys, columns]
            do = do_ref[rows, columns]
            scores = masked(matmul_nt(q, k), start, length)
            expo = jnp.exp(scores - jnp.max(scores, axis=-1, keepdims=True))
            probs = expo / jnp.sum(expo, axis=-1, keepdims=True)
            dprobs = matmul_nt(do, v)
            mean = jnp.sum(probs * dprobs, axis=-1, keepdims=True)
            dscores = (probs * (dprobs - mean)).astype(BF16)
            dq_ref[rows, columns] = matmul(dscores, k) * SCALE
            k_total[keys, :] += matmul_tn(dscores, q)
            v_total[keys, :] += matmul_tn(probs.astype(BF16), do)
        dk_ref[:, columns] = k_total[...] * SCALE
        dv_ref[:, columns] = v_total[...].astype(BF16)
    dgain_ref[...] = jnp.zeros_like(dgain_ref)
    for start in range(0, seq, tile):
        rows = slice(start, start + tile)
        squares = as_columns(squares_ref[:, rows])
        cosine, sine = cos_ref[rows, :], sin_ref[rows, :]
        both = []
        for part, out_ref in ((0, dq_ref), (1, dk_ref)):
            scale = lax.rsqrt(squares[:, part : part + 1] / width + EPSILON)
            dot = jnp.zeros((tile, 1), F32)
            for first in range(0, own, HEAD_DIM):
                columns = slice(first, first + HEAD_DIM)
                raw = qkv_ref[rows, part * own + first : part * own + first + HEAD_DIM]
                grad = turn_back(out_ref[rows, columns], cosine, sine)
                dgain_ref[part : part + 1, columns] += jnp.sum(
                    grad * raw * scale, axis=0, keepdims=True
                )
                grad = grad * gain_ref[part : part + 1, columns]
                dot += jnp.sum(grad * raw, axis=-1, keepdims=True)
                out_ref[rows, columns] = grad * scale
            both.append(dot)
        dots_ref[:, rows] = as_rows(*both)


def attend(length, qkv, squares, gains, cosine, sine):
    seq, own = qkv.shape[0], qkv.shape[1] // 3
    shape = jax.ShapeDtypeStruct((seq, own), BF16)
    return pl.pallas_call(
        attend_kernel,
        out_shape=[shape] * 4,
        in_specs=[SMEM_SPEC] + [VMEM_SPEC] * 5,
        out_specs=[VMEM_SPEC] * 4,
        compiler_params=params(),
        cost_estimate=cost(4 * seq * seq * own, 20 * seq * own, seq * seq),
    )(length, qkv, squares, gains, cosine, sine)


def attend_back(length, qkv, squares, gains, cosine, sine, q, k, v, do):
    seq, own = q.shape
    wide = jax.ShapeDtypeStruct((seq, own), F32)
    return pl.pallas_call(
        attend_back_kernel,
        out_shape=[
            wide,
            wide,
            jax.ShapeDtypeStruct((seq, own), BF16),
            jax.ShapeDtypeStruct((8, seq), F32),
            jax.ShapeDtypeStruct((2, own), F32),
        ],
        in_specs=[SMEM_SPEC] + [VMEM_SPEC] * 9,
        out_specs=[VMEM_SPEC] * 5,
        scratch_shapes=[pltpu.VMEM((seq, HEAD_DIM), F32)] * 2,
        compiler_params=params(),
        cost_estimate=cost(10 * seq * seq * own, 40 * seq * own, seq * seq),
    )(length, qkv, squares, gains, cosine, sine, q, k, v, do)


def finish_kernel(
    dq_ref, dk_ref, dv_ref, qkv_ref, squares_ref, dots_ref, w_ref, dqkv_ref, din_ref
):
    own = dq_ref.shape[1]
    width = HEADS * HEAD_DIM
    scale = lax.rsqrt(as_columns(squares_ref[...]) / width + EPSILON)
    factor = scale * scale * scale * as_columns(dots_ref[...]) / width
    for part, grad_ref in ((0, dq_ref), (1, dk_ref)):
        columns = slice(part * own, (part + 1) * own)
        grad = grad_ref[...] - qkv_ref[:, columns] * factor[:, part : part + 1]
        dqkv_ref[:, columns] = grad.astype(BF16)
    dqkv_ref[:, 2 * own :] = dv_ref[...]
    din_ref[...] = matmul_nt(dqkv_ref[...], w_ref[...]).astype(BF16)


def finish(dq, dk, dv, qkv, squares, dots, w_qkv):
    seq, own = dq.shape
    width = w_qkv.shape[0]
    tile = min(256, seq)
    narrow = pl.BlockSpec((tile, own), lambda i: (i, 0))
    wide = pl.BlockSpec((tile, 3 * own), lambda i: (i, 0))
    flat = pl.BlockSpec((8, tile), lambda i: (0, i))
    return pl.pallas_call(
        finish_kernel,
        grid=(seq // tile,),
        out_shape=[
            jax.ShapeDtypeStruct((seq, 3 * own), BF16),
            jax.ShapeDtypeStruct((seq, width), BF16),
        ],
        in_specs=[narrow, narrow, narrow, wide, flat, flat]
        + [pl.BlockSpec((width, 3 * own), lambda i: (0, 0))],
        out_specs=[wide, pl.BlockSpec((tile, width), lambda i: (i, 0))],
        compiler_params=params(),
        cost_estimate=cost(6 * seq * width * own, 4 * seq * width),
    )(dq, dk, dv, qkv, squares, dots, w_qkv)


def expert_kernel(n_pieces, piece_rows, n_blocks, n_slices, index_ref, column_ref, *refs):
    pieces, refs = refs[:n_pieces], refs[n_pieces:]
    hits_refs, router_ref, refs = refs[:n_blocks], refs[n_blocks], refs[n_blocks + 1 :]
    local_experts, _, wide = refs[0].shape
    gate_ref, up_ref, gate_rows_ref, up_rows_ref, refs = *refs[:4], refs[4:]
    back_refs = refs[: n_blocks * local_experts]
    x_ref, weight_ref, dots_ref, made_ref, grads_ref, sems, row_sems = refs[-7:]
    rows_out, dots_out, *outs = refs[-7 - n_blocks - 5 : -7 - n_blocks]
    grad_outs = refs[-7 - n_blocks : -7]
    step = pl.program_id(0)
    total, block = x_ref.shape[0], x_ref.shape[0] // n_blocks
    hidden_units = wide * n_slices
    slot = lax.rem(step, 2)
    lane = lax.broadcasted_iota(jnp.int32, (total, 128), 1)

    def row_copy(source, target, at, which):
        return pltpu.make_async_copy(
            source.at[pl.ds(at * block, block)],
            target.at[pl.ds(index_ref[at] * block, block)],
            row_sems.at[which, at],
        )

    def made_copy(which, at, of_step, from_slot):
        span = local_experts * wide
        return pltpu.make_async_copy(
            made_ref.at[from_slot, which, pl.ds(at * block, block)],
            outs[which].at[
                pl.ds(index_ref[at] * block, block),
                pl.ds(pl.multiple_of(column_ref[of_step] * span, span), span),
            ],
            sems.at[from_slot, which, at],
        )

    def all_made(of_step, from_slot):
        return [made_copy(w, at, of_step, from_slot) for w in range(3) for at in range(n_blocks)]

    def hit_of(expert):
        return jnp.concatenate([ref[:, expert : expert + 1] for ref in hits_refs], axis=0)

    @pl.when(step == 0)
    def _():
        start = 0
        for piece, rows in zip(pieces, piece_rows):
            x_ref[start : start + rows, :] = piece[...]
            start += rows
        for at in range(n_blocks):
            row_copy(x_ref, rows_out, at, 0).start()
        logits = matmul(x_ref[...], router_ref[...])
        expo = jnp.exp(logits - jnp.max(logits, axis=-1, keepdims=True))
        probs = expo / jnp.sum(expo, axis=-1, keepdims=True)
        which = lax.broadcasted_iota(jnp.int32, probs.shape, 1)
        weights = jnp.zeros((total, 128), F32)
        for expert in range(local_experts):
            mine = which == index_ref[n_blocks] * local_experts + expert
            weight = jnp.sum(jnp.where(mine, probs, 0.0), axis=-1, keepdims=True)
            weights = jnp.where(lane == expert, weight * hit_of(expert), weights)
        weight_ref[...] = weights
        dots_ref[...] = jnp.zeros_like(dots_ref)

    @pl.when((step >= 2) & (step < n_slices))
    def _():
        for copy in all_made(step - 2, slot):
            copy.wait()

    @pl.when(step < n_slices)
    def _():
        for expert in range(local_experts):
            gate = matmul(x_ref[...], gate_ref[expert])
            up = matmul(x_ref[...], up_ref[expert])
            back = jnp.concatenate(
                [ref[...] for ref in back_refs[n_blocks * expert : n_blocks * (expert + 1)]], axis=0
            ).astype(F32)
            weight = weight_ref[:, expert : expert + 1]
            sig = 0.5 + 0.5 * jnp.tanh(0.5 * gate)
            silu = gate * sig
            hidden = silu * up
            dot = jnp.sum(hidden * back, axis=-1, keepdims=True)
            dots_ref[...] += jnp.where(lane == expert, dot, 0.0)
            back = back * weight
            dgate = (back * up * (sig + silu * (1.0 - sig))).astype(BF16)
            dup = (back * silu).astype(BF16)
            columns = slice(expert * wide, (expert + 1) * wide)
            made_ref[slot, 0, :, columns] = (hidden * weight).astype(BF16)
            for which, value in ((0, dgate), (1, dup)):
                made_ref[slot, 1 + which, :, columns] = value
                first = (which * local_experts + expert) * hidden_units
                grads_ref[:, pl.ds(pl.multiple_of(first + step * wide, wide), wide)] = value
        for copy in all_made(step, slot):
            copy.start()

    @pl.when(step == n_slices - 1)
    def _():
        for expert in range(local_experts):
            dots_ref[...] = jnp.where(lane == expert, dots_ref[...] * hit_of(expert), dots_ref[...])
        for at in range(n_blocks):
            row_copy(dots_ref, dots_out, at, 1).start()

    @pl.when(step >= n_slices)
    def _():
        result = None
        for which, weights in enumerate((gate_rows_ref, up_rows_ref)):
            for expert in range(local_experts):
                first = (which * local_experts + expert) * hidden_units
                part = matmul_nt(grads_ref[:, first : first + hidden_units], weights[expert])
                result = part if result is None else result + part
        for at in range(n_blocks):
            grad_outs[at][...] = result[at * block : (at + 1) * block].astype(BF16)

    @pl.when(step == pl.num_programs(0) - 1)
    def _():
        for at in range(n_blocks):
            row_copy(x_ref, rows_out, at, 0).wait()
            row_copy(dots_ref, dots_out, at, 1).wait()
        for copy in all_made(n_slices - 1, (n_slices - 1) % 2) + all_made(
            n_slices - 2, n_slices % 2
        ):
            copy.wait()


def expert_call(index, column_place, pieces, hits, router, w_gate, w_up, backs, held, seq):
    local_experts, width, hidden_units = w_gate.shape
    n_slices, n_blocks = column_place.shape[0], index.shape[0] - 1
    wide = hidden_units // n_slices
    total = sum(piece.shape[0] for piece in pieces)
    block = total // n_blocks
    span = local_experts * hidden_units
    tile = 512
    assert n_slices >= 2

    def at_slice(step):
        return jnp.minimum(step, n_slices - 1)

    def at_tile(step):
        return jnp.maximum(step - n_slices, 0)

    weight_spec = pl.BlockSpec(
        (local_experts, width, wide), lambda i, index, column: (0, 0, at_slice(i))
    )
    rows_spec = pl.BlockSpec(
        (local_experts, tile, hidden_units), lambda i, index, column: (0, at_tile(i), 0)
    )

    def block_spec(at, columns, tiled):
        if tiled:
            return pl.BlockSpec(
                (block, columns), lambda i, index, column: (index[at], at_slice(i))
            )
        return pl.BlockSpec((block, columns), lambda i, index, column: (index[at], 0))

    in_specs = [pl.BlockSpec(piece.shape, lambda i, index, column: (0, 0)) for piece in pieces]
    in_specs += [block_spec(at, local_experts, False) for at in range(n_blocks)]
    in_specs += [pl.BlockSpec(router.shape, lambda i, index, column: (0, 0))]
    in_specs += [weight_spec, weight_spec, rows_spec, rows_spec]
    in_specs += [block_spec(at, wide, True) for _ in range(local_experts) for at in range(n_blocks)]
    operands = [*pieces, *[hits] * n_blocks, router, w_gate, w_up, w_gate, w_up]
    operands += [back for back in backs for _ in range(n_blocks)]
    aliases = {}
    if held is not None:
        aliases = {2 + len(operands) + i: i for i in range(5)}
        in_specs += [ANY_SPEC] * 5
        operands += held
    made = jax.ShapeDtypeStruct((seq, span), BF16)
    rows = [piece.shape[0] for piece in pieces]
    results = pl.pallas_call(
        lambda *refs: expert_kernel(len(pieces), rows, n_blocks, n_slices, *refs),
        out_shape=[
            jax.ShapeDtypeStruct((seq, width), BF16),
            jax.ShapeDtypeStruct((seq, 128), F32),
            made,
            made,
            made,
        ]
        + [jax.ShapeDtypeStruct((block, width), BF16)] * n_blocks,
        grid_spec=pltpu.PrefetchScalarGridSpec(
            num_scalar_prefetch=2,
            grid=(n_slices + width // tile,),
            in_specs=in_specs,
            out_specs=[ANY_SPEC] * 5
            + [pl.BlockSpec((block, tile), lambda i, index, column: (0, at_tile(i)))] * n_blocks,
            scratch_shapes=[
                pltpu.VMEM((total, width), BF16),
                pltpu.VMEM((total, 128), F32),
                pltpu.VMEM((total, 128), F32),
                pltpu.VMEM((2, 3, total, local_experts * wide), BF16),
                pltpu.VMEM((total, 2 * span), BF16),
                pltpu.SemaphoreType.DMA((2, 3, n_blocks)),
                pltpu.SemaphoreType.DMA((2, n_blocks)),
            ],
        ),
        input_output_aliases=aliases,
        compiler_params=params(),
        cost_estimate=cost(
            8 * total * width * span, 8 * width * span + 10 * total * span, total * span
        ),
    )(index, column_place, *operands)
    return results[:5], results[5:]


def back_rows_kernel(n_blocks, n_arrays, index_ref, column_ref, *refs):
    rows_refs, refs = refs[: n_blocks * n_arrays], refs[n_blocks * n_arrays :]
    weight_refs, outs, held = refs[:n_arrays], refs[n_arrays:-1], refs[-1]
    local_experts, _, hidden_units = weight_refs[0].shape
    n_slices = column_ref.shape[0]
    wide = hidden_units // n_slices
    block = rows_refs[0].shape[0]

    @pl.when(pl.program_id(0) == 0)
    def _():
        for at in range(n_blocks):
            for array in range(n_arrays):
                for expert in range(local_experts):
                    for part in range(n_slices):
                        first = (array * local_experts + expert) * hidden_units + part * wide
                        source = pl.multiple_of(
                            (column_ref[part] * local_experts + expert) * wide, 128
                        )
                        held[at * block : (at + 1) * block, first : first + wide] = rows_refs[
                            at * n_arrays + array
                        ][:, pl.ds(source, wide)]

    total = None
    for array in range(n_arrays):
        for expert in range(local_experts):
            first = (array * local_experts + expert) * hidden_units
            part = matmul_nt(held[:, first : first + hidden_units], weight_refs[array][expert])
            total = part if total is None else total + part
    for at in range(n_blocks):
        outs[at][...] = total[at * block : (at + 1) * block].astype(BF16)


def back_rows(index, column_place, arrays, weights, block, tile=256):
    n_blocks, n_arrays = index.shape[0], len(arrays)
    local_experts, width, hidden_units = weights[0].shape
    span = local_experts * hidden_units

    def row_spec(at):
        return pl.BlockSpec((block, span), lambda i, index, column: (index[at], 0))

    return pl.pallas_call(
        lambda *refs: back_rows_kernel(n_blocks, n_arrays, *refs),
        out_shape=[jax.ShapeDtypeStruct((block, width), BF16)] * n_blocks,
        grid_spec=pltpu.PrefetchScalarGridSpec(
            num_scalar_prefetch=2,
            grid=(width // tile,),
            in_specs=[row_spec(at) for at in range(n_blocks) for _ in range(n_arrays)]
            + [
                pl.BlockSpec(
                    (local_experts, tile, hidden_units), lambda i, index, column: (0, i, 0)
                )
            ]
            * n_arrays,
            out_specs=[pl.BlockSpec((block, tile), lambda i, index, column: (0, i))] * n_blocks,
            scratch_shapes=[pltpu.VMEM((n_blocks * block, n_arrays * span), BF16)],
        ),
        compiler_params=params(),
        cost_estimate=cost(
            2 * n_blocks * block * width * span * n_arrays, 2 * width * span * n_arrays
        ),
    )(index, column_place, *(list(arrays) * n_blocks), *weights)


def weight_grad_kernel(n_adds, left_ref, right_ref, *refs):
    total = matmul_tn(left_ref[...], right_ref[...])
    for ref in refs[:n_adds]:
        total += ref[...].astype(F32)
    out_ref = refs[-1]
    if len(out_ref.shape) == 2:
        out_ref[...] = total.astype(out_ref.dtype)
    else:
        wide = out_ref.shape[2]
        for expert in range(out_ref.shape[0]):
            out_ref[expert] = total[:, expert * wide : (expert + 1) * wide]


def weight_grad(left, right, first, columns, adds=(), experts=None, tile=512):
    seq, width = left.shape
    assert first % columns == 0
    if experts is None:
        out_shape = jax.ShapeDtypeStruct((width, columns), BF16)
        out_spec = pl.BlockSpec((tile, columns), lambda i: (i, 0))
    else:
        out_shape = jax.ShapeDtypeStruct((experts, width, columns // experts), F32)
        out_spec = pl.BlockSpec((experts, tile, columns // experts), lambda i: (0, i, 0))

    def add_spec(at):
        return pl.BlockSpec((tile, columns), lambda i: (i, at))

    return pl.pallas_call(
        lambda *refs: weight_grad_kernel(len(adds), *refs),
        out_shape=out_shape,
        grid=(width // tile,),
        in_specs=[
            pl.BlockSpec((seq, tile), lambda i: (0, i)),
            pl.BlockSpec((seq, columns), lambda i: (0, first // columns)),
        ]
        + [add_spec(at) for _, at in adds],
        out_specs=out_spec,
        compiler_params=params(),
        cost_estimate=cost(2 * seq * width * columns, 2 * width * (seq + columns)),
    )(left, right, *(value for value, _ in adds))


def body(
    tokens,
    seq_lengths,
    routes,
    w_query,
    w_key,
    w_value,
    w_out,
    gain_attn,
    gain_query,
    gain_key,
    gain_ffn,
    w_router,
    w_gate,
    w_up,
    w_down_t,
    cotangent,
):
    rows, width = tokens.shape
    local_experts, _, hidden_units = w_gate.shape
    groups, n_dp = lax.axis_size("expert"), lax.axis_size("dp")
    experts_all = local_experts * groups
    seq = groups * rows
    own = width // groups
    weight_rows = w_query.shape[0]
    chips = n_dp // CORES
    me, dp = lax.axis_index("expert"), lax.axis_index("dp")
    both_axes = ("dp", "expert")
    ring = Ring(groups)
    positions = jnp.arange(seq, dtype=jnp.int32)
    my_rows = me * rows + jnp.arange(rows, dtype=jnp.int32)
    seq_length = lax.dynamic_index_in_dim(seq_lengths, dp, 0, keepdims=True)
    used = (my_rows < seq_length[0]).astype(F32)[:, None]

    expert_ids = jnp.arange(experts_all, dtype=jnp.int32)
    chosen = jnp.any(routes[:, :, None] == expert_ids[None, None, :], axis=1)
    chosen_low = chosen.astype(BF16)

    hit_columns = rows * local_experts // weight_rows
    hits_out = chosen_low.reshape(rows, groups, local_experts).transpose(1, 0, 2)
    extra = jnp.concatenate(
        [jnp.stack([gain_attn, gain_query, gain_key, gain_ffn], axis=1), w_router], axis=1
    )
    extra_columns = extra.shape[1]
    pad = -(extra_columns + hit_columns) % 128
    send = jnp.concatenate(
        [w.reshape(weight_rows, groups, own).transpose(1, 0, 2) for w in (w_query, w_key, w_value)]
        + [
            jnp.broadcast_to(extra[None], (groups, weight_rows, extra_columns)),
            hits_out.reshape(groups, weight_rows, hit_columns),
            jnp.zeros((groups, weight_rows, pad), BF16),
        ],
        axis=2,
    )
    got = lax.all_to_all(send, "expert", split_axis=0, concat_axis=0, tiled=True)
    hits = got[:, :, 3 * own + extra_columns : 3 * own + extra_columns + hit_columns]
    hits = hits.reshape(seq, local_experts).astype(F32)
    projections = dp_gather(got.reshape(groups * weight_rows, -1), n_dp)
    w_qkv = projections[:, : 3 * own]
    small = projections[:, 3 * own : 3 * own + extra_columns]
    gains_full = small[:, :4].T.astype(F32)
    full_router = small[:, 4:]
    moves = [(e * n_dp + i, i * groups + e) for e in range(groups) for i in range(n_dp)]
    own_out = dp_gather(lax.ppermute(w_out, both_axes, moves), n_dp)

    resid_in = tokens.astype(F32)
    attn_gain, ffn_gain = gains_full[0:1], gains_full[3:4]
    tokens_all = place_blocks(ring, ring.gather(tokens), rows, width)
    [cot_own] = together((cotangent,), (tokens_all,))
    cot_all = lax.all_gather(cot_own, "expert", axis=0, tiled=True)
    attn_in, qkv, squares = project(tokens_all, attn_gain, w_qkv)
    own_out, squares = lax.optimization_barrier((own_out, squares))
    squares = expert_sum(squares, groups)
    gains_own = lax.dynamic_slice(gains_full, (1, me * own), (2, own))
    half = HEAD_DIM // 2
    frequency = ROPE_BASE ** (-(jnp.arange(half, dtype=F32) * 2.0) / HEAD_DIM)
    angles = positions.astype(F32)[:, None] * frequency[None, :]
    cosine, sine = jnp.cos(angles), jnp.sin(angles)
    cosine = jnp.concatenate([cosine, cosine], axis=1)
    sine = jnp.concatenate([-sine, sine], axis=1)
    q, k, v, attended = attend(seq_length, qkv, squares, gains_own, cosine, sine)

    def block_of(value, o):
        return lax.dynamic_slice(value, (ring.natural[o] * rows, 0), (rows, value.shape[1]))

    far = groups // 2
    out_far = matmul(block_of(attended, far), own_out).astype(BF16)
    out_part = matmul(attended, own_out).astype(BF16)
    backs = []

    def make_back(expert):
        backs.append(matmul(cot_all, w_down_t[expert]).astype(BF16))
        return (backs[-1],)

    hooks = {
        2: lambda: make_back(0),
        3: lambda: [make_back(expert)[0] for expert in range(1, local_experts)],
    }
    resid_mid = resid_in + ring.scatter(
        lambda o: out_far if o == far else block_of(out_part, o), hooks
    )
    mid_scale = norm_scale(resid_mid)
    ffn_in = (resid_mid * mid_scale * ffn_gain).astype(BF16)

    distances = (
        [2 * y + 1 for y in range(chips)] + [2 * y for y in range(1, chips)] + [0]
    )
    place_of = np.zeros((n_dp,), np.int32)
    place_of[np.array(distances)] = np.arange(n_dp)
    column_place = jnp.asarray(place_of)[jnp.arange(n_dp, dtype=jnp.int32) ^ dp]
    per_call = 4
    calls = groups // per_call
    held, drow_terms = [], {}

    def expert_pieces(pieces, at):
        given = pieces[at:] if at + per_call == groups else pieces[at : at + per_call]
        order = [o for o, _, _ in given[:per_call]]
        result, blocks = expert_call(
            jnp.stack([ring.natural[o] for o in order] + [me]),
            column_place,
            [piece for _, _, piece in given],
            hits,
            full_router,
            w_gate,
            w_up,
            backs,
            held[-1] if held else None,
            seq,
        )
        held.append(result)
        drow_terms.update(zip(order, blocks))
        return result

    hooks = {}
    for call in range(calls - 1):
        step = (call + 1) * per_call // 2 + 1
        hooks[step] = lambda pieces, at=call * per_call: expert_pieces(pieces, at)
    pieces = ring.gather(ffn_in, hooks)
    expert_pieces(pieces, groups - per_call)
    ffn_all, pair_dots, scaled_hidden, dgates, dups = held[-1]
    pairs = []

    def make_pairs():
        out = pair_dots[:, :local_experts].reshape(groups, rows, local_experts).transpose(0, 2, 1)
        pairs.append(lax.all_to_all(out, "expert", split_axis=0, concat_axis=0, tiled=True))
        return tuple(pairs)

    slice_columns = local_experts * hidden_units // n_dp
    swap = [(i, i ^ 1) for i in range(n_dp)]
    sides = [(cot_all, scaled_hidden), (ffn_all, dgates), (ffn_all, dups)]
    other, adds = {}, {}

    def make_sent(which):
        sent = weight_grad(*sides[which], 0, chips * slice_columns)
        other[which] = lax.ppermute(sent, "dp", swap)
        adds[which] = [(other[which], 0)]
        return (sent,)

    parts = {}

    def make_part(which):
        parts[which] = [
            weight_grad(
                *sides[which],
                (chips + y - 1) * slice_columns,
                slice_columns,
                [(other[which], y)],
            )
            for y in range(1, chips)
        ]
        return tuple(parts[which])

    def send_part(which, after):
        sent = together(tuple(parts[which]), (after,))
        got = [
            lax.ppermute(part, "dp", [(i, i ^ (2 * y)) for i in range(n_dp)])
            for y, part in zip(range(1, chips), sent)
        ]
        adds[which] += [(part, 0) for part in got]
        return tuple(got)

    hooks = {
        far - 2: lambda: make_sent(0),
        far - 1: lambda: (*make_sent(1), *make_part(0)),
        far: lambda: (*make_pairs(), *make_sent(2), *make_part(1)),
    }
    drow = ring.scatter(lambda o: drow_terms[o], hooks)

    grad_rows = cotangent.astype(F32)
    dprobs = pairs[0].reshape(experts_all, rows).T
    probs = jax.nn.softmax(matmul(ffn_in, full_router), axis=-1)
    dlogits = probs * (dprobs - jnp.sum(probs * dprobs, axis=1, keepdims=True))
    dlogits = dlogits.astype(BF16)
    grad_router = matmul_tn(ffn_in, dlogits)
    dffn = drow + matmul_nt(dlogits, full_router)
    grad_gain_ffn = jnp.sum(dffn * resid_mid * mid_scale, axis=0, keepdims=True)
    scaled = dffn * ffn_gain
    mid_grads = (
        grad_rows
        + mid_scale * scaled
        - resid_mid * mid_scale**3 * jnp.mean(scaled * resid_mid, axis=1, keepdims=True)
    )
    mid_low = mid_grads.astype(BF16)

    def make_moe(pieces):
        return back_rows(
            jnp.zeros((1,), jnp.int32), column_place, (scaled_hidden,), (w_down_t,), seq
        )

    moe_made = []
    first = send_part(0, mid_low)
    mid_pieces = ring.gather(
        mid_low,
        {
            1: lambda pieces: make_part(2),
            2: lambda pieces: moe_made.extend(make_moe(pieces)) or moe_made,
        },
    )
    mid_all = place_blocks(ring, mid_pieces, rows, width)
    [mid_all] = together((mid_all,), first)
    second = send_part(1, mid_all)
    grad_heads = matmul_nt(mid_all, own_out).astype(BF16)

    moe_part, grad_heads = lax.optimization_barrier((moe_made[0], grad_heads))
    moe_rows = lax.psum_scatter(moe_part, "expert", scatter_dimension=0, tiled=True).astype(F32)
    output = (resid_mid + moe_rows).astype(BF16)

    dq, dk, dv, dots, dgains = attend_back(
        seq_length, qkv, squares, gains_own, cosine, sine, q, k, v, grad_heads
    )
    dots = expert_sum(dots, groups)
    dqkv, din_part = finish(dq, dk, dv, qkv, squares, dots, w_qkv)
    third = []

    def make_own(which, after):
        left, right = sides[which]
        [left] = together((left,), after)
        return weight_grad(
            left,
            right,
            (n_dp - 1) * slice_columns,
            slice_columns,
            adds[which],
            local_experts,
        )

    def middle():
        third.extend(send_part(2, second[0]))
        return second

    spread_gains = lax.dynamic_update_slice(jnp.zeros((2, width), F32), dgains, (0, me * own))
    lane = lax.broadcasted_iota(jnp.int32, (1, width), 1)
    sums = jnp.where(
        lane == 0,
        jnp.sum(used * resid_mid * resid_mid),
        jnp.where(lane == 1, jnp.sum(used * moe_rows * moe_rows), 0.0),
    )
    rest = jnp.concatenate([spread_gains, grad_gain_ffn, sums, grad_router.T], axis=0)
    hooks = {far - 2: middle, far: lambda: (rest,)}
    dattn = ring.scatter(lambda o: block_of(din_part, o), hooks)
    [rest] = together((rest,), (dattn,))
    own_grads = []
    for at in range(groups.bit_length() - 1):
        rest = rest + lax.ppermute(rest, "expert", [(i, i ^ (1 << at)) for i in range(groups)])
        if at < 3:
            own_grads.append(make_own(at, (rest,)))
            [rest] = together((rest,), ())
    rest = dp_sum(rest, n_dp)
    grad_down, grad_gate_w, grad_up_w = own_grads
    in_scale = norm_scale(resid_in)
    scaled = dattn * attn_gain
    input_grad = (
        mid_grads
        + in_scale * scaled
        - resid_in * in_scale**3 * jnp.mean(scaled * resid_in, axis=1, keepdims=True)
    ).astype(BF16)

    block = width // n_dp

    def projection_term(rel):
        left = lax.dynamic_slice(attn_in, (0, (dp ^ rel) * block), (seq, block))
        return matmul_tn(left, dqkv)

    reduced = dp_reduce(projection_term, n_dp).astype(BF16)
    [reduced] = together((reduced,), (dattn,))
    reduced = lax.all_to_all(
        reduced.reshape(groups, weight_rows, 3 * own),
        "expert",
        split_axis=0,
        concat_axis=0,
        tiled=True,
    ).astype(F32)
    grads = [
        reduced[:, :, i * own : (i + 1) * own].transpose(1, 0, 2).reshape(weight_rows, width)
        for i in range(3)
    ]
    grad_gain_attn = (
        sum(jnp.sum(g * w.astype(F32), axis=1) for g, w in zip(grads, (w_query, w_key, w_value)))
        / gain_attn.astype(F32)
    )
    out_grads = matmul_tn(attended, mid_all)

    def out_term(rel):
        return lax.dynamic_slice(out_grads, ((dp ^ rel) * weight_rows, 0), (weight_rows, width))

    grad_out = dp_reduce(out_term, n_dp).astype(BF16)
    [grad_out] = together((grad_out,), (dattn,))
    grad_out = lax.ppermute(grad_out, both_axes, [(b, a) for a, b in moves]).astype(F32)

    mine = lax.dynamic_slice(
        rest, (0, (dp * groups + me) * weight_rows), (rest.shape[0], weight_rows)
    )
    counted = jnp.sum(seq_lengths).astype(F32) * width
    rms_resid = jnp.sqrt(rest[3, 0] / counted)
    rms_moe = jnp.sqrt(rest[3, 1] / counted)
    return (
        output,
        input_grad,
        grads[0],
        grads[1],
        grads[2],
        grad_out,
        grad_gain_attn,
        mine[0],
        mine[1],
        mine[2],
        mine[4:].T,
        grad_gate_w,
        grad_up_w,
        grad_down,
        rms_resid,
        rms_moe,
    )


def solution(mesh):
    both = ("dp", "expert")
    row, vector, expert = P(both, None), P(both), P("expert", None, None)
    placed = (
        row,
        P(),
        row,
        row,
        row,
        row,
        row,
        vector,
        vector,
        vector,
        vector,
        row,
        expert,
        expert,
        expert,
        row,
    )
    grads = P("expert", None, "dp")
    return jax.shard_map(
        body,
        mesh=mesh,
        in_specs=placed,
        out_specs=(row,) * 6 + (vector,) * 4 + (row, grads, grads, grads, P(), P()),
        check_vma=False,
    )
```

```python
import jax
import jax.numpy as jnp
import numpy as np
from jax import lax
from jax.experimental import pallas as pl
from jax.experimental.pallas import tpu as pltpu
from jax.sharding import PartitionSpec as P

HEADS = 16
HEAD_DIM = 128
TOP = 8
EPSILON = 1e-05
ROPE_BASE = 10000.0
SCALE = HEAD_DIM ** (-0.5)
NEG = -1e30
Z_CHIPS = 4
CORES = 2
F32 = jnp.float32
BF16 = jnp.bfloat16


def ring_tables(groups):
    x_chips = groups // Z_CHIPS
    walk = []
    for x in range(x_chips):
        column = range(1, Z_CHIPS) if x % 2 == 0 else range(Z_CHIPS - 1, 0, -1)
        walk += [z * x_chips + x for z in column]
    walk += [x for x in range(x_chips - 1, -1, -1)]
    place = np.zeros((groups,), np.int32)
    for at, owner in enumerate(walk):
        place[owner] = at
    return np.array(walk, np.int32), place


class Ring:
    def __init__(self, groups):
        self.size = groups
        self.walk, self.place = ring_tables(groups)
        size = groups
        self.ahead = [(int(self.walk[i]), int(self.walk[(i + 1) % size])) for i in range(size)]
        self.back = [(b, a) for a, b in self.ahead]
        mine = jnp.asarray(self.place)[lax.axis_index("expert")]
        self.natural = jnp.asarray(self.walk)[(mine + jnp.arange(size, dtype=jnp.int32)) % size]

    def up(self, value):
        return lax.ppermute(value, "expert", self.ahead)

    def down(self, value):
        return lax.ppermute(value, "expert", self.back)

    def gather(self, block, hooks=None):
        hooks = hooks or {}
        half = self.size // 2
        rows = block.shape[0]
        pieces = [(0, 0, block)]
        up, down = block, block
        for step in range(1, half):
            made = hooks[step](pieces) if step in hooks else ()
            up, down = together((self.up(up), self.down(down)), made)
            pieces += [(self.size - step, 0, up), (step, 0, down)]
        made = hooks[half](pieces) if half in hooks else ()
        up, down = together((self.up(up[: rows // 2]), self.down(down[rows // 2 :])), made)
        pieces += [(half, 0, up), (half, rows // 2, down)]
        return pieces

    def scatter(self, term, hooks=None):
        hooks = hooks or {}
        half = self.size // 2
        far = term(half)
        rows = far.shape[0]
        up = self.up(far[: rows // 2])
        down = self.down(far[rows // 2 :])

        def add(left, right):
            return (left.astype(F32) + right.astype(F32)).astype(BF16)

        for step in range(half - 1, 0, -1):
            made = hooks[half - step]() if half - step in hooks else ()
            up, down = together((up, down), made)
            ahead, behind = term(step), term(self.size - step)
            if step == half - 1:
                ahead = jnp.concatenate([add(up, ahead[: rows // 2]), ahead[rows // 2 :]], axis=0)
                behind = jnp.concatenate(
                    [behind[: rows // 2], add(down, behind[rows // 2 :])], axis=0
                )
            else:
                ahead, behind = add(up, ahead), add(down, behind)
            up, down = self.up(ahead), self.down(behind)
        made = hooks[half]() if half in hooks else ()
        up, down = together((up, down), made)
        return up.astype(F32) + down.astype(F32) + term(0).astype(F32)


def together(values, made):
    if not made:
        return values
    return lax.optimization_barrier((*values, *made))[: len(values)]


def place_blocks(ring, pieces, rows, width, dtype=BF16):
    buffer = jnp.zeros((ring.size * rows, width), dtype)
    for o, start, piece in pieces:
        buffer = lax.dynamic_update_slice(
            buffer, piece.astype(dtype), (ring.natural[o] * rows + start, 0)
        )
    return buffer


def expert_sum(value, groups):
    step = 1
    while step < groups:
        value = value + lax.ppermute(value, "expert", [(i, i ^ step) for i in range(groups)])
        step *= 2
    return value


def dp_sum(value, n_dp):
    step = 1
    while step < n_dp:
        value = value + lax.ppermute(value, "dp", [(i, i ^ step) for i in range(n_dp)])
        step *= 2
    return value


class DpGather:
    def __init__(self, chunk, n_dp):
        self.chunk, self.n_dp = chunk, n_dp

    def over_y(self):
        n_dp = self.n_dp
        self.held = [(0, self.chunk)] + [
            (2 * y, lax.ppermute(self.chunk, "dp", [(i, i ^ (2 * y)) for i in range(n_dp)]))
            for y in range(1, n_dp // CORES)
        ]
        return tuple(part for _, part in self.held[1:])

    def over_cores(self):
        swap = [(i, i ^ 1) for i in range(self.n_dp)]
        new = [(rel ^ 1, lax.ppermute(part, "dp", swap)) for rel, part in self.held]
        self.held += new
        return tuple(part for _, part in new)

    def rows(self):
        rows, width = self.chunk.shape
        me = lax.axis_index("dp")
        buffer = jnp.zeros((self.n_dp * rows, width), self.chunk.dtype)
        for rel, part in self.held:
            buffer = lax.dynamic_update_slice(buffer, part, ((me ^ rel) * rows, 0))
        return buffer


def dp_reduce(term, n_dp):
    swap = [(i, i ^ 1) for i in range(n_dp)]
    chips = n_dp // CORES
    other = [lax.ppermute(term(2 * y + 1).astype(BF16), "dp", swap) for y in range(chips)]
    total = None
    for y in range(1, chips):
        part = (term(2 * y) + other[y].astype(F32)).astype(BF16)
        part = lax.ppermute(part, "dp", [(i, i ^ (2 * y)) for i in range(n_dp)]).astype(F32)
        total = part if total is None else total + part
    own = term(0) + other[0].astype(F32)
    return own if total is None else own + total


def norm_scale(values):
    return lax.rsqrt(jnp.mean(values * values, axis=-1, keepdims=True) + EPSILON)


def matmul(left, right):
    return jnp.dot(left, right, preferred_element_type=F32)


def matmul_nt(left, right):
    return lax.dot_general(left, right, (((1,), (1,)), ((), ())), preferred_element_type=F32)


def matmul_tn(left, right):
    return lax.dot_general(left, right, (((0,), (0,)), ((), ())), preferred_element_type=F32)


def masked(scores, first_row, length):
    rows, columns = scores.shape
    row = first_row + lax.broadcasted_iota(jnp.int32, (rows, columns), 0)
    column = lax.broadcasted_iota(jnp.int32, (rows, columns), 1)
    return jnp.where((column <= row) & (column < length), scores * SCALE, NEG)


def turn(values, cosine, sine):
    return values * cosine + pltpu.roll(values, HEAD_DIM // 2, 1) * sine


def turn_back(values, cosine, sine):
    return values * cosine - pltpu.roll(values, HEAD_DIM // 2, 1) * sine


VMEM_LIMIT = 56 << 20
SMEM_SPEC = pl.BlockSpec(memory_space=pltpu.SMEM)
VMEM_SPEC = pl.BlockSpec(memory_space=pltpu.VMEM)
ANY_SPEC = pl.BlockSpec(memory_space=pl.ANY)


def params():
    return pltpu.CompilerParams(vmem_limit_bytes=VMEM_LIMIT)


def cost(flops, bytes_accessed, transcendentals=0):
    return pl.CostEstimate(
        flops=flops, bytes_accessed=bytes_accessed, transcendentals=transcendentals
    )


def as_rows(first, second):
    lane = lax.broadcasted_iota(jnp.int32, (first.shape[0], 128), 1)
    both = jnp.where(lane == 0, first, jnp.where(lane == 1, second, 0.0))
    return both.T[:8]


def as_columns(rows):
    return rows.T


def project_kernel(tokens_ref, gain_ref, w_ref, in_ref, qkv_ref, squares_ref):
    own = qkv_ref.shape[1] // 3
    values = tokens_ref[...].astype(F32)
    normed = (values * norm_scale(values) * gain_ref[...]).astype(BF16)
    in_ref[...] = normed
    qkv = matmul(normed, w_ref[...])
    qkv_ref[...] = qkv
    query, key = qkv[:, :own], qkv[:, own : 2 * own]
    squares_ref[...] = as_rows(
        jnp.sum(query * query, axis=1, keepdims=True), jnp.sum(key * key, axis=1, keepdims=True)
    )


def project(tokens, gain, w_qkv, columns):
    seq, width = tokens.shape
    tile = min(256, seq)
    return pl.pallas_call(
        project_kernel,
        grid=(seq // tile,),
        out_shape=[
            jax.ShapeDtypeStruct((seq, width), BF16),
            jax.ShapeDtypeStruct((seq, columns), F32),
            jax.ShapeDtypeStruct((8, seq), F32),
        ],
        in_specs=[
            pl.BlockSpec((tile, width), lambda i: (i, 0)),
            pl.BlockSpec((1, width), lambda i: (0, 0)),
            pl.BlockSpec((width, columns), lambda i: (0, 0)),
        ],
        out_specs=[
            pl.BlockSpec((tile, width), lambda i: (i, 0)),
            pl.BlockSpec((tile, columns), lambda i: (i, 0)),
            pl.BlockSpec((8, tile), lambda i: (0, i)),
        ],
        compiler_params=params(),
        cost_estimate=cost(2 * seq * width * columns, 8 * seq * width),
    )(tokens, gain, w_qkv)


def attend_kernel(
    length_ref, qkv_ref, squares_ref, gain_ref, cos_ref, sin_ref, q_ref, k_ref, v_ref, o_ref
):
    seq, own = q_ref.shape
    tile = min(256, seq)
    width = HEADS * HEAD_DIM
    length = length_ref[0]
    for start in range(0, seq, tile):
        rows = slice(start, start + tile)
        squares = as_columns(squares_ref[:, rows])
        cosine, sine = cos_ref[rows, :], sin_ref[rows, :]
        for part, out_ref in ((0, q_ref), (1, k_ref)):
            scale = lax.rsqrt(squares[:, part : part + 1] / width + EPSILON)
            for first in range(0, own, HEAD_DIM):
                columns = slice(first, first + HEAD_DIM)
                raw = qkv_ref[rows, part * own + first : part * own + first + HEAD_DIM]
                normed = raw * scale * gain_ref[part : part + 1, columns]
                out_ref[rows, columns] = turn(normed, cosine, sine).astype(BF16)
        v_ref[rows, :] = qkv_ref[rows, 2 * own : 3 * own].astype(BF16)
    for first in range(0, own, HEAD_DIM):
        columns = slice(first, first + HEAD_DIM)
        for start in range(0, seq, tile):
            rows, keys = slice(start, start + tile), slice(0, start + tile)
            scores = masked(matmul_nt(q_ref[rows, columns], k_ref[keys, columns]), start, length)
            expo = jnp.exp(scores - jnp.max(scores, axis=-1, keepdims=True))
            total = jnp.sum(expo, axis=-1, keepdims=True)
            probs = (expo / total).astype(BF16)
            o_ref[rows, columns] = matmul(probs, v_ref[keys, columns]).astype(BF16)


def attend_back_kernel(
    length_ref,
    qkv_ref,
    squares_ref,
    gain_ref,
    cos_ref,
    sin_ref,
    q_ref,
    k_ref,
    v_ref,
    do_ref,
    dq_ref,
    dk_ref,
    dv_ref,
    dots_ref,
    dgain_ref,
    k_total,
    v_total,
):
    seq, own = q_ref.shape
    tile = min(256, seq)
    width = HEADS * HEAD_DIM
    length = length_ref[0]
    for first in range(0, own, HEAD_DIM):
        columns = slice(first, first + HEAD_DIM)
        k_total[...] = jnp.zeros_like(k_total)
        v_total[...] = jnp.zeros_like(v_total)
        for start in range(0, seq, tile):
            rows, keys = slice(start, start + tile), slice(0, start + tile)
            q, k, v = q_ref[rows, columns], k_ref[keys, columns], v_ref[keys, columns]
            do = do_ref[rows, columns]
            scores = masked(matmul_nt(q, k), start, length)
            expo = jnp.exp(scores - jnp.max(scores, axis=-1, keepdims=True))
            probs = expo / jnp.sum(expo, axis=-1, keepdims=True)
            dprobs = matmul_nt(do, v)
            mean = jnp.sum(probs * dprobs, axis=-1, keepdims=True)
            dscores = (probs * (dprobs - mean)).astype(BF16)
            dq_ref[rows, columns] = matmul(dscores, k) * SCALE
            k_total[keys, :] += matmul_tn(dscores, q)
            v_total[keys, :] += matmul_tn(probs.astype(BF16), do)
        dk_ref[:, columns] = k_total[...] * SCALE
        dv_ref[:, columns] = v_total[...].astype(BF16)
    dgain_ref[...] = jnp.zeros_like(dgain_ref)
    for start in range(0, seq, tile):
        rows = slice(start, start + tile)
        squares = as_columns(squares_ref[:, rows])
        cosine, sine = cos_ref[rows, :], sin_ref[rows, :]
        both = []
        for part, out_ref in ((0, dq_ref), (1, dk_ref)):
            scale = lax.rsqrt(squares[:, part : part + 1] / width + EPSILON)
            dot = jnp.zeros((tile, 1), F32)
            for first in range(0, own, HEAD_DIM):
                columns = slice(first, first + HEAD_DIM)
                raw = qkv_ref[rows, part * own + first : part * own + first + HEAD_DIM]
                grad = turn_back(out_ref[rows, columns], cosine, sine)
                dgain_ref[part : part + 1, columns] += jnp.sum(
                    grad * raw * scale, axis=0, keepdims=True
                )
                grad = grad * gain_ref[part : part + 1, columns]
                dot += jnp.sum(grad * raw, axis=-1, keepdims=True)
                out_ref[rows, columns] = grad * scale
            both.append(dot)
        dots_ref[:, rows] = as_rows(*both)


def attend(length, qkv, squares, gains, cosine, sine):
    seq, own = qkv.shape[0], qkv.shape[1] // 3
    shape = jax.ShapeDtypeStruct((seq, own), BF16)
    return pl.pallas_call(
        attend_kernel,
        out_shape=[shape] * 4,
        in_specs=[SMEM_SPEC] + [VMEM_SPEC] * 5,
        out_specs=[VMEM_SPEC] * 4,
        compiler_params=params(),
        cost_estimate=cost(4 * seq * seq * own, 20 * seq * own, seq * seq),
    )(length, qkv, squares, gains, cosine, sine)


def attend_back(length, qkv, squares, gains, cosine, sine, q, k, v, do):
    seq, own = q.shape
    wide = jax.ShapeDtypeStruct((seq, own), F32)
    return pl.pallas_call(
        attend_back_kernel,
        out_shape=[
            wide,
            wide,
            jax.ShapeDtypeStruct((seq, own), BF16),
            jax.ShapeDtypeStruct((8, seq), F32),
            jax.ShapeDtypeStruct((2, own), F32),
        ],
        in_specs=[SMEM_SPEC] + [VMEM_SPEC] * 9,
        out_specs=[VMEM_SPEC] * 5,
        scratch_shapes=[pltpu.VMEM((seq, HEAD_DIM), F32)] * 2,
        compiler_params=params(),
        cost_estimate=cost(10 * seq * seq * own, 40 * seq * own, seq * seq),
    )(length, qkv, squares, gains, cosine, sine, q, k, v, do)


def finish_kernel(
    dq_ref, dk_ref, dv_ref, qkv_ref, squares_ref, dots_ref, w_ref, dqkv_ref, din_ref
):
    own = dq_ref.shape[1]
    width = HEADS * HEAD_DIM
    scale = lax.rsqrt(as_columns(squares_ref[...]) / width + EPSILON)
    factor = scale * scale * scale * as_columns(dots_ref[...]) / width
    for part, grad_ref in ((0, dq_ref), (1, dk_ref)):
        columns = slice(part * own, (part + 1) * own)
        grad = grad_ref[...] - qkv_ref[:, columns] * factor[:, part : part + 1]
        dqkv_ref[:, columns] = grad.astype(BF16)
    dqkv_ref[:, 2 * own :] = dv_ref[...]
    din_ref[...] = matmul_nt(dqkv_ref[...], w_ref[...]).astype(BF16)


def finish(dq, dk, dv, qkv, squares, dots, w_qkv):
    seq, own = dq.shape
    width = w_qkv.shape[0]
    tile = min(256, seq)
    narrow = pl.BlockSpec((tile, own), lambda i: (i, 0))
    wide = pl.BlockSpec((tile, 3 * own), lambda i: (i, 0))
    flat = pl.BlockSpec((8, tile), lambda i: (0, i))
    return pl.pallas_call(
        finish_kernel,
        grid=(seq // tile,),
        out_shape=[
            jax.ShapeDtypeStruct((seq, 3 * own), BF16),
            jax.ShapeDtypeStruct((seq, width), BF16),
        ],
        in_specs=[narrow, narrow, narrow, wide, flat, flat]
        + [pl.BlockSpec((width, 3 * own), lambda i: (0, 0))],
        out_specs=[wide, pl.BlockSpec((tile, width), lambda i: (i, 0))],
        compiler_params=params(),
        cost_estimate=cost(6 * seq * width * own, 4 * seq * width),
    )(dq, dk, dv, qkv, squares, dots, w_qkv)


def expert_kernel(n_pieces, piece_rows, n_blocks, n_slices, index_ref, column_ref, *refs):
    pieces, refs = refs[:n_pieces], refs[n_pieces:]
    hits_refs, router_ref, refs = refs[:n_blocks], refs[n_blocks], refs[n_blocks + 1 :]
    local_experts, _, wide = refs[0].shape
    gate_ref, up_ref, gate_rows_ref, up_rows_ref, refs = *refs[:4], refs[4:]
    back_refs = refs[: n_blocks * local_experts]
    x_ref, weight_ref, dots_ref, made_ref, grads_ref, sems, row_sems = refs[-7:]
    rows_out, dots_out, *outs = refs[-7 - n_blocks - 5 : -7 - n_blocks]
    grad_outs = refs[-7 - n_blocks : -7]
    step = pl.program_id(0)
    total, block = x_ref.shape[0], x_ref.shape[0] // n_blocks
    hidden_units = wide * n_slices
    slot = lax.rem(step, 2)
    lane = lax.broadcasted_iota(jnp.int32, (total, 128), 1)

    def row_copy(source, target, at, which):
        return pltpu.make_async_copy(
            source.at[pl.ds(at * block, block)],
            target.at[pl.ds(index_ref[at] * block, block)],
            row_sems.at[which, at],
        )

    def made_copy(which, at, of_step, from_slot):
        span = local_experts * wide
        return pltpu.make_async_copy(
            made_ref.at[from_slot, which, pl.ds(at * block, block)],
            outs[which].at[
                pl.ds(index_ref[at] * block, block),
                pl.ds(pl.multiple_of(column_ref[of_step] * span, span), span),
            ],
            sems.at[from_slot, which, at],
        )

    def all_made(of_step, from_slot):
        return [made_copy(w, at, of_step, from_slot) for w in range(3) for at in range(n_blocks)]

    def hit_of(expert):
        return jnp.concatenate([ref[:, expert : expert + 1] for ref in hits_refs], axis=0)

    @pl.when(step == 0)
    def _():
        start = 0
        for piece, rows in zip(pieces, piece_rows):
            x_ref[start : start + rows, :] = piece[...]
            start += rows
        for at in range(n_blocks):
            row_copy(x_ref, rows_out, at, 0).start()
        logits = matmul(x_ref[...], router_ref[...])
        expo = jnp.exp(logits - jnp.max(logits, axis=-1, keepdims=True))
        probs = expo / jnp.sum(expo, axis=-1, keepdims=True)
        which = lax.broadcasted_iota(jnp.int32, probs.shape, 1)
        weights = jnp.zeros((total, 128), F32)
        for expert in range(local_experts):
            mine = which == index_ref[n_blocks] * local_experts + expert
            weight = jnp.sum(jnp.where(mine, probs, 0.0), axis=-1, keepdims=True)
            weights = jnp.where(lane == expert, weight * hit_of(expert), weights)
        weight_ref[...] = weights
        dots_ref[...] = jnp.zeros_like(dots_ref)

    @pl.when((step >= 2) & (step < n_slices))
    def _():
        for copy in all_made(step - 2, slot):
            copy.wait()

    @pl.when(step < n_slices)
    def _():
        for expert in range(local_experts):
            gate = matmul(x_ref[...], gate_ref[expert])
            up = matmul(x_ref[...], up_ref[expert])
            back = jnp.concatenate(
                [ref[...] for ref in back_refs[n_blocks * expert : n_blocks * (expert + 1)]], axis=0
            ).astype(F32)
            weight = weight_ref[:, expert : expert + 1]
            sig = 0.5 + 0.5 * jnp.tanh(0.5 * gate)
            silu = gate * sig
            hidden = silu * up
            dot = jnp.sum(hidden * back, axis=-1, keepdims=True)
            dots_ref[...] += jnp.where(lane == expert, dot, 0.0)
            back = back * weight
            dgate = (back * up * (sig + silu * (1.0 - sig))).astype(BF16)
            dup = (back * silu).astype(BF16)
            columns = slice(expert * wide, (expert + 1) * wide)
            made_ref[slot, 0, :, columns] = (hidden * weight).astype(BF16)
            for which, value in ((0, dgate), (1, dup)):
                made_ref[slot, 1 + which, :, columns] = value
                first = (which * local_experts + expert) * hidden_units
                grads_ref[:, pl.ds(pl.multiple_of(first + step * wide, wide), wide)] = value
        for copy in all_made(step, slot):
            copy.start()

    @pl.when(step == n_slices - 1)
    def _():
        for expert in range(local_experts):
            dots_ref[...] = jnp.where(lane == expert, dots_ref[...] * hit_of(expert), dots_ref[...])
        for at in range(n_blocks):
            row_copy(dots_ref, dots_out, at, 1).start()

    @pl.when(step >= n_slices)
    def _():
        result = None
        for which, weights in enumerate((gate_rows_ref, up_rows_ref)):
            for expert in range(local_experts):
                first = (which * local_experts + expert) * hidden_units
                part = matmul_nt(grads_ref[:, first : first + hidden_units], weights[expert])
                result = part if result is None else result + part
        for at in range(n_blocks):
            grad_outs[at][...] = result[at * block : (at + 1) * block].astype(BF16)

    @pl.when(step == pl.num_programs(0) - 1)
    def _():
        for at in range(n_blocks):
            row_copy(x_ref, rows_out, at, 0).wait()
            row_copy(dots_ref, dots_out, at, 1).wait()
        for copy in all_made(n_slices - 1, (n_slices - 1) % 2) + all_made(
            n_slices - 2, n_slices % 2
        ):
            copy.wait()


def expert_call(index, column_place, pieces, hits, router, w_gate, w_up, backs, held, seq):
    local_experts, width, hidden_units = w_gate.shape
    n_slices, n_blocks = column_place.shape[0], index.shape[0] - 1
    wide = hidden_units // n_slices
    total = sum(piece.shape[0] for piece in pieces)
    block = total // n_blocks
    span = local_experts * hidden_units
    tile = 512
    assert n_slices >= 2

    def at_slice(step):
        return jnp.minimum(step, n_slices - 1)

    def at_tile(step):
        return jnp.maximum(step - n_slices, 0)

    weight_spec = pl.BlockSpec(
        (local_experts, width, wide), lambda i, index, column: (0, 0, at_slice(i))
    )
    rows_spec = pl.BlockSpec(
        (local_experts, tile, hidden_units), lambda i, index, column: (0, at_tile(i), 0)
    )

    def block_spec(at, columns, tiled):
        if tiled:
            return pl.BlockSpec(
                (block, columns), lambda i, index, column: (index[at], at_slice(i))
            )
        return pl.BlockSpec((block, columns), lambda i, index, column: (index[at], 0))

    in_specs = [pl.BlockSpec(piece.shape, lambda i, index, column: (0, 0)) for piece in pieces]
    in_specs += [block_spec(at, local_experts, False) for at in range(n_blocks)]
    in_specs += [pl.BlockSpec(router.shape, lambda i, index, column: (0, 0))]
    in_specs += [weight_spec, weight_spec, rows_spec, rows_spec]
    in_specs += [block_spec(at, wide, True) for _ in range(local_experts) for at in range(n_blocks)]
    operands = [*pieces, *[hits] * n_blocks, router, w_gate, w_up, w_gate, w_up]
    operands += [back for back in backs for _ in range(n_blocks)]
    aliases = {}
    if held is not None:
        aliases = {2 + len(operands) + i: i for i in range(5)}
        in_specs += [ANY_SPEC] * 5
        operands += held
    made = jax.ShapeDtypeStruct((seq, span), BF16)
    rows = [piece.shape[0] for piece in pieces]
    results = pl.pallas_call(
        lambda *refs: expert_kernel(len(pieces), rows, n_blocks, n_slices, *refs),
        out_shape=[
            jax.ShapeDtypeStruct((seq, width), BF16),
            jax.ShapeDtypeStruct((seq, 128), F32),
            made,
            made,
            made,
        ]
        + [jax.ShapeDtypeStruct((block, width), BF16)] * n_blocks,
        grid_spec=pltpu.PrefetchScalarGridSpec(
            num_scalar_prefetch=2,
            grid=(n_slices + width // tile,),
            in_specs=in_specs,
            out_specs=[ANY_SPEC] * 5
            + [pl.BlockSpec((block, tile), lambda i, index, column: (0, at_tile(i)))] * n_blocks,
            scratch_shapes=[
                pltpu.VMEM((total, width), BF16),
                pltpu.VMEM((total, 128), F32),
                pltpu.VMEM((total, 128), F32),
                pltpu.VMEM((2, 3, total, local_experts * wide), BF16),
                pltpu.VMEM((total, 2 * span), BF16),
                pltpu.SemaphoreType.DMA((2, 3, n_blocks)),
                pltpu.SemaphoreType.DMA((2, n_blocks)),
            ],
        ),
        input_output_aliases=aliases,
        compiler_params=params(),
        cost_estimate=cost(
            8 * total * width * span, 8 * width * span + 10 * total * span, total * span
        ),
    )(index, column_place, *operands)
    return results[:5], results[5:]


def back_rows_kernel(n_blocks, n_arrays, index_ref, column_ref, *refs):
    rows_refs, refs = refs[: n_blocks * n_arrays], refs[n_blocks * n_arrays :]
    weight_refs, outs, held = refs[:n_arrays], refs[n_arrays:-1], refs[-1]
    local_experts, _, hidden_units = weight_refs[0].shape
    n_slices = column_ref.shape[0]
    wide = hidden_units // n_slices
    block = rows_refs[0].shape[0]

    @pl.when(pl.program_id(0) == 0)
    def _():
        for at in range(n_blocks):
            for array in range(n_arrays):
                for expert in range(local_experts):
                    for part in range(n_slices):
                        first = (array * local_experts + expert) * hidden_units + part * wide
                        source = pl.multiple_of(
                            (column_ref[part] * local_experts + expert) * wide, 128
                        )
                        held[at * block : (at + 1) * block, first : first + wide] = rows_refs[
                            at * n_arrays + array
                        ][:, pl.ds(source, wide)]

    total = None
    for array in range(n_arrays):
        for expert in range(local_experts):
            first = (array * local_experts + expert) * hidden_units
            part = matmul_nt(held[:, first : first + hidden_units], weight_refs[array][expert])
            total = part if total is None else total + part
    for at in range(n_blocks):
        outs[at][...] = total[at * block : (at + 1) * block].astype(BF16)


def back_rows(index, column_place, arrays, weights, block, tile=256):
    n_blocks, n_arrays = index.shape[0], len(arrays)
    local_experts, width, hidden_units = weights[0].shape
    span = local_experts * hidden_units

    def row_spec(at):
        return pl.BlockSpec((block, span), lambda i, index, column: (index[at], 0))

    return pl.pallas_call(
        lambda *refs: back_rows_kernel(n_blocks, n_arrays, *refs),
        out_shape=[jax.ShapeDtypeStruct((block, width), BF16)] * n_blocks,
        grid_spec=pltpu.PrefetchScalarGridSpec(
            num_scalar_prefetch=2,
            grid=(width // tile,),
            in_specs=[row_spec(at) for at in range(n_blocks) for _ in range(n_arrays)]
            + [
                pl.BlockSpec(
                    (local_experts, tile, hidden_units), lambda i, index, column: (0, i, 0)
                )
            ]
            * n_arrays,
            out_specs=[pl.BlockSpec((block, tile), lambda i, index, column: (0, i))] * n_blocks,
            scratch_shapes=[pltpu.VMEM((n_blocks * block, n_arrays * span), BF16)],
        ),
        compiler_params=params(),
        cost_estimate=cost(
            2 * n_blocks * block * width * span * n_arrays, 2 * width * span * n_arrays
        ),
    )(index, column_place, *(list(arrays) * n_blocks), *weights)


def weight_grad_kernel(n_adds, left_ref, right_ref, *refs):
    total = matmul_tn(left_ref[...], right_ref[...])
    for ref in refs[:n_adds]:
        total += ref[...].astype(F32)
    out_ref = refs[-1]
    if len(out_ref.shape) == 2:
        out_ref[...] = total.astype(out_ref.dtype)
    else:
        wide = out_ref.shape[2]
        for expert in range(out_ref.shape[0]):
            out_ref[expert] = total[:, expert * wide : (expert + 1) * wide]


def weight_grad(left, right, first, columns, adds=(), experts=None, tile=512):
    seq, width = left.shape
    assert first % columns == 0
    if experts is None:
        out_shape = jax.ShapeDtypeStruct((width, columns), BF16)
        out_spec = pl.BlockSpec((tile, columns), lambda i: (i, 0))
    else:
        out_shape = jax.ShapeDtypeStruct((experts, width, columns // experts), F32)
        out_spec = pl.BlockSpec((experts, tile, columns // experts), lambda i: (0, i, 0))

    def add_spec(at):
        return pl.BlockSpec((tile, columns), lambda i: (i, at))

    return pl.pallas_call(
        lambda *refs: weight_grad_kernel(len(adds), *refs),
        out_shape=out_shape,
        grid=(width // tile,),
        in_specs=[
            pl.BlockSpec((seq, tile), lambda i: (0, i)),
            pl.BlockSpec((seq, columns), lambda i: (0, first // columns)),
        ]
        + [add_spec(at) for _, at in adds],
        out_specs=out_spec,
        compiler_params=params(),
        cost_estimate=cost(2 * seq * width * columns, 2 * width * (seq + columns)),
    )(left, right, *(value for value, _ in adds))


def body(
    tokens,
    seq_lengths,
    routes,
    w_query,
    w_key,
    w_value,
    w_out,
    gain_attn,
    gain_query,
    gain_key,
    gain_ffn,
    w_router,
    w_gate,
    w_up,
    w_down_t,
    cotangent,
):
    rows, width = tokens.shape
    local_experts, _, hidden_units = w_gate.shape
    groups, n_dp = lax.axis_size("expert"), lax.axis_size("dp")
    experts_all = local_experts * groups
    seq = groups * rows
    own = width // groups
    weight_rows = w_query.shape[0]
    chips = n_dp // CORES
    me, dp = lax.axis_index("expert"), lax.axis_index("dp")
    both_axes = ("dp", "expert")
    ring = Ring(groups)
    positions = jnp.arange(seq, dtype=jnp.int32)
    my_rows = me * rows + jnp.arange(rows, dtype=jnp.int32)
    seq_length = lax.dynamic_index_in_dim(seq_lengths, dp, 0, keepdims=True)
    used = (my_rows < seq_length[0]).astype(F32)[:, None]

    expert_ids = jnp.arange(experts_all, dtype=jnp.int32)
    chosen = jnp.any(routes[:, :, None] == expert_ids[None, None, :], axis=1)
    chosen_low = chosen.astype(BF16)

    hit_columns = rows * local_experts // weight_rows
    hits_out = chosen_low.reshape(rows, groups, local_experts).transpose(1, 0, 2)
    extra = jnp.concatenate(
        [jnp.stack([gain_attn, gain_query, gain_key, gain_ffn], axis=1), w_router], axis=1
    )
    extra_columns = extra.shape[1]
    pad = -(extra_columns + hit_columns) % 128
    send = jnp.concatenate(
        [w.reshape(weight_rows, groups, own).transpose(1, 0, 2) for w in (w_query, w_key, w_value)]
        + [
            jnp.broadcast_to(extra[None], (groups, weight_rows, extra_columns)),
            hits_out.reshape(groups, weight_rows, hit_columns),
            jnp.zeros((groups, weight_rows, pad), BF16),
        ],
        axis=2,
    )
    moves = [(e * n_dp + i, i * groups + e) for e in range(groups) for i in range(n_dp)]
    half = HEAD_DIM // 2
    frequency = ROPE_BASE ** (-(jnp.arange(half, dtype=F32) * 2.0) / HEAD_DIM)
    angles = positions.astype(F32)[:, None] * frequency[None, :]
    cosine, sine = jnp.cos(angles), jnp.sin(angles)
    cosine = jnp.concatenate([cosine, cosine], axis=1)
    sine = jnp.concatenate([-sine, sine], axis=1)
    start = {}
    far = groups // 2
    arrival = [0] + [o for step in range(1, far) for o in (groups - step, step)] + [far]
    per_call = 4
    calls = groups // per_call
    call_index = [
        jnp.stack([ring.natural[o] for o in arrival[at : at + per_call]] + [me])
        for at in range(0, groups, per_call)
    ]

    def make_got(pieces):
        start["got"] = lax.all_to_all(send, "expert", split_axis=0, concat_axis=0, tiled=True)
        start["in"] = DpGather(start["got"].reshape(groups * weight_rows, -1), n_dp)
        return (start["got"], cosine, sine, *call_index)

    def make_y(pieces):
        start["out"] = DpGather(lax.ppermute(w_out, both_axes, moves), n_dp)
        return (*start["in"].over_y(), start["out"].chunk)

    hooks = {far - 1: make_got, far: make_y}
    tokens_all = place_blocks(ring, ring.gather(tokens, hooks), rows, width)
    start["in"].over_cores()
    got, projections = start["got"], start["in"].rows()
    hits = got[:, :, 3 * own + extra_columns : 3 * own + extra_columns + hit_columns]
    hits = hits.reshape(seq, local_experts).astype(F32)
    w_qkv = projections
    small = projections[:, 3 * own : 3 * own + extra_columns]
    gains_full = small[:, :4].T.astype(F32)
    full_router = small[:, 4:]

    resid_in = tokens.astype(F32)
    attn_gain, ffn_gain = gains_full[0:1], gains_full[3:4]
    [cot_own] = together((cotangent,), (tokens_all,))
    cot_all = lax.all_gather(cot_own, "expert", axis=0, tiled=True)
    attn_in, qkv, squares = project(tokens_all, attn_gain, w_qkv, 3 * own)
    [start["out"].chunk] = together((start["out"].chunk,), (squares,))
    out_over_y = start["out"].over_y()
    [squares] = together((expert_sum(squares, groups),), out_over_y)
    gains_own = lax.dynamic_slice(gains_full, (1, me * own), (2, own))
    q, k, v, attended = attend(seq_length, qkv, squares, gains_own, cosine, sine)
    [attended] = together((attended,), start["out"].over_cores())
    own_out = start["out"].rows()

    def block_of(value, o):
        return lax.dynamic_slice(value, (ring.natural[o] * rows, 0), (rows, value.shape[1]))

    out_far = matmul(block_of(attended, far), own_out).astype(BF16)
    out_part = matmul(attended, own_out).astype(BF16)
    backs = []

    def make_back(expert):
        backs.append(matmul(cot_all, w_down_t[expert]).astype(BF16))
        return (backs[-1],)

    hooks = {
        far - 1: lambda: make_back(0),
        far: lambda: (
            *[make_back(expert)[0] for expert in range(1, local_experts)],
            full_router,
            hits,
        ),
    }
    resid_mid = resid_in + ring.scatter(
        lambda o: out_far if o == far else block_of(out_part, o), hooks
    )
    mid_scale = norm_scale(resid_mid)
    ffn_in = (resid_mid * mid_scale * ffn_gain).astype(BF16)

    distances = (
        [2 * y + 1 for y in range(chips)] + [2 * y for y in range(1, chips)] + [0]
    )
    place_of = np.zeros((n_dp,), np.int32)
    place_of[np.array(distances)] = np.arange(n_dp)
    column_place = jnp.asarray(place_of)[jnp.arange(n_dp, dtype=jnp.int32) ^ dp]
    held, drow_terms = [], {}

    def expert_pieces(pieces, at):
        given = pieces[at:] if at + per_call == groups else pieces[at : at + per_call]
        order = [o for o, _, _ in given[:per_call]]
        result, blocks = expert_call(
            call_index[at // per_call],
            column_place,
            [piece for _, _, piece in given],
            hits,
            full_router,
            w_gate,
            w_up,
            backs,
            held[-1] if held else None,
            seq,
        )
        held.append(result)
        drow_terms.update(zip(order, blocks))
        return result

    hooks = {}
    for call in range(calls - 1):
        step = (call + 1) * per_call // 2 + 1
        hooks[step] = lambda pieces, at=call * per_call: expert_pieces(pieces, at)
    pieces = ring.gather(ffn_in, hooks)
    expert_pieces(pieces, groups - per_call)
    ffn_all, pair_dots, scaled_hidden, dgates, dups = held[-1]
    pairs = []

    def make_pairs():
        out = pair_dots[:, :local_experts].reshape(groups, rows, local_experts).transpose(0, 2, 1)
        pairs.append(lax.all_to_all(out, "expert", split_axis=0, concat_axis=0, tiled=True))
        return tuple(pairs)

    slice_columns = local_experts * hidden_units // n_dp
    swap = [(i, i ^ 1) for i in range(n_dp)]
    sides = [(cot_all, scaled_hidden), (ffn_all, dgates), (ffn_all, dups)]
    other, adds = {}, {}

    def make_sent(which):
        sent = weight_grad(*sides[which], 0, chips * slice_columns)
        other[which] = lax.ppermute(sent, "dp", swap)
        adds[which] = [(other[which], 0)]
        return (sent,)

    parts = {}

    def make_part(which):
        parts[which] = [
            weight_grad(
                *sides[which],
                (chips + y - 1) * slice_columns,
                slice_columns,
                [(other[which], y)],
            )
            for y in range(1, chips)
        ]
        return tuple(parts[which])

    def send_part(which, after):
        sent = together(tuple(parts[which]), (after,))
        got = [
            lax.ppermute(part, "dp", [(i, i ^ (2 * y)) for i in range(n_dp)])
            for y, part in zip(range(1, chips), sent)
        ]
        adds[which] += [(part, 0) for part in got]
        return tuple(got)

    hooks = {
        far - 2: lambda: make_sent(0),
        far - 1: lambda: (*make_sent(1), *make_part(0)),
        far: lambda: (*make_pairs(), *make_sent(2), *make_part(1)),
    }
    drow = ring.scatter(lambda o: drow_terms[o], hooks)

    grad_rows = cotangent.astype(F32)
    dprobs = pairs[0].reshape(experts_all, rows).T
    probs = jax.nn.softmax(matmul(ffn_in, full_router), axis=-1)
    dlogits = probs * (dprobs - jnp.sum(probs * dprobs, axis=1, keepdims=True))
    dlogits = dlogits.astype(BF16)
    grad_router = matmul_tn(ffn_in, dlogits)
    dffn = drow + matmul_nt(dlogits, full_router)
    grad_gain_ffn = jnp.sum(dffn * resid_mid * mid_scale, axis=0, keepdims=True)
    scaled = dffn * ffn_gain
    mid_grads = (
        grad_rows
        + mid_scale * scaled
        - resid_mid * mid_scale**3 * jnp.mean(scaled * resid_mid, axis=1, keepdims=True)
    )
    mid_low = mid_grads.astype(BF16)

    def make_moe(pieces):
        return back_rows(
            jnp.zeros((1,), jnp.int32), column_place, (scaled_hidden,), (w_down_t,), seq
        )

    moe_made = []
    first = send_part(0, mid_low)
    mid_pieces = ring.gather(
        mid_low,
        {
            1: lambda pieces: make_part(2),
            2: lambda pieces: moe_made.extend(make_moe(pieces)) or moe_made,
        },
    )
    mid_all = place_blocks(ring, mid_pieces, rows, width)
    [mid_all] = together((mid_all,), first)
    second = send_part(1, mid_all)
    grad_heads = matmul_nt(mid_all, own_out).astype(BF16)

    moe_part, grad_heads = lax.optimization_barrier((moe_made[0], grad_heads))
    moe_rows = lax.psum_scatter(moe_part, "expert", scatter_dimension=0, tiled=True).astype(F32)
    output = (resid_mid + moe_rows).astype(BF16)

    dq, dk, dv, dots, dgains = attend_back(
        seq_length, qkv, squares, gains_own, cosine, sine, q, k, v, grad_heads
    )
    dots = expert_sum(dots, groups)
    dqkv, din_part = finish(dq, dk, dv, qkv, squares, dots, w_qkv)
    third = []

    def make_own(which, after):
        left, right = sides[which]
        [left] = together((left,), after)
        return weight_grad(
            left,
            right,
            (n_dp - 1) * slice_columns,
            slice_columns,
            adds[which],
            local_experts,
        )

    def middle():
        third.extend(send_part(2, second[0]))
        return second

    spread_gains = lax.dynamic_update_slice(jnp.zeros((2, width), F32), dgains, (0, me * own))
    lane = lax.broadcasted_iota(jnp.int32, (1, width), 1)
    sums = jnp.where(
        lane == 0,
        jnp.sum(used * resid_mid * resid_mid),
        jnp.where(lane == 1, jnp.sum(used * moe_rows * moe_rows), 0.0),
    )
    rest = jnp.concatenate([spread_gains, grad_gain_ffn, sums, grad_router.T], axis=0)
    hooks = {far - 2: middle, far: lambda: (rest,)}
    dattn = ring.scatter(lambda o: block_of(din_part, o), hooks)
    [rest] = together((rest,), (dattn,))
    rest = expert_sum(rest, groups)
    all_hops = rest
    own_grads = [make_own(which, (rest,)) for which in range(3)]
    rest = dp_sum(rest, n_dp)
    grad_down, grad_gate_w, grad_up_w = own_grads
    in_scale = norm_scale(resid_in)
    scaled = dattn * attn_gain
    input_grad = (
        mid_grads
        + in_scale * scaled
        - resid_in * in_scale**3 * jnp.mean(scaled * resid_in, axis=1, keepdims=True)
    ).astype(BF16)

    block = width // n_dp

    def projection_term(rel):
        left = lax.dynamic_slice(attn_in, (0, (dp ^ rel) * block), (seq, block))
        return matmul_tn(left, dqkv)

    reduced = dp_reduce(projection_term, n_dp).astype(BF16)
    [reduced] = together((reduced,), (all_hops,))
    reduced = lax.all_to_all(
        reduced.reshape(groups, weight_rows, 3 * own),
        "expert",
        split_axis=0,
        concat_axis=0,
        tiled=True,
    ).astype(F32)
    grads = [
        reduced[:, :, i * own : (i + 1) * own].transpose(1, 0, 2).reshape(weight_rows, width)
        for i in range(3)
    ]
    grad_gain_attn = (
        sum(jnp.sum(g * w.astype(F32), axis=1) for g, w in zip(grads, (w_query, w_key, w_value)))
        / gain_attn.astype(F32)
    )
    out_grads = matmul_tn(attended, mid_all)

    def out_term(rel):
        return lax.dynamic_slice(out_grads, ((dp ^ rel) * weight_rows, 0), (weight_rows, width))

    grad_out = dp_reduce(out_term, n_dp).astype(BF16)
    [grad_out] = together((grad_out,), (all_hops,))
    grad_out = lax.ppermute(grad_out, both_axes, [(b, a) for a, b in moves]).astype(F32)

    mine = lax.dynamic_slice(
        rest, (0, (dp * groups + me) * weight_rows), (rest.shape[0], weight_rows)
    )
    counted = jnp.sum(seq_lengths).astype(F32) * width
    rms_resid = jnp.sqrt(rest[3, 0] / counted)
    rms_moe = jnp.sqrt(rest[3, 1] / counted)
    return (
        output,
        input_grad,
        grads[0],
        grads[1],
        grads[2],
        grad_out,
        grad_gain_attn,
        mine[0],
        mine[1],
        mine[2],
        mine[4:].T,
        grad_gate_w,
        grad_up_w,
        grad_down,
        rms_resid,
        rms_moe,
    )


def solution(mesh):
    both = ("dp", "expert")
    row, vector, expert = P(both, None), P(both), P("expert", None, None)
    placed = (
        row,
        P(),
        row,
        row,
        row,
        row,
        row,
        vector,
        vector,
        vector,
        vector,
        row,
        expert,
        expert,
        expert,
        row,
    )
    grads = P("expert", None, "dp")
    return jax.shard_map(
        body,
        mesh=mesh,
        in_specs=placed,
        out_specs=(row,) * 6 + (vector,) * 4 + (row, grads, grads, grads, P(), P()),
        check_vma=False,
    )
```

```python
import jax
import jax.numpy as jnp
import numpy as np
from jax import lax
from jax.experimental import pallas as pl
from jax.experimental.pallas import tpu as pltpu
from jax.sharding import PartitionSpec as P

HEADS = 16
HEAD_DIM = 128
TOP = 8
EPSILON = 1e-05
ROPE_BASE = 10000.0
SCALE = HEAD_DIM ** (-0.5)
NEG = -1e30
Z_CHIPS = 4
CORES = 2
F32 = jnp.float32
BF16 = jnp.bfloat16


def ring_tables(groups):
    x_chips = groups // Z_CHIPS
    walk = []
    for x in range(x_chips):
        column = range(1, Z_CHIPS) if x % 2 == 0 else range(Z_CHIPS - 1, 0, -1)
        walk += [z * x_chips + x for z in column]
    walk += [x for x in range(x_chips - 1, -1, -1)]
    place = np.zeros((groups,), np.int32)
    for at, owner in enumerate(walk):
        place[owner] = at
    return np.array(walk, np.int32), place


class Ring:
    def __init__(self, groups):
        self.size = groups
        self.walk, self.place = ring_tables(groups)
        size = groups
        self.ahead = [(int(self.walk[i]), int(self.walk[(i + 1) % size])) for i in range(size)]
        self.back = [(b, a) for a, b in self.ahead]
        mine = jnp.asarray(self.place)[lax.axis_index("expert")]
        self.natural = jnp.asarray(self.walk)[(mine + jnp.arange(size, dtype=jnp.int32)) % size]

    def up(self, value):
        return lax.ppermute(value, "expert", self.ahead)

    def down(self, value):
        return lax.ppermute(value, "expert", self.back)

    def gather(self, block, hooks=None):
        hooks = hooks or {}
        half = self.size // 2
        rows = block.shape[0]
        pieces = [(0, 0, block)]
        up, down = block, block
        for step in range(1, half):
            made = hooks[step](pieces) if step in hooks else ()
            up, down = together((self.up(up), self.down(down)), made)
            pieces += [(self.size - step, 0, up), (step, 0, down)]
        made = hooks[half](pieces) if half in hooks else ()
        up, down = together((self.up(up[: rows // 2]), self.down(down[rows // 2 :])), made)
        pieces += [(half, 0, up), (half, rows // 2, down)]
        return pieces

    def scatter(self, term, hooks=None):
        hooks = hooks or {}
        half = self.size // 2
        far = term(half)
        rows = far.shape[0]
        up = self.up(far[: rows // 2])
        down = self.down(far[rows // 2 :])

        def add(left, right):
            return (left.astype(F32) + right.astype(F32)).astype(BF16)

        for step in range(half - 1, 0, -1):
            made = hooks[half - step]() if half - step in hooks else ()
            up, down = together((up, down), made)
            ahead, behind = term(step), term(self.size - step)
            if step == half - 1:
                ahead = jnp.concatenate([add(up, ahead[: rows // 2]), ahead[rows // 2 :]], axis=0)
                behind = jnp.concatenate(
                    [behind[: rows // 2], add(down, behind[rows // 2 :])], axis=0
                )
            else:
                ahead, behind = add(up, ahead), add(down, behind)
            up, down = self.up(ahead), self.down(behind)
        made = hooks[half]() if half in hooks else ()
        up, down = together((up, down), made)
        return up.astype(F32) + down.astype(F32) + term(0).astype(F32)


def together(values, made):
    if not made:
        return values
    return lax.optimization_barrier((*values, *made))[: len(values)]


def place_blocks(ring, pieces, rows, width, dtype=BF16):
    buffer = jnp.zeros((ring.size * rows, width), dtype)
    for o, start, piece in pieces:
        buffer = lax.dynamic_update_slice(
            buffer, piece.astype(dtype), (ring.natural[o] * rows + start, 0)
        )
    return buffer


def expert_sum(value, groups):
    step = 1
    while step < groups:
        value = value + lax.ppermute(value, "expert", [(i, i ^ step) for i in range(groups)])
        step *= 2
    return value


def dp_sum(value, n_dp):
    step = 1
    while step < n_dp:
        value = value + lax.ppermute(value, "dp", [(i, i ^ step) for i in range(n_dp)])
        step *= 2
    return value


class DpGather:
    def __init__(self, chunk, n_dp):
        self.chunk, self.n_dp = chunk, n_dp

    def over_y(self):
        n_dp = self.n_dp
        self.held = [(0, self.chunk)] + [
            (2 * y, lax.ppermute(self.chunk, "dp", [(i, i ^ (2 * y)) for i in range(n_dp)]))
            for y in range(1, n_dp // CORES)
        ]
        return tuple(part for _, part in self.held[1:])

    def over_cores(self):
        swap = [(i, i ^ 1) for i in range(self.n_dp)]
        new = [(rel ^ 1, lax.ppermute(part, "dp", swap)) for rel, part in self.held]
        self.held += new
        return tuple(part for _, part in new)

    def rows(self):
        rows, width = self.chunk.shape
        me = lax.axis_index("dp")
        buffer = jnp.zeros((self.n_dp * rows, width), self.chunk.dtype)
        for rel, part in self.held:
            buffer = lax.dynamic_update_slice(buffer, part, ((me ^ rel) * rows, 0))
        return buffer


def dp_reduce(term, n_dp):
    swap = [(i, i ^ 1) for i in range(n_dp)]
    chips = n_dp // CORES
    other = [lax.ppermute(term(2 * y + 1).astype(BF16), "dp", swap) for y in range(chips)]
    total = None
    for y in range(1, chips):
        part = (term(2 * y) + other[y].astype(F32)).astype(BF16)
        part = lax.ppermute(part, "dp", [(i, i ^ (2 * y)) for i in range(n_dp)]).astype(F32)
        total = part if total is None else total + part
    own = term(0) + other[0].astype(F32)
    return own if total is None else own + total


def norm_scale(values):
    return lax.rsqrt(jnp.mean(values * values, axis=-1, keepdims=True) + EPSILON)


def matmul(left, right):
    return jnp.dot(left, right, preferred_element_type=F32)


def matmul_nt(left, right):
    return lax.dot_general(left, right, (((1,), (1,)), ((), ())), preferred_element_type=F32)


def matmul_tn(left, right):
    return lax.dot_general(left, right, (((0,), (0,)), ((), ())), preferred_element_type=F32)


def masked(scores, first_row, length):
    rows, columns = scores.shape
    row = first_row + lax.broadcasted_iota(jnp.int32, (rows, columns), 0)
    column = lax.broadcasted_iota(jnp.int32, (rows, columns), 1)
    return jnp.where((column <= row) & (column < length), scores * SCALE, NEG)


def turn(values, cosine, sine):
    return values * cosine + pltpu.roll(values, HEAD_DIM // 2, 1) * sine


def turn_back(values, cosine, sine):
    return values * cosine - pltpu.roll(values, HEAD_DIM // 2, 1) * sine


VMEM_LIMIT = 56 << 20
SMEM_SPEC = pl.BlockSpec(memory_space=pltpu.SMEM)
VMEM_SPEC = pl.BlockSpec(memory_space=pltpu.VMEM)
ANY_SPEC = pl.BlockSpec(memory_space=pl.ANY)


def params():
    return pltpu.CompilerParams(vmem_limit_bytes=VMEM_LIMIT)


def cost(flops, bytes_accessed, transcendentals=0):
    return pl.CostEstimate(
        flops=flops, bytes_accessed=bytes_accessed, transcendentals=transcendentals
    )


def as_rows(first, second):
    lane = lax.broadcasted_iota(jnp.int32, (first.shape[0], 128), 1)
    both = jnp.where(lane == 0, first, jnp.where(lane == 1, second, 0.0))
    return both.T[:8]


def as_columns(rows):
    return rows.T


def project_kernel(tokens_ref, gain_ref, w_ref, in_ref, qkv_ref, squares_ref):
    own = qkv_ref.shape[1] // 3
    values = tokens_ref[...].astype(F32)
    normed = (values * norm_scale(values) * gain_ref[...]).astype(BF16)
    in_ref[...] = normed
    qkv = matmul(normed, w_ref[...])
    qkv_ref[...] = qkv
    query, key = qkv[:, :own], qkv[:, own : 2 * own]
    squares_ref[...] = as_rows(
        jnp.sum(query * query, axis=1, keepdims=True), jnp.sum(key * key, axis=1, keepdims=True)
    )


def project(tokens, gain, w_qkv, columns):
    seq, width = tokens.shape
    tile = min(256, seq)
    return pl.pallas_call(
        project_kernel,
        grid=(seq // tile,),
        out_shape=[
            jax.ShapeDtypeStruct((seq, width), BF16),
            jax.ShapeDtypeStruct((seq, columns), F32),
            jax.ShapeDtypeStruct((8, seq), F32),
        ],
        in_specs=[
            pl.BlockSpec((tile, width), lambda i: (i, 0)),
            pl.BlockSpec((1, width), lambda i: (0, 0)),
            pl.BlockSpec((width, columns), lambda i: (0, 0)),
        ],
        out_specs=[
            pl.BlockSpec((tile, width), lambda i: (i, 0)),
            pl.BlockSpec((tile, columns), lambda i: (i, 0)),
            pl.BlockSpec((8, tile), lambda i: (0, i)),
        ],
        compiler_params=params(),
        cost_estimate=cost(2 * seq * width * columns, 8 * seq * width),
    )(tokens, gain, w_qkv)


def attend_kernel(
    length_ref, qkv_ref, squares_ref, gain_ref, cos_ref, sin_ref, q_ref, k_ref, v_ref, o_ref
):
    seq, own = q_ref.shape
    tile = min(256, seq)
    width = HEADS * HEAD_DIM
    length = length_ref[0]
    for start in range(0, seq, tile):
        rows = slice(start, start + tile)
        squares = as_columns(squares_ref[:, rows])
        cosine, sine = cos_ref[rows, :], sin_ref[rows, :]
        for part, out_ref in ((0, q_ref), (1, k_ref)):
            scale = lax.rsqrt(squares[:, part : part + 1] / width + EPSILON)
            for first in range(0, own, HEAD_DIM):
                columns = slice(first, first + HEAD_DIM)
                raw = qkv_ref[rows, part * own + first : part * own + first + HEAD_DIM]
                normed = raw * scale * gain_ref[part : part + 1, columns]
                out_ref[rows, columns] = turn(normed, cosine, sine).astype(BF16)
        v_ref[rows, :] = qkv_ref[rows, 2 * own : 3 * own].astype(BF16)
    for first in range(0, own, HEAD_DIM):
        columns = slice(first, first + HEAD_DIM)
        for start in range(0, seq, tile):
            rows, keys = slice(start, start + tile), slice(0, start + tile)
            scores = masked(matmul_nt(q_ref[rows, columns], k_ref[keys, columns]), start, length)
            expo = jnp.exp(scores - jnp.max(scores, axis=-1, keepdims=True))
            total = jnp.sum(expo, axis=-1, keepdims=True)
            probs = (expo / total).astype(BF16)
            o_ref[rows, columns] = matmul(probs, v_ref[keys, columns]).astype(BF16)


def attend_back_kernel(
    length_ref,
    qkv_ref,
    squares_ref,
    gain_ref,
    cos_ref,
    sin_ref,
    q_ref,
    k_ref,
    v_ref,
    do_ref,
    dq_ref,
    dk_ref,
    dv_ref,
    dots_ref,
    dgain_ref,
    k_total,
    v_total,
):
    seq, own = q_ref.shape
    tile = min(256, seq)
    width = HEADS * HEAD_DIM
    length = length_ref[0]
    for first in range(0, own, HEAD_DIM):
        columns = slice(first, first + HEAD_DIM)
        k_total[...] = jnp.zeros_like(k_total)
        v_total[...] = jnp.zeros_like(v_total)
        for start in range(0, seq, tile):
            rows, keys = slice(start, start + tile), slice(0, start + tile)
            q, k, v = q_ref[rows, columns], k_ref[keys, columns], v_ref[keys, columns]
            do = do_ref[rows, columns]
            scores = masked(matmul_nt(q, k), start, length)
            expo = jnp.exp(scores - jnp.max(scores, axis=-1, keepdims=True))
            probs = expo / jnp.sum(expo, axis=-1, keepdims=True)
            dprobs = matmul_nt(do, v)
            mean = jnp.sum(probs * dprobs, axis=-1, keepdims=True)
            dscores = (probs * (dprobs - mean)).astype(BF16)
            dq_ref[rows, columns] = matmul(dscores, k) * SCALE
            k_total[keys, :] += matmul_tn(dscores, q)
            v_total[keys, :] += matmul_tn(probs.astype(BF16), do)
        dk_ref[:, columns] = k_total[...] * SCALE
        dv_ref[:, columns] = v_total[...].astype(BF16)
    dgain_ref[...] = jnp.zeros_like(dgain_ref)
    for start in range(0, seq, tile):
        rows = slice(start, start + tile)
        squares = as_columns(squares_ref[:, rows])
        cosine, sine = cos_ref[rows, :], sin_ref[rows, :]
        both = []
        for part, out_ref in ((0, dq_ref), (1, dk_ref)):
            scale = lax.rsqrt(squares[:, part : part + 1] / width + EPSILON)
            dot = jnp.zeros((tile, 1), F32)
            for first in range(0, own, HEAD_DIM):
                columns = slice(first, first + HEAD_DIM)
                raw = qkv_ref[rows, part * own + first : part * own + first + HEAD_DIM]
                grad = turn_back(out_ref[rows, columns], cosine, sine)
                dgain_ref[part : part + 1, columns] += jnp.sum(
                    grad * raw * scale, axis=0, keepdims=True
                )
                grad = grad * gain_ref[part : part + 1, columns]
                dot += jnp.sum(grad * raw, axis=-1, keepdims=True)
                out_ref[rows, columns] = grad * scale
            both.append(dot)
        dots_ref[:, rows] = as_rows(*both)


def attend(length, qkv, squares, gains, cosine, sine):
    seq, own = qkv.shape[0], qkv.shape[1] // 3
    shape = jax.ShapeDtypeStruct((seq, own), BF16)
    return pl.pallas_call(
        attend_kernel,
        out_shape=[shape] * 4,
        in_specs=[SMEM_SPEC] + [VMEM_SPEC] * 5,
        out_specs=[VMEM_SPEC] * 4,
        compiler_params=params(),
        cost_estimate=cost(4 * seq * seq * own, 20 * seq * own, seq * seq),
    )(length, qkv, squares, gains, cosine, sine)


def attend_back(length, qkv, squares, gains, cosine, sine, q, k, v, do):
    seq, own = q.shape
    wide = jax.ShapeDtypeStruct((seq, own), F32)
    return pl.pallas_call(
        attend_back_kernel,
        out_shape=[
            wide,
            wide,
            jax.ShapeDtypeStruct((seq, own), BF16),
            jax.ShapeDtypeStruct((8, seq), F32),
            jax.ShapeDtypeStruct((2, own), F32),
        ],
        in_specs=[SMEM_SPEC] + [VMEM_SPEC] * 9,
        out_specs=[VMEM_SPEC] * 5,
        scratch_shapes=[pltpu.VMEM((seq, HEAD_DIM), F32)] * 2,
        compiler_params=params(),
        cost_estimate=cost(10 * seq * seq * own, 40 * seq * own, seq * seq),
    )(length, qkv, squares, gains, cosine, sine, q, k, v, do)


def finish_kernel(
    dq_ref, dk_ref, dv_ref, qkv_ref, squares_ref, dots_ref, w_ref, dqkv_ref, din_ref
):
    own = dq_ref.shape[1]
    width = HEADS * HEAD_DIM
    scale = lax.rsqrt(as_columns(squares_ref[...]) / width + EPSILON)
    factor = scale * scale * scale * as_columns(dots_ref[...]) / width
    for part, grad_ref in ((0, dq_ref), (1, dk_ref)):
        columns = slice(part * own, (part + 1) * own)
        grad = grad_ref[...] - qkv_ref[:, columns] * factor[:, part : part + 1]
        dqkv_ref[:, columns] = grad.astype(BF16)
    dqkv_ref[:, 2 * own :] = dv_ref[...]
    din_ref[...] = matmul_nt(dqkv_ref[...], w_ref[...]).astype(BF16)


def finish(dq, dk, dv, qkv, squares, dots, w_qkv):
    seq, own = dq.shape
    width = w_qkv.shape[0]
    tile = min(256, seq)
    narrow = pl.BlockSpec((tile, own), lambda i: (i, 0))
    wide = pl.BlockSpec((tile, 3 * own), lambda i: (i, 0))
    flat = pl.BlockSpec((8, tile), lambda i: (0, i))
    return pl.pallas_call(
        finish_kernel,
        grid=(seq // tile,),
        out_shape=[
            jax.ShapeDtypeStruct((seq, 3 * own), BF16),
            jax.ShapeDtypeStruct((seq, width), BF16),
        ],
        in_specs=[narrow, narrow, narrow, wide, flat, flat]
        + [pl.BlockSpec((width, 3 * own), lambda i: (0, 0))],
        out_specs=[wide, pl.BlockSpec((tile, width), lambda i: (i, 0))],
        compiler_params=params(),
        cost_estimate=cost(6 * seq * width * own, 4 * seq * width),
    )(dq, dk, dv, qkv, squares, dots, w_qkv)


def expert_kernel(n_pieces, piece_rows, n_blocks, n_slices, index_ref, column_ref, *refs):
    pieces, refs = refs[:n_pieces], refs[n_pieces:]
    hits_refs, router_ref, refs = refs[:n_blocks], refs[n_blocks], refs[n_blocks + 1 :]
    local_experts, _, wide = refs[0].shape
    gate_ref, up_ref, gate_rows_ref, up_rows_ref, refs = *refs[:4], refs[4:]
    back_refs = refs[: n_blocks * local_experts]
    x_ref, weight_ref, dots_ref, made_ref, grads_ref, sems, row_sems = refs[-7:]
    rows_out, dots_out, *outs = refs[-7 - n_blocks - 5 : -7 - n_blocks]
    grad_outs = refs[-7 - n_blocks : -7]
    step = pl.program_id(0)
    total, block = x_ref.shape[0], x_ref.shape[0] // n_blocks
    hidden_units = wide * n_slices
    slot = lax.rem(step, 2)
    lane = lax.broadcasted_iota(jnp.int32, (total, 128), 1)

    def row_copy(source, target, at, which):
        return pltpu.make_async_copy(
            source.at[pl.ds(at * block, block)],
            target.at[pl.ds(index_ref[at] * block, block)],
            row_sems.at[which, at],
        )

    def made_copy(which, at, of_step, from_slot):
        span = local_experts * wide
        return pltpu.make_async_copy(
            made_ref.at[from_slot, which, pl.ds(at * block, block)],
            outs[which].at[
                pl.ds(index_ref[at] * block, block),
                pl.ds(pl.multiple_of(column_ref[of_step] * span, span), span),
            ],
            sems.at[from_slot, which, at],
        )

    def all_made(of_step, from_slot):
        return [made_copy(w, at, of_step, from_slot) for w in range(3) for at in range(n_blocks)]

    def hit_of(expert):
        return jnp.concatenate([ref[:, expert : expert + 1] for ref in hits_refs], axis=0)

    @pl.when(step == 0)
    def _():
        start = 0
        for piece, rows in zip(pieces, piece_rows):
            x_ref[start : start + rows, :] = piece[...]
            start += rows
        for at in range(n_blocks):
            row_copy(x_ref, rows_out, at, 0).start()
        logits = matmul(x_ref[...], router_ref[...])
        expo = jnp.exp(logits - jnp.max(logits, axis=-1, keepdims=True))
        probs = expo / jnp.sum(expo, axis=-1, keepdims=True)
        which = lax.broadcasted_iota(jnp.int32, probs.shape, 1)
        weights = jnp.zeros((total, 128), F32)
        for expert in range(local_experts):
            mine = which == index_ref[n_blocks] * local_experts + expert
            weight = jnp.sum(jnp.where(mine, probs, 0.0), axis=-1, keepdims=True)
            weights = jnp.where(lane == expert, weight * hit_of(expert), weights)
        weight_ref[...] = weights
        dots_ref[...] = jnp.zeros_like(dots_ref)

    @pl.when((step >= 2) & (step < n_slices))
    def _():
        for copy in all_made(step - 2, slot):
            copy.wait()

    @pl.when(step < n_slices)
    def _():
        for expert in range(local_experts):
            gate = matmul(x_ref[...], gate_ref[expert])
            up = matmul(x_ref[...], up_ref[expert])
            back = jnp.concatenate(
                [ref[...] for ref in back_refs[n_blocks * expert : n_blocks * (expert + 1)]], axis=0
            ).astype(F32)
            weight = weight_ref[:, expert : expert + 1]
            sig = 0.5 + 0.5 * jnp.tanh(0.5 * gate)
            silu = gate * sig
            hidden = silu * up
            dot = jnp.sum(hidden * back, axis=-1, keepdims=True)
            dots_ref[...] += jnp.where(lane == expert, dot, 0.0)
            back = back * weight
            dgate = (back * up * (sig + silu * (1.0 - sig))).astype(BF16)
            dup = (back * silu).astype(BF16)
            columns = slice(expert * wide, (expert + 1) * wide)
            made_ref[slot, 0, :, columns] = (hidden * weight).astype(BF16)
            for which, value in ((0, dgate), (1, dup)):
                made_ref[slot, 1 + which, :, columns] = value
                first = (which * local_experts + expert) * hidden_units
                grads_ref[:, pl.ds(pl.multiple_of(first + step * wide, wide), wide)] = value
        for copy in all_made(step, slot):
            copy.start()

    @pl.when(step == n_slices - 1)
    def _():
        for expert in range(local_experts):
            dots_ref[...] = jnp.where(lane == expert, dots_ref[...] * hit_of(expert), dots_ref[...])
        for at in range(n_blocks):
            row_copy(dots_ref, dots_out, at, 1).start()

    @pl.when(step >= n_slices)
    def _():
        result = None
        for which, weights in enumerate((gate_rows_ref, up_rows_ref)):
            for expert in range(local_experts):
                first = (which * local_experts + expert) * hidden_units
                part = matmul_nt(grads_ref[:, first : first + hidden_units], weights[expert])
                result = part if result is None else result + part
        for at in range(n_blocks):
            grad_outs[at][...] = result[at * block : (at + 1) * block].astype(BF16)

    @pl.when(step == pl.num_programs(0) - 1)
    def _():
        for at in range(n_blocks):
            row_copy(x_ref, rows_out, at, 0).wait()
            row_copy(dots_ref, dots_out, at, 1).wait()
        for copy in all_made(n_slices - 1, (n_slices - 1) % 2) + all_made(
            n_slices - 2, n_slices % 2
        ):
            copy.wait()


def expert_call(index, column_place, pieces, hits, router, w_gate, w_up, backs, held, seq):
    local_experts, width, hidden_units = w_gate.shape
    n_slices, n_blocks = column_place.shape[0], index.shape[0] - 1
    wide = hidden_units // n_slices
    total = sum(piece.shape[0] for piece in pieces)
    block = total // n_blocks
    span = local_experts * hidden_units
    tile = 512
    assert n_slices >= 2

    def at_slice(step):
        return jnp.minimum(step, n_slices - 1)

    def at_tile(step):
        return jnp.maximum(step - n_slices, 0)

    weight_spec = pl.BlockSpec(
        (local_experts, width, wide), lambda i, index, column: (0, 0, at_slice(i))
    )
    rows_spec = pl.BlockSpec(
        (local_experts, tile, hidden_units), lambda i, index, column: (0, at_tile(i), 0)
    )

    def block_spec(at, columns, tiled):
        if tiled:
            return pl.BlockSpec(
                (block, columns), lambda i, index, column: (index[at], at_slice(i))
            )
        return pl.BlockSpec((block, columns), lambda i, index, column: (index[at], 0))

    in_specs = [pl.BlockSpec(piece.shape, lambda i, index, column: (0, 0)) for piece in pieces]
    in_specs += [block_spec(at, local_experts, False) for at in range(n_blocks)]
    in_specs += [pl.BlockSpec(router.shape, lambda i, index, column: (0, 0))]
    in_specs += [weight_spec, weight_spec, rows_spec, rows_spec]
    in_specs += [block_spec(at, wide, True) for _ in range(local_experts) for at in range(n_blocks)]
    operands = [*pieces, *[hits] * n_blocks, router, w_gate, w_up, w_gate, w_up]
    operands += [back for back in backs for _ in range(n_blocks)]
    aliases = {}
    if held is not None:
        aliases = {2 + len(operands) + i: i for i in range(5)}
        in_specs += [ANY_SPEC] * 5
        operands += held
    made = jax.ShapeDtypeStruct((seq, span), BF16)
    rows = [piece.shape[0] for piece in pieces]
    results = pl.pallas_call(
        lambda *refs: expert_kernel(len(pieces), rows, n_blocks, n_slices, *refs),
        out_shape=[
            jax.ShapeDtypeStruct((seq, width), BF16),
            jax.ShapeDtypeStruct((seq, 128), F32),
            made,
            made,
            made,
        ]
        + [jax.ShapeDtypeStruct((block, width), BF16)] * n_blocks,
        grid_spec=pltpu.PrefetchScalarGridSpec(
            num_scalar_prefetch=2,
            grid=(n_slices + width // tile,),
            in_specs=in_specs,
            out_specs=[ANY_SPEC] * 5
            + [pl.BlockSpec((block, tile), lambda i, index, column: (0, at_tile(i)))] * n_blocks,
            scratch_shapes=[
                pltpu.VMEM((total, width), BF16),
                pltpu.VMEM((total, 128), F32),
                pltpu.VMEM((total, 128), F32),
                pltpu.VMEM((2, 3, total, local_experts * wide), BF16),
                pltpu.VMEM((total, 2 * span), BF16),
                pltpu.SemaphoreType.DMA((2, 3, n_blocks)),
                pltpu.SemaphoreType.DMA((2, n_blocks)),
            ],
        ),
        input_output_aliases=aliases,
        compiler_params=params(),
        cost_estimate=cost(
            8 * total * width * span, 8 * width * span + 10 * total * span, total * span
        ),
    )(index, column_place, *operands)
    return results[:5], results[5:]


def back_rows_kernel(n_blocks, n_arrays, index_ref, column_ref, *refs):
    rows_refs, refs = refs[: n_blocks * n_arrays], refs[n_blocks * n_arrays :]
    weight_refs, outs, held = refs[:n_arrays], refs[n_arrays:-1], refs[-1]
    local_experts, _, hidden_units = weight_refs[0].shape
    n_slices = column_ref.shape[0]
    wide = hidden_units // n_slices
    block = rows_refs[0].shape[0]

    @pl.when(pl.program_id(0) == 0)
    def _():
        for at in range(n_blocks):
            for array in range(n_arrays):
                for expert in range(local_experts):
                    for part in range(n_slices):
                        first = (array * local_experts + expert) * hidden_units + part * wide
                        source = pl.multiple_of(
                            (column_ref[part] * local_experts + expert) * wide, 128
                        )
                        held[at * block : (at + 1) * block, first : first + wide] = rows_refs[
                            at * n_arrays + array
                        ][:, pl.ds(source, wide)]

    total = None
    for array in range(n_arrays):
        for expert in range(local_experts):
            first = (array * local_experts + expert) * hidden_units
            part = matmul_nt(held[:, first : first + hidden_units], weight_refs[array][expert])
            total = part if total is None else total + part
    for at in range(n_blocks):
        outs[at][...] = total[at * block : (at + 1) * block].astype(BF16)


def back_rows(index, column_place, arrays, weights, block, tile=256):
    n_blocks, n_arrays = index.shape[0], len(arrays)
    local_experts, width, hidden_units = weights[0].shape
    span = local_experts * hidden_units

    def row_spec(at):
        return pl.BlockSpec((block, span), lambda i, index, column: (index[at], 0))

    return pl.pallas_call(
        lambda *refs: back_rows_kernel(n_blocks, n_arrays, *refs),
        out_shape=[jax.ShapeDtypeStruct((block, width), BF16)] * n_blocks,
        grid_spec=pltpu.PrefetchScalarGridSpec(
            num_scalar_prefetch=2,
            grid=(width // tile,),
            in_specs=[row_spec(at) for at in range(n_blocks) for _ in range(n_arrays)]
            + [
                pl.BlockSpec(
                    (local_experts, tile, hidden_units), lambda i, index, column: (0, i, 0)
                )
            ]
            * n_arrays,
            out_specs=[pl.BlockSpec((block, tile), lambda i, index, column: (0, i))] * n_blocks,
            scratch_shapes=[pltpu.VMEM((n_blocks * block, n_arrays * span), BF16)],
        ),
        compiler_params=params(),
        cost_estimate=cost(
            2 * n_blocks * block * width * span * n_arrays, 2 * width * span * n_arrays
        ),
    )(index, column_place, *(list(arrays) * n_blocks), *weights)


def weight_grad_kernel(n_adds, left_ref, right_ref, *refs):
    total = matmul_tn(left_ref[...], right_ref[...])
    for ref in refs[:n_adds]:
        total += ref[...].astype(F32)
    out_ref = refs[-1]
    if len(out_ref.shape) == 2:
        out_ref[...] = total.astype(out_ref.dtype)
    else:
        wide = out_ref.shape[2]
        for expert in range(out_ref.shape[0]):
            out_ref[expert] = total[:, expert * wide : (expert + 1) * wide]


def weight_grad(left, right, first, columns, adds=(), experts=None, tile=512):
    seq, width = left.shape
    assert first % columns == 0
    if experts is None:
        out_shape = jax.ShapeDtypeStruct((width, columns), BF16)
        out_spec = pl.BlockSpec((tile, columns), lambda i: (i, 0))
    else:
        out_shape = jax.ShapeDtypeStruct((experts, width, columns // experts), F32)
        out_spec = pl.BlockSpec((experts, tile, columns // experts), lambda i: (0, i, 0))

    def add_spec(at):
        return pl.BlockSpec((tile, columns), lambda i: (i, at))

    return pl.pallas_call(
        lambda *refs: weight_grad_kernel(len(adds), *refs),
        out_shape=out_shape,
        grid=(width // tile,),
        in_specs=[
            pl.BlockSpec((seq, tile), lambda i: (0, i)),
            pl.BlockSpec((seq, columns), lambda i: (0, first // columns)),
        ]
        + [add_spec(at) for _, at in adds],
        out_specs=out_spec,
        compiler_params=params(),
        cost_estimate=cost(2 * seq * width * columns, 2 * width * (seq + columns)),
    )(left, right, *(value for value, _ in adds))


def body(
    tokens,
    seq_lengths,
    routes,
    w_query,
    w_key,
    w_value,
    w_out,
    gain_attn,
    gain_query,
    gain_key,
    gain_ffn,
    w_router,
    w_gate,
    w_up,
    w_down_t,
    cotangent,
):
    rows, width = tokens.shape
    local_experts, _, hidden_units = w_gate.shape
    groups, n_dp = lax.axis_size("expert"), lax.axis_size("dp")
    experts_all = local_experts * groups
    seq = groups * rows
    own = width // groups
    weight_rows = w_query.shape[0]
    chips = n_dp // CORES
    me, dp = lax.axis_index("expert"), lax.axis_index("dp")
    both_axes = ("dp", "expert")
    ring = Ring(groups)
    positions = jnp.arange(seq, dtype=jnp.int32)
    my_rows = me * rows + jnp.arange(rows, dtype=jnp.int32)
    seq_length = lax.dynamic_index_in_dim(seq_lengths, dp, 0, keepdims=True)
    used = (my_rows < seq_length[0]).astype(F32)[:, None]

    expert_ids = jnp.arange(experts_all, dtype=jnp.int32)
    chosen = jnp.any(routes[:, :, None] == expert_ids[None, None, :], axis=1)
    chosen_low = chosen.astype(BF16)

    hit_columns = rows * local_experts // weight_rows
    hits_out = chosen_low.reshape(rows, groups, local_experts).transpose(1, 0, 2)
    extra = jnp.concatenate(
        [jnp.stack([gain_attn, gain_query, gain_key, gain_ffn], axis=1), w_router], axis=1
    )
    extra_columns = extra.shape[1]
    pad = -(extra_columns + hit_columns) % 128
    send = jnp.concatenate(
        [w.reshape(weight_rows, groups, own).transpose(1, 0, 2) for w in (w_query, w_key, w_value)]
        + [
            jnp.broadcast_to(extra[None], (groups, weight_rows, extra_columns)),
            hits_out.reshape(groups, weight_rows, hit_columns),
            jnp.zeros((groups, weight_rows, pad), BF16),
        ],
        axis=2,
    )
    moves = [(e * n_dp + i, i * groups + e) for e in range(groups) for i in range(n_dp)]
    half = HEAD_DIM // 2
    frequency = ROPE_BASE ** (-(jnp.arange(half, dtype=F32) * 2.0) / HEAD_DIM)
    angles = positions.astype(F32)[:, None] * frequency[None, :]
    cosine, sine = jnp.cos(angles), jnp.sin(angles)
    cosine = jnp.concatenate([cosine, cosine], axis=1)
    sine = jnp.concatenate([-sine, sine], axis=1)
    start = {}
    far = groups // 2
    arrival = [0] + [o for step in range(1, far) for o in (groups - step, step)] + [far]
    per_call = 4
    calls = groups // per_call
    call_index = [
        jnp.stack([ring.natural[o] for o in arrival[at : at + per_call]] + [me])
        for at in range(0, groups, per_call)
    ]

    def make_got(pieces):
        start["got"] = lax.all_to_all(send, "expert", split_axis=0, concat_axis=0, tiled=True)
        start["in"] = DpGather(start["got"].reshape(groups * weight_rows, -1), n_dp)
        return (start["got"], cosine, sine, *call_index)

    def make_y(pieces):
        start["out"] = DpGather(lax.ppermute(w_out, both_axes, moves), n_dp)
        return (*start["in"].over_y(), start["out"].chunk)

    hooks = {far - 1: make_got, far: make_y}
    tokens_all = place_blocks(ring, ring.gather(tokens, hooks), rows, width)
    start["in"].over_cores()
    got, projections = start["got"], start["in"].rows()
    hits = got[:, :, 3 * own + extra_columns : 3 * own + extra_columns + hit_columns]
    hits = hits.reshape(seq, local_experts).astype(F32)
    w_qkv = projections
    small = projections[:, 3 * own : 3 * own + extra_columns]
    gains_full = small[:, :4].T.astype(F32)
    full_router = small[:, 4:]

    resid_in = tokens.astype(F32)
    attn_gain, ffn_gain = gains_full[0:1], gains_full[3:4]
    [cot_own] = together((cotangent,), (tokens_all,))
    cot_all = lax.all_gather(cot_own, "expert", axis=0, tiled=True)
    attn_in, qkv, squares = project(tokens_all, attn_gain, w_qkv, 3 * own)
    [start["out"].chunk] = together((start["out"].chunk,), (squares,))
    out_over_y = start["out"].over_y()
    [squares] = together((expert_sum(squares, groups),), out_over_y)
    gains_own = lax.dynamic_slice(gains_full, (1, me * own), (2, own))
    q, k, v, attended = attend(seq_length, qkv, squares, gains_own, cosine, sine)
    [attended] = together((attended,), start["out"].over_cores())
    own_out = start["out"].rows()

    def block_of(value, o):
        return lax.dynamic_slice(value, (ring.natural[o] * rows, 0), (rows, value.shape[1]))

    out_far = matmul(block_of(attended, far), own_out).astype(BF16)
    out_part = matmul(attended, own_out).astype(BF16)
    backs = []

    def make_back(expert):
        backs.append(matmul(cot_all, w_down_t[expert]).astype(BF16))
        return (backs[-1],)

    hooks = {
        far - 1: lambda: make_back(0),
        far: lambda: (
            *[make_back(expert)[0] for expert in range(1, local_experts)],
            full_router,
            hits,
        ),
    }
    resid_mid = resid_in + ring.scatter(
        lambda o: out_far if o == far else block_of(out_part, o), hooks
    )
    mid_scale = norm_scale(resid_mid)
    ffn_in = (resid_mid * mid_scale * ffn_gain).astype(BF16)

    distances = (
        [2 * y + 1 for y in range(chips)] + [2 * y for y in range(1, chips)] + [0]
    )
    place_of = np.zeros((n_dp,), np.int32)
    place_of[np.array(distances)] = np.arange(n_dp)
    column_place = jnp.asarray(place_of)[jnp.arange(n_dp, dtype=jnp.int32) ^ dp]
    held, drow_terms = [], {}

    def expert_pieces(pieces, at):
        given = pieces[at:] if at + per_call == groups else pieces[at : at + per_call]
        order = [o for o, _, _ in given[:per_call]]
        result, blocks = expert_call(
            call_index[at // per_call],
            column_place,
            [piece for _, _, piece in given],
            hits,
            full_router,
            w_gate,
            w_up,
            backs,
            held[-1] if held else None,
            seq,
        )
        held.append(result)
        drow_terms.update(zip(order, blocks))
        return result

    hooks = {}
    for call in range(calls - 1):
        step = (call + 1) * per_call // 2 + 1
        hooks[step] = lambda pieces, at=call * per_call: expert_pieces(pieces, at)
    pieces = ring.gather(ffn_in, hooks)
    expert_pieces(pieces, groups - per_call)
    ffn_all, pair_dots, scaled_hidden, dgates, dups = held[-1]
    pairs = []

    def make_pairs():
        out = pair_dots[:, :local_experts].reshape(groups, rows, local_experts).transpose(0, 2, 1)
        pairs.append(lax.all_to_all(out, "expert", split_axis=0, concat_axis=0, tiled=True))
        return tuple(pairs)

    slice_columns = local_experts * hidden_units // n_dp
    swap = [(i, i ^ 1) for i in range(n_dp)]
    sides = [(cot_all, scaled_hidden), (ffn_all, dgates), (ffn_all, dups)]
    other, adds = {}, {}

    def make_sent(which):
        sent = weight_grad(*sides[which], 0, chips * slice_columns)
        other[which] = lax.ppermute(sent, "dp", swap)
        adds[which] = [(other[which], 0)]
        return (sent,)

    parts = {}

    def make_part(which):
        parts[which] = [
            weight_grad(
                *sides[which],
                (chips + y - 1) * slice_columns,
                slice_columns,
                [(other[which], y)],
            )
            for y in range(1, chips)
        ]
        return tuple(parts[which])

    def send_part(which, after):
        sent = together(tuple(parts[which]), (after,))
        got = [
            lax.ppermute(part, "dp", [(i, i ^ (2 * y)) for i in range(n_dp)])
            for y, part in zip(range(1, chips), sent)
        ]
        adds[which] += [(part, 0) for part in got]
        return tuple(got)

    hooks = {
        far - 2: lambda: make_sent(0),
        far - 1: lambda: (*make_sent(1), *make_part(0)),
        far: lambda: (*make_pairs(), *make_sent(2), *make_part(1)),
    }
    drow = ring.scatter(lambda o: drow_terms[o], hooks)

    grad_rows = cotangent.astype(F32)
    dprobs = pairs[0].reshape(experts_all, rows).T
    probs = jax.nn.softmax(matmul(ffn_in, full_router), axis=-1)
    dlogits = probs * (dprobs - jnp.sum(probs * dprobs, axis=1, keepdims=True))
    dlogits = dlogits.astype(BF16)
    grad_router = matmul_tn(ffn_in, dlogits)
    dffn = drow + matmul_nt(dlogits, full_router)
    grad_gain_ffn = jnp.sum(dffn * resid_mid * mid_scale, axis=0, keepdims=True)
    scaled = dffn * ffn_gain
    mid_grads = (
        grad_rows
        + mid_scale * scaled
        - resid_mid * mid_scale**3 * jnp.mean(scaled * resid_mid, axis=1, keepdims=True)
    )
    mid_low = mid_grads.astype(BF16)

    def make_moe(pieces):
        return back_rows(
            jnp.zeros((1,), jnp.int32), column_place, (scaled_hidden,), (w_down_t,), seq
        )

    moe_made = []
    first = send_part(0, mid_low)
    mid_pieces = ring.gather(
        mid_low,
        {
            1: lambda pieces: make_part(2),
            2: lambda pieces: moe_made.extend(make_moe(pieces)) or moe_made,
        },
    )
    mid_all = place_blocks(ring, mid_pieces, rows, width)
    [mid_all] = together((mid_all,), first)
    second = send_part(1, mid_all)
    grad_heads = matmul_nt(mid_all, own_out).astype(BF16)

    moe_part, grad_heads = lax.optimization_barrier((moe_made[0], grad_heads))
    moe_rows = lax.psum_scatter(moe_part, "expert", scatter_dimension=0, tiled=True).astype(F32)
    output = (resid_mid + moe_rows).astype(BF16)

    dq, dk, dv, dots, dgains = attend_back(
        seq_length, qkv, squares, gains_own, cosine, sine, q, k, v, grad_heads
    )
    dots = expert_sum(dots, groups)
    dqkv, din_part = finish(dq, dk, dv, qkv, squares, dots, w_qkv)
    third = []

    def make_own(which, after):
        left, right = sides[which]
        [left] = together((left,), after)
        return weight_grad(
            left,
            right,
            (n_dp - 1) * slice_columns,
            slice_columns,
            adds[which],
            local_experts,
        )

    def middle():
        third.extend(send_part(2, second[0]))
        return second

    spread_gains = lax.dynamic_update_slice(jnp.zeros((2, width), F32), dgains, (0, me * own))
    lane = lax.broadcasted_iota(jnp.int32, (1, width), 1)
    sums = jnp.where(
        lane == 0,
        jnp.sum(used * resid_mid * resid_mid),
        jnp.where(lane == 1, jnp.sum(used * moe_rows * moe_rows), 0.0),
    )
    rest = jnp.concatenate([spread_gains, grad_gain_ffn, sums, grad_router.T], axis=0)
    own_grads = []

    def first_own():
        own_grads.append(make_own(0, second))
        return tuple(own_grads)

    hooks = {far - 3: middle, far - 1: first_own, far: lambda: (rest,)}
    dattn = ring.scatter(lambda o: block_of(din_part, o), hooks)
    [rest] = together((rest,), (dattn,))
    rest = expert_sum(rest, groups)
    all_hops = rest
    own_grads += [make_own(which, (rest,)) for which in (1, 2)]
    rest = dp_sum(rest, n_dp)
    grad_down, grad_gate_w, grad_up_w = own_grads
    in_scale = norm_scale(resid_in)
    scaled = dattn * attn_gain
    input_grad = (
        mid_grads
        + in_scale * scaled
        - resid_in * in_scale**3 * jnp.mean(scaled * resid_in, axis=1, keepdims=True)
    ).astype(BF16)

    block = width // n_dp

    def projection_term(rel):
        left = lax.dynamic_slice(attn_in, (0, (dp ^ rel) * block), (seq, block))
        return matmul_tn(left, dqkv)

    reduced = dp_reduce(projection_term, n_dp).astype(BF16)
    [reduced] = together((reduced,), (all_hops,))
    reduced = lax.all_to_all(
        reduced.reshape(groups, weight_rows, 3 * own),
        "expert",
        split_axis=0,
        concat_axis=0,
        tiled=True,
    ).astype(F32)
    grads = [
        reduced[:, :, i * own : (i + 1) * own].transpose(1, 0, 2).reshape(weight_rows, width)
        for i in range(3)
    ]
    grad_gain_attn = (
        sum(jnp.sum(g * w.astype(F32), axis=1) for g, w in zip(grads, (w_query, w_key, w_value)))
        / gain_attn.astype(F32)
    )
    out_grads = matmul_tn(attended, mid_all)

    def out_term(rel):
        return lax.dynamic_slice(out_grads, ((dp ^ rel) * weight_rows, 0), (weight_rows, width))

    grad_out = dp_reduce(out_term, n_dp).astype(BF16)
    [grad_out] = together((grad_out,), (all_hops,))
    grad_out = lax.ppermute(grad_out, both_axes, [(b, a) for a, b in moves]).astype(F32)

    mine = lax.dynamic_slice(
        rest, (0, (dp * groups + me) * weight_rows), (rest.shape[0], weight_rows)
    )
    counted = jnp.sum(seq_lengths).astype(F32) * width
    rms_resid = jnp.sqrt(rest[3, 0] / counted)
    rms_moe = jnp.sqrt(rest[3, 1] / counted)
    return (
        output,
        input_grad,
        grads[0],
        grads[1],
        grads[2],
        grad_out,
        grad_gain_attn,
        mine[0],
        mine[1],
        mine[2],
        mine[4:].T,
        grad_gate_w,
        grad_up_w,
        grad_down,
        rms_resid,
        rms_moe,
    )


def solution(mesh):
    both = ("dp", "expert")
    row, vector, expert = P(both, None), P(both), P("expert", None, None)
    placed = (
        row,
        P(),
        row,
        row,
        row,
        row,
        row,
        vector,
        vector,
        vector,
        vector,
        row,
        expert,
        expert,
        expert,
        row,
    )
    grads = P("expert", None, "dp")
    return jax.shard_map(
        body,
        mesh=mesh,
        in_specs=placed,
        out_specs=(row,) * 6 + (vector,) * 4 + (row, grads, grads, grads, P(), P()),
        check_vma=False,
    )
```
